32 devices in a mesh: gx: 8 (over z, x), gy: 4 (over y, core).
Axes of the slice: x: 2, y: 2, z: 4, core: 2. Of those that a mesh axis runs over, the one named last changes fastest.
Arguments:
- charges: float32 [192, 256, 128], P('gx', 'gy'), may hold values from -4 to 4
- kernel_fine: bfloat16 [15, 15, 15], replicated, may hold values from 0 to 1
- kernel_mid: bfloat16 [15, 15, 15], replicated, may hold values from 0 to 1
- kernel_top: bfloat16 [15, 15, 15], replicated, may hold values from 0 to 1
Outputs:
- potential: float32 [192, 256, 128], P('gx', 'gy')
The draws below stay inside these ranges and needn't reach their ends.
All inputs are finite; a program needn't handle non-finite values.
Results may differ from the reference program's by a relative error of at most 0.0035.
Values may be sent and summed in bfloat16 or wider, within the bound.
No kernel may reach another device: no remote copies, remote signals or barrier semaphores. Data moves between devices by JAX's collectives and lax.ppermute only.
A program may use at most 256 MiB of HBM per device.

```python
import jax
import jax.numpy as jnp
from jax import lax

NZ = 128
NX = 192
NY = 256


def draw_charges(key, part):
    return jnp.clip(jax.random.normal(key, (NX, NY, NZ), jnp.float32), -4.0, 4.0)


def kernel_values(key, level):
    key = jax.random.fold_in(key, 101 + level)
    offsets = jnp.arange(15, dtype=jnp.float32) - 7.0
    radius = offsets[:, None, None] * offsets[:, None, None] + offsets[None, :, None] * offsets[None, :, None] + offsets[None, None, :] * offsets[None, None, :]
    envelope = 1.0 / jnp.sqrt(1.0 + radius / 16.0)
    factor = jax.random.uniform(key, (15, 15, 15), jnp.float32, 0.5, 1.5)
    values = envelope * factor
    values = values * 0.5 ** level / jnp.sqrt(jnp.sum(values * values))
    return values.astype(jnp.bfloat16)


def draw_kernel_fine(key, part):
    return kernel_values(key, 0)


def draw_kernel_mid(key, part):
    return kernel_values(key, 1)


def draw_kernel_top(key, part):
    return kernel_values(key, 2)


def setup_inputs(seed: int = 0) -> dict:
    key_list = jax.random.split(jax.random.key(seed), 5)
    charges = draw_charges(jax.random.fold_in(key_list[4], 71), 0)
    kernel_fine = draw_kernel_fine(jax.random.fold_in(key_list[4], 71), 0)
    kernel_mid = draw_kernel_mid(jax.random.fold_in(key_list[4], 71), 0)
    kernel_top = draw_kernel_top(jax.random.fold_in(key_list[4], 71), 0)
    return dict(charges=charges, kernel_fine=kernel_fine, kernel_mid=kernel_mid, kernel_top=kernel_top)


def restrict_axis(values, axis, count):
    left_part = lax.slice_in_dim(values, 0, 2 * count, 2, axis)
    middle_part = lax.slice_in_dim(values, 1, 2 * count, 2, axis)
    right_part = lax.slice_in_dim(values, 2, 2 * count + 1, 2, axis)
    return 0.5 * left_part + middle_part + 0.5 * right_part


def restrict(field):
    count_x, count_y, count_z = field.shape
    values = jnp.pad(field.astype(jnp.float32), ((1, 0), (1, 0), (1, 0)))
    values = restrict_axis(values, 0, count_x // 2)
    values = restrict_axis(values, 1, count_y // 2)
    return restrict_axis(values, 2, count_z // 2)


def prolong_axis(values, axis, count):
    first_part = lax.slice_in_dim(values, 0, count, 1, axis)
    second_part = lax.slice_in_dim(values, 1, count + 1, 1, axis)
    middle_part = 0.5 * (first_part + second_part)
    joined = jnp.stack((first_part, middle_part), axis=axis + 1)
    new_shape = list(values.shape)
    new_shape[axis] = 2 * count
    return joined.reshape(new_shape)


def prolong(coarse):
    count_x, count_y, count_z = coarse.shape
    values = jnp.pad(coarse, ((0, 1), (0, 1), (0, 1)))
    values = prolong_axis(values, 0, count_x)
    values = prolong_axis(values, 1, count_y)
    return prolong_axis(values, 2, count_z)


def correlate(field, kernel):
    grid_shape = field.shape
    padded_sizes = tuple(extent + 16 for extent in grid_shape)
    flipped = kernel.astype(jnp.float32)[::-1, ::-1, ::-1]
    kernel_grid = jnp.zeros(padded_sizes, field.dtype).at[:15, :15, :15].set(flipped.astype(field.dtype))
    kernel_grid = jnp.roll(kernel_grid, (-7, -7, -7), axis=(0, 1, 2))
    spectrum = jnp.fft.rfftn(field, s=padded_sizes) * jnp.fft.rfftn(kernel_grid, s=padded_sizes)
    result = jnp.fft.irfftn(spectrum, s=padded_sizes)
    return result[:grid_shape[0], :grid_shape[1], :grid_shape[2]].astype(field.dtype)


def widen(values):
    return lax.optimization_barrier(values).astype(jnp.float32)


def reference(charges, kernel_fine, kernel_mid, kernel_top):
    fine_q = charges.astype(jnp.bfloat16)
    mid_r = restrict(widen(fine_q))
    mid_q = mid_r.astype(jnp.bfloat16)
    top_r = restrict(widen(mid_q))
    top_q = top_r.astype(jnp.bfloat16)
    fine_e = correlate(widen(fine_q), kernel_fine)
    mid_e = correlate(widen(mid_q), kernel_mid)
    top_e = correlate(widen(top_q), kernel_top)
    mid_u = mid_e + prolong(top_e)
    return fine_e + prolong(mid_u)
```

```python
import functools

import jax
import jax.numpy as jnp
import numpy as np
from jax import lax
from jax.experimental import pallas as pl
from jax.experimental.pallas import tpu as pltpu
from jax.sharding import PartitionSpec as P

BF = jnp.bfloat16
F32 = jnp.float32
LANES = 128


def two(matrix):
    high = np.asarray(matrix, np.float64).astype(BF)
    low = (matrix - high.astype(np.float64)).astype(BF)
    return high, low


def beside(real, imag):
    out = np.zeros((real.shape[0], 2 * LANES))
    out[:, : real.shape[1]] = real
    out[:, LANES : LANES + imag.shape[1]] = imag
    return out


def three_terms(matrix):
    high, low = two(matrix)
    return np.concatenate([high, high, low], 1)


def up(count):
    out = np.zeros((2 * count, count + 1))
    for i in range(count):
        out[2 * i, i] = 1.0
        out[2 * i + 1, i] = out[2 * i + 1, i + 1] = 0.5
    return out


def up_closed(count):
    return up(count)[:, :count]


class Level:
    def __init__(self, taps, out_x, out_y, shift, period_y, size_z, rows_y, rows_y_end, cols_z):
        half = taps // 2
        self.taps, self.out_x, self.in_x = taps, out_x, out_x + taps - 1
        self.period_y, self.size_z = period_y, size_z
        period_z = size_z + half + (size_z + half) % 2
        assert period_y >= shift + out_y + half and shift >= half and period_y % 16 == 0
        freq_z = np.arange(period_z // 2 + 1)
        assert len(freq_z) <= LANES
        freq_y = np.arange(period_y)
        turn_z, turn_y = 2 * np.pi / period_z, 2 * np.pi / period_y
        angle = turn_z * np.outer(np.arange(size_z), freq_z)
        self.to_z = np.concatenate(two(beside(np.cos(angle), -np.sin(angle))), 0)
        angle = turn_y * np.outer(freq_y, np.arange(period_y))
        self.to_y = three_terms(np.concatenate([np.cos(angle), np.sin(angle)], 0))
        offsets = np.arange(taps) - half
        angle = turn_z * np.outer(offsets, freq_z)
        table = np.zeros((LANES, 2 * LANES))
        table[:taps] = beside(np.cos(angle), np.sin(angle))
        self.kernel_z = np.concatenate(two(table), 0)
        angle = turn_y * np.outer(freq_y, np.pad(offsets, (0, 1)))
        self.kernel_y = three_terms(np.concatenate([np.cos(angle), np.sin(angle)], 0))
        angle = turn_y * np.outer(np.arange(out_y) + shift, freq_y)
        self.from_y = [
            three_terms(
                np.concatenate([rows @ np.cos(angle), rows @ np.sin(angle)], 0) / period_y
            )
            for rows in (rows_y, rows_y_end)
        ]
        weight = np.where((freq_z == 0) | (2 * freq_z == period_z), 1.0, 2.0)[:, None] / period_z
        angle = turn_z * np.outer(freq_z, np.arange(size_z))
        table = np.zeros((2 * LANES, cols_z.shape[0]))
        table[: len(freq_z)] = (weight * np.cos(angle)) @ cols_z.T
        table[LANES : LANES + len(freq_z)] = (-weight * np.sin(angle)) @ cols_z.T
        high, low = two(table)
        self.from_z = np.concatenate([high, high, low], 0)


def down(count, first, length):
    out = np.zeros((count, length))
    for j in range(count):
        for a, w in ((-1, 0.5), (0, 1.0), (1, 0.5)):
            if 0 <= first + 2 * j + a < length:
                out[j, first + 2 * j + a] = w
    return out


def dot(a, b):
    return jnp.dot(a, b, preferred_element_type=F32)


def split(value, terms):
    out = []
    for _ in range(terms - 1):
        out.append(value.astype(BF))
        value = value - out[-1].astype(F32)
    return out + [value.astype(BF)]


def stacked(value):
    high, low = split(value, 2)
    return jnp.concatenate([high, low, high], 0)


def z_transform(cells, table):
    size_z = cells.shape[1]
    if size_z % LANES == 0:
        return dot(jnp.concatenate([cells, cells], 1), table[...])
    return dot(cells, table[:size_z]) + dot(cells, table[size_z:])


def forward(cells, to_z, to_y, real, imag, x):
    period = real.shape[1]
    spread = dot(to_y[...], stacked(z_transform(cells, to_z)))
    real[x] = spread[:period, :LANES] + spread[period:, LANES:]
    imag[x] = spread[:period, LANES:] - spread[period:, :LANES]


def backward(real, imag, from_y, from_z):
    count = from_y.shape[0] // 2
    spread = dot(from_y[...], stacked(jnp.concatenate([real, imag], 1)))
    real = spread[:count, :LANES] - spread[count:, LANES:]
    imag = spread[:count, LANES:] + spread[count:, :LANES]
    high, low = split(jnp.concatenate([real, imag], 1), 2)
    return dot(jnp.concatenate([high, low, high], 1), from_z[...])


def along_x(real, imag, spectrum, out_real, out_imag, block):
    kernel_r, kernel_d, kernel_s = spectrum
    taps, period = kernel_r.shape[:2]
    out_x = out_real.shape[0]

    def body(part, _):
        rows = pl.ds(pl.multiple_of(8 * part, 8), 8)
        for start in range(0, out_x, block):
            count = min(block, out_x - start)
            sums = [[None] * 3 for _ in range(count)]
            seen = {}
            for a in range(taps):
                weights = kernel_r[a, rows, :], kernel_d[a, rows, :], kernel_s[a, rows, :]
                for i in range(count):
                    x = start + i + a
                    if x not in seen:
                        r, m = real[x, rows, :], imag[x, rows, :]
                        seen[x] = r + m, r, m
                    for k in range(3):
                        term = weights[k] * seen[x][k]
                        sums[i][k] = term if a == 0 else sums[i][k] + term
            for i in range(count):
                out_real[start + i, rows, :] = sums[i][0] - sums[i][2]
                out_imag[start + i, rows, :] = sums[i][0] + sums[i][1]
        return 0

    lax.fori_loop(0, period // 8, body, 0)


def rows_loop(count, step, body):
    def trip(i, _):
        for k in range(step):
            body(i * step + k)
        return 0

    lax.fori_loop(0, count // step, trip, 0)
    for x in range(count - count % step, count):
        body(x)


def restrict_row(low, middle, high, down_y, down_z):
    total = 0.5 * low.astype(F32) + middle.astype(F32) + 0.5 * high.astype(F32)
    total = dot(down_y[...], jnp.concatenate(split(total, 3), 0))
    parts = split(total, 3)
    return sum(dot(part, down_z[...]) for part in reversed(parts))


def spectra_kernel(taps, kernels, *refs):
    levels = kernels.shape[0]
    tables, outs, mid = refs[: 2 * levels], refs[2 * levels : -1], refs[-1]
    for level in range(levels):
        kernel_z, kernel_y = tables[2 * level : 2 * level + 2]
        out_r, out_d, out_s = outs[3 * level : 3 * level + 3]
        period = out_r.shape[1]
        cells = kernels[level]
        mid[...] = dot(jnp.concatenate([cells, cells], 1), kernel_z[...])

        def body(a, kernel_y=kernel_y, out_r=out_r, out_d=out_d, out_s=out_s, period=period):
            rows = mid[pl.ds(pl.multiple_of(16 * a, 16), 16), :]
            spread = dot(kernel_y[...], stacked(rows))
            real = spread[:period, :LANES] - spread[period:, LANES:]
            imag = spread[:period, LANES:] + spread[period:, :LANES]
            out_r[a] = real
            out_d[a] = imag - real
            out_s[a] = imag + real

        rows_loop(taps, 3, body)


def restrict_kernel(valid, fine, down_y, down_z, out):
    def body(t):
        row = restrict_row(fine[2 * t], fine[2 * t + 1], fine[2 * t + 2], down_y, down_z)
        out[t] = jnp.where(t < valid[0], row, 0.0).astype(BF)

    rows_loop(out.shape[0], 1, body)


def fine_kernel(fine, kr, kd, ks, to_z, to_y, from_y, from_z, out, real, imag, er, ei):
    rows_loop(real.shape[0], 2, lambda x: forward(fine[x], to_z, to_y, real, imag, x))
    along_x(real, imag, (kr, kd, ks), er, ei, 8)

    def body(x):
        out[x] = backward(er[x], ei[x], from_y, from_z)

    rows_loop(out.shape[0], 2, body)


def coarse_kernel(
    valid,
    inside,
    mid,
    fine_e,
    down_y,
    down_z,
    mr,
    md,
    ms,
    m_to_z,
    m_to_y,
    m_from_y,
    m_from_z,
    tr,
    td,
    ts,
    t_to_z,
    t_to_y,
    t_from_y,
    t_from_z,
    out,
    m_real,
    m_imag,
    m_er,
    m_ei,
    m_out,
    t_real,
    t_imag,
    t_er,
    t_ei,
    t_out,
):
    skip = (mid.shape[0] - m_real.shape[0]) // 2
    cols = (mid.shape[1] - m_real.shape[1]) // 2

    def mid_body(x):
        cells = mid[x + skip, cols : cols + m_real.shape[1], :]
        forward(cells, m_to_z, m_to_y, m_real, m_imag, x)

    rows_loop(m_real.shape[0], 1, mid_body)

    def top_body(t):
        row = restrict_row(mid[2 * t], mid[2 * t + 1], mid[2 * t + 2], down_y, down_z)
        row = jnp.where(t < valid[0], row, 0.0).astype(BF)
        forward(row, t_to_z, t_to_y, t_real, t_imag, t)

    rows_loop(t_real.shape[0], 1, top_body)
    along_x(m_real, m_imag, (mr, md, ms), m_er, m_ei, 7)
    along_x(t_real, t_imag, (tr, td, ts), t_er, t_ei, 7)

    def top_out(x):
        t_out[x] = backward(t_er[x], t_ei[x], t_from_y, t_from_z)

    rows_loop(t_out.shape[0], 1, top_out)
    last = t_out.shape[0] - 1
    t_out[last] = t_out[last] * inside[0]

    def mid_out(x):
        m_out[x] = backward(m_er[x], m_ei[x], m_from_y, m_from_z)

    rows_loop(m_out.shape[0], 1, mid_out)
    for i in range(last):
        m_out[2 * i] += t_out[i]
        m_out[2 * i + 1] += 0.5 * (t_out[i] + t_out[i + 1])
    m_out[2 * last] = (m_out[2 * last] + t_out[last]) * inside[0]

    def finish(i):
        out[2 * i] = fine_e[2 * i] + m_out[i]
        out[2 * i + 1] = fine_e[2 * i + 1] + 0.5 * (m_out[i] + m_out[i + 1])

    rows_loop(out.shape[0] // 2, 1, finish)


def call(kernel, outs, scratch, scalars, args):
    vmem = pl.BlockSpec(memory_space=pltpu.VMEM)
    smem = pl.BlockSpec(memory_space=pltpu.SMEM)
    return pl.pallas_call(
        kernel,
        out_shape=outs,
        in_specs=[smem] * len(scalars) + [vmem] * len(args),
        out_specs=jax.tree.map(lambda _: vmem, outs),
        scratch_shapes=[pltpu.VMEM(shape, F32) for shape in scratch],
        compiler_params=pltpu.CompilerParams(vmem_limit_bytes=60 << 20),
    )(*scalars, *args)


def shifted(value, axis, by):
    length = lax.axis_size(axis)
    return lax.ppermute(
        value, axis, [(i, i + by) for i in range(length) if 0 <= i + by < length]
    )


def shards(charges, kernel_fine, kernel_mid, kernel_top):
    nx, ny, nz = charges.shape
    taps = kernel_fine.shape[0]
    half = taps // 2
    gx, gy = lax.axis_index("gx"), lax.axis_index("gy")
    left_x = lax.axis_size("gx") - gx
    end_y = gy == lax.axis_size("gy") - 1
    wide = half + 1

    ident = np.eye(ny)
    fine = Level(taps, nx, ny, wide, ny + 2 * wide, nz, ident, ident, np.eye(nz))
    my, mz = ny // 2, nz // 2
    to_fine = up(my)
    ended = np.diag([1.0] * my + [0.0])
    mid = Level(
        taps, nx // 2 + 1, my + 1, wide, my + 2 * wide, mz, to_fine, to_fine @ ended, up_closed(mz)
    )
    ty, tz = my // 2, mz // 2
    to_mid = np.concatenate([up(ty), np.eye(ty + 1)[-1:]], 0)
    top_ended = np.diag([1.0] * ty + [0.0])
    top = Level(
        taps,
        nx // 4 + 1,
        ty + 1,
        wide,
        ty + 2 * wide,
        tz,
        to_fine @ to_mid,
        to_fine @ to_mid @ top_ended,
        up_closed(mz) @ up_closed(tz),
    )

    cells = jnp.stack([kernel_fine, kernel_mid, kernel_top])
    cells = jnp.pad(cells, ((0, 0), (0, 0), (0, 1), (0, LANES - taps)))
    cells = cells.reshape(3, taps * 16, LANES)
    levels = (fine, mid, top)
    outs = [
        jax.ShapeDtypeStruct((taps, level.period_y, LANES), F32)
        for level in levels
        for _ in range(3)
    ]
    tables = [table for level in levels for table in (level.kernel_z, level.kernel_y)]
    spectra = call(
        functools.partial(spectra_kernel, taps),
        outs,
        [(taps * 16, 2 * LANES)],
        [],
        [cells, *tables],
    )

    fine_q = charges.astype(BF)
    fine_x = jnp.concatenate(
        [shifted(fine_q[-half:], "gx", 1), fine_q, shifted(fine_q[:wide], "gx", -1)], 0
    )
    fine_ext = jnp.concatenate(
        [shifted(fine_x[:, -wide:], "gy", 1), fine_x, shifted(fine_x[:, :wide], "gy", -1)], 1
    )

    lead = (half - 1) // 2
    rows = lead + nx // 2 + wide // 2
    down_y = np.tile(down(my, wide, ny + 2 * wide), (1, 3)).astype(BF)
    down_z = down(mz, 0, nz).T.astype(BF)
    valid = jnp.where(left_x == 1, lead + nx // 2, rows)[None].astype(jnp.int32)
    mid_q = call(
        restrict_kernel,
        jax.ShapeDtypeStruct((rows, my, mz), BF),
        [],
        [valid],
        [fine_ext, down_y, down_z],
    )
    mx = nx // 2
    reach = 2 * half + 1
    assert lead + mx >= reach and my >= 2 * wide
    mid_x = jnp.concatenate(
        [
            shifted(mid_q[lead + mx - reach : mx], "gx", 1),
            mid_q,
            shifted(mid_q[rows - mx :], "gx", -1),
        ],
        0,
    )
    mid_ext = jnp.concatenate(
        [
            shifted(mid_x[:, -2 * wide :], "gy", 1),
            mid_x,
            shifted(mid_x[:, : 2 * wide], "gy", -1),
        ],
        1,
    )

    fine_e = call(
        fine_kernel,
        jax.ShapeDtypeStruct((nx, ny, nz), F32),
        [(fine.in_x, fine.period_y, LANES)] * 2 + [(nx, fine.period_y, LANES)] * 2,
        [],
        [
            fine_ext,
            *spectra[:3],
            fine.to_z,
            fine.to_y,
            fine.from_y[0],
            fine.from_z,
        ],
    )

    tx = nx // 4
    down_y = down(ty + 2 * wide, 0, my + 4 * wide)
    keep = jnp.arange(ty + 2 * wide)[:, None] < jnp.where(end_y, wide + ty, ty + 2 * wide)
    down_y = jnp.where(keep, np.tile(down_y, (1, 3)).astype(BF), 0)
    down_z = down(tz, 0, mz).T.astype(BF)
    valid = jnp.minimum(left_x * tx + half, top.in_x)[None].astype(jnp.int32)
    inside = jnp.where(left_x == 1, 0.0, 1.0)[None].astype(F32)

    def pick(pair):
        return jnp.where(end_y, pair[1], pair[0])

    return call(
        coarse_kernel,
        jax.ShapeDtypeStruct((nx, ny, nz), F32),
        [(mid.in_x, mid.period_y, LANES)] * 2
        + [(mid.out_x, mid.period_y, LANES)] * 2
        + [(mid.out_x, ny, nz)]
        + [(top.in_x, top.period_y, LANES)] * 2
        + [(top.out_x, top.period_y, LANES)] * 2
        + [(top.out_x, ny, nz)],
        [valid, inside],
        [
            mid_ext,
            fine_e,
            down_y,
            down_z,
            *spectra[3:6],
            mid.to_z,
            mid.to_y,
            pick(mid.from_y),
            mid.from_z,
            *spectra[6:9],
            top.to_z,
            top.to_y,
            pick(top.from_y),
            top.from_z,
        ],
    )


def solution(mesh):
    placed = (P("gx", "gy", None), P(), P(), P())
    return jax.shard_map(
        shards, mesh=mesh, in_specs=placed, out_specs=P("gx", "gy", None), check_vma=False
    )
```

```python
import functools

import jax
import jax.numpy as jnp
import numpy as np
from jax import lax
from jax.experimental import pallas as pl
from jax.experimental.pallas import tpu as pltpu
from jax.sharding import PartitionSpec as P

BF = jnp.bfloat16
F32 = jnp.float32
LANES = 128


def two(matrix):
    high = np.asarray(matrix, np.float64).astype(BF)
    low = (matrix - high.astype(np.float64)).astype(BF)
    return high, low


def beside(real, imag):
    out = np.zeros((real.shape[0], 2 * LANES))
    out[:, : real.shape[1]] = real
    out[:, LANES : LANES + imag.shape[1]] = imag
    return out


def three_terms(matrix):
    high, low = two(matrix)
    return np.concatenate([high, high, low], 1)


def up(count):
    out = np.zeros((2 * count, count + 1))
    for i in range(count):
        out[2 * i, i] = 1.0
        out[2 * i + 1, i] = out[2 * i + 1, i + 1] = 0.5
    return out


def up_closed(count):
    return up(count)[:, :count]


class Level:
    def __init__(self, taps, out_x, out_y, shift, period_y, size_z, rows_y, rows_y_end, cols_z):
        half = taps // 2
        self.taps, self.out_x, self.in_x = taps, out_x, out_x + taps - 1
        self.period_y, self.size_z = period_y, size_z
        period_z = size_z + half + (size_z + half) % 2
        assert period_y >= shift + out_y + half and shift >= half and period_y % 16 == 0
        freq_z = np.arange(period_z // 2 + 1)
        assert len(freq_z) <= LANES
        freq_y = np.arange(period_y)
        turn_z, turn_y = 2 * np.pi / period_z, 2 * np.pi / period_y
        angle = turn_z * np.outer(np.arange(size_z), freq_z)
        self.to_z = np.concatenate(two(beside(np.cos(angle), -np.sin(angle))), 0)
        angle = turn_y * np.outer(freq_y, np.arange(period_y))
        self.to_y = three_terms(np.concatenate([np.cos(angle), np.sin(angle)], 0))
        offsets = np.arange(taps) - half
        angle = turn_z * np.outer(offsets, freq_z)
        table = np.zeros((LANES, 2 * LANES))
        table[:taps] = beside(np.cos(angle), np.sin(angle))
        self.kernel_z = np.concatenate(two(table), 0)
        angle = turn_y * np.outer(freq_y, np.pad(offsets, (0, 1)))
        self.kernel_y = three_terms(np.concatenate([np.cos(angle), np.sin(angle)], 0))
        angle = turn_y * np.outer(np.arange(out_y) + shift, freq_y)
        self.from_y = [
            three_terms(
                np.concatenate([rows @ np.cos(angle), rows @ np.sin(angle)], 0) / period_y
            )
            for rows in (rows_y, rows_y_end)
        ]
        weight = np.where((freq_z == 0) | (2 * freq_z == period_z), 1.0, 2.0)[:, None] / period_z
        angle = turn_z * np.outer(freq_z, np.arange(size_z))
        table = np.zeros((2 * LANES, cols_z.shape[0]))
        table[: len(freq_z)] = (weight * np.cos(angle)) @ cols_z.T
        table[LANES : LANES + len(freq_z)] = (-weight * np.sin(angle)) @ cols_z.T
        high, low = two(table)
        self.from_z = np.concatenate([high, high, low], 0)


def down(count, first, length):
    out = np.zeros((count, length))
    for j in range(count):
        for a, w in ((-1, 0.5), (0, 1.0), (1, 0.5)):
            if 0 <= first + 2 * j + a < length:
                out[j, first + 2 * j + a] = w
    return out


def dot(a, b):
    return jnp.dot(a, b, preferred_element_type=F32)


def split(value, terms):
    out = []
    for _ in range(terms - 1):
        out.append(value.astype(BF))
        value = value - out[-1].astype(F32)
    return out + [value.astype(BF)]


def stacked(value):
    high, low = split(value, 2)
    return jnp.concatenate([high, low, high], 0)


def batches(count, size, body):
    def trip(i, _):
        first = i * size
        body([first + k for k in range(size)], first)
        return 0

    whole = count // size
    if whole > 1:
        lax.fori_loop(0, whole, trip, 0)
    else:
        whole = 0
    for first in range(whole * size, count, size):
        body(list(range(first, min(count, first + size))), first)


def rows_at(first, period, count):
    return pl.ds(first * period if isinstance(first, int) else pl.multiple_of(first * period, 16), count * period)


def to_frequencies_z(read, count, size, table, terms):
    period = terms.shape[1] // count

    def body(xs, first):
        cells = jnp.concatenate([read(x) for x in xs], 0)
        size_z = cells.shape[1]
        if size_z % LANES == 0:
            value = dot(jnp.concatenate([cells, cells], 1), table[...])
        else:
            value = dot(cells, table[:size_z]) + dot(cells, table[size_z:])
        high, low = split(value, 2)
        terms[0, rows_at(first, period, len(xs)), :] = high
        terms[1, rows_at(first, period, len(xs)), :] = low

    batches(count, size, body)


def to_frequencies_y(terms, size, to_y, real, imag):
    count, period = real.shape[:2]

    def body(xs, first):
        spreads = []
        for x in xs:
            rows = rows_at(x, period, 1)
            high, low = terms[0, rows, :], terms[1, rows, :]
            spreads.append(dot(to_y[...], jnp.concatenate([high, low, high], 0)))
        for x, spread in zip(xs, spreads):
            real[x] = spread[:period, :LANES] + spread[period:, LANES:]
            imag[x] = spread[:period, LANES:] - spread[period:, :LANES]

    batches(count, size, body)


def from_frequencies_y(real, imag, size, from_y, terms):
    count = real.shape[0]
    rows = from_y.shape[0] // 2

    def body(xs, first):
        spreads = [
            dot(from_y[...], stacked(jnp.concatenate([real[x], imag[x]], 1))) for x in xs
        ]
        for x, spread in zip(xs, spreads):
            r = spread[:rows, :LANES] - spread[rows:, LANES:]
            i = spread[rows:, :LANES] + spread[:rows, LANES:]
            high, low = split(jnp.concatenate([r, i], 1), 2)
            terms[0, rows_at(x, rows, 1), :] = high
            terms[1, rows_at(x, rows, 1), :] = low

    batches(count, size, body)


def from_frequencies_z(terms, count, size, from_z, write):
    rows = terms.shape[1] // count

    def body(xs, first):
        span = rows_at(first, rows, len(xs))
        high, low = terms[0, span, :], terms[1, span, :]
        value = dot(jnp.concatenate([high, low, high], 1), from_z[...])
        for k, x in enumerate(xs):
            write(x, value[k * rows : (k + 1) * rows])

    batches(count, size, body)


def along_x(real, imag, spectrum, out_real, out_imag, block):
    kernel_r, kernel_d, kernel_s = spectrum
    taps, period = kernel_r.shape[:2]
    out_x = out_real.shape[0]

    def body(part, _):
        rows = pl.ds(pl.multiple_of(8 * part, 8), 8)
        for start in range(0, out_x, block):
            count = min(block, out_x - start)
            sums = [[None] * 3 for _ in range(count)]
            seen = {}
            for a in range(taps):
                weights = kernel_r[a, rows, :], kernel_d[a, rows, :], kernel_s[a, rows, :]
                for i in range(count):
                    x = start + i + a
                    if x not in seen:
                        r, m = real[x, rows, :], imag[x, rows, :]
                        seen[x] = r + m, r, m
                    for k in range(3):
                        term = weights[k] * seen[x][k]
                        sums[i][k] = term if a == 0 else sums[i][k] + term
            for i in range(count):
                out_real[start + i, rows, :] = sums[i][0] - sums[i][2]
                out_imag[start + i, rows, :] = sums[i][0] + sums[i][1]
        return 0

    lax.fori_loop(0, period // 8, body, 0)


def rows_loop(count, step, body):
    def trip(i, _):
        for k in range(step):
            body(i * step + k)
        return 0

    lax.fori_loop(0, count // step, trip, 0)
    for x in range(count - count % step, count):
        body(x)


def restrict_rows(read, down_y, down_z, xs):
    rows = down_y.shape[0]
    totals = [
        0.5 * read(2 * x).astype(F32) + read(2 * x + 1).astype(F32) + 0.5 * read(2 * x + 2).astype(F32)
        for x in xs
    ]
    totals = [dot(down_y[...], jnp.concatenate(split(total, 3), 0)) for total in totals]
    parts = split(jnp.concatenate(totals, 0), 3)
    value = sum(dot(part, down_z[...]) for part in reversed(parts))
    return [value[k * rows : (k + 1) * rows] for k in range(len(xs))]


def spectra_kernel(taps, kernels, *refs):
    levels = kernels.shape[0]
    tables, outs, mid = refs[: 2 * levels], refs[2 * levels : -1], refs[-1]
    for level in range(levels):
        kernel_z, kernel_y = tables[2 * level : 2 * level + 2]
        out_r, out_d, out_s = outs[3 * level : 3 * level + 3]
        period = out_r.shape[1]
        cells = kernels[level]
        mid[...] = dot(jnp.concatenate([cells, cells], 1), kernel_z[...])

        def body(xs, first, kernel_y=kernel_y, outs=(out_r, out_d, out_s), period=period):
            spreads = [dot(kernel_y[...], stacked(mid[rows_at(a, 16, 1), :])) for a in xs]
            for a, spread in zip(xs, spreads):
                real = spread[:period, :LANES] - spread[period:, LANES:]
                imag = spread[:period, LANES:] + spread[period:, :LANES]
                outs[0][a] = real
                outs[1][a] = imag - real
                outs[2][a] = imag + real

        batches(taps, 5, body)


def restrict_kernel(valid, fine, down_y, down_z, out):
    def body(xs, first):
        for t, row in zip(xs, restrict_rows(lambda x: fine[x], down_y, down_z, xs)):
            out[t] = jnp.where(t < valid[0], row, 0.0).astype(BF)

    batches(out.shape[0], 10, body)


def fine_kernel(fine, kr, kd, ks, to_z, to_y, from_y, from_z, out, real, imag, er, ei, ahead, back):
    to_frequencies_z(lambda x: fine[x], real.shape[0], 4, to_z, ahead)
    to_frequencies_y(ahead, 4, to_y, real, imag)
    along_x(real, imag, (kr, kd, ks), er, ei, 8)
    from_frequencies_y(er, ei, 4, from_y, back)

    def write(x, value):
        out[x] = value

    from_frequencies_z(back, out.shape[0], 4, from_z, write)


def coarse_kernel(
    valid,
    inside,
    mid,
    fine_e,
    down_y,
    down_z,
    mr,
    md,
    ms,
    m_to_z,
    m_to_y,
    m_from_y,
    m_from_z,
    tr,
    td,
    ts,
    t_to_z,
    t_to_y,
    t_from_y,
    t_from_z,
    out,
    m_real,
    m_imag,
    m_er,
    m_ei,
    m_out,
    t_real,
    t_imag,
    t_er,
    t_ei,
    t_out,
    m_ahead,
    m_back,
    t_cells,
    t_ahead,
    t_back,
):
    skip = (mid.shape[0] - m_real.shape[0]) // 2
    cols = (mid.shape[1] - m_real.shape[1]) // 2

    def mid_cells(x):
        return mid[x + skip, cols : cols + m_real.shape[1], :]

    to_frequencies_z(mid_cells, m_real.shape[0], 9, m_to_z, m_ahead)
    to_frequencies_y(m_ahead, 9, m_to_y, m_real, m_imag)

    def restrict_body(xs, first):
        for t, row in zip(xs, restrict_rows(lambda x: mid[x], down_y, down_z, xs)):
            t_cells[t] = jnp.where(t < valid[0], row, 0.0).astype(BF)

    batches(t_real.shape[0], 7, restrict_body)
    to_frequencies_z(lambda x: t_cells[x], t_real.shape[0], 7, t_to_z, t_ahead)
    to_frequencies_y(t_ahead, 7, t_to_y, t_real, t_imag)
    along_x(m_real, m_imag, (mr, md, ms), m_er, m_ei, 7)
    along_x(t_real, t_imag, (tr, td, ts), t_er, t_ei, 7)

    def top_write(x, value):
        t_out[x] = value

    def mid_write(x, value):
        m_out[x] = value

    from_frequencies_y(t_er, t_ei, 7, t_from_y, t_back)
    from_frequencies_y(m_er, m_ei, 7, m_from_y, m_back)
    from_frequencies_z(t_back, t_out.shape[0], 7, t_from_z, top_write)
    from_frequencies_z(m_back, m_out.shape[0], 7, m_from_z, mid_write)
    last = t_out.shape[0] - 1
    t_out[last] = t_out[last] * inside[0]
    for i in range(last):
        m_out[2 * i] += t_out[i]
        m_out[2 * i + 1] += 0.5 * (t_out[i] + t_out[i + 1])
    m_out[2 * last] = (m_out[2 * last] + t_out[last]) * inside[0]

    def finish(i):
        out[2 * i] = fine_e[2 * i] + m_out[i]
        out[2 * i + 1] = fine_e[2 * i + 1] + 0.5 * (m_out[i] + m_out[i + 1])

    rows_loop(out.shape[0] // 2, 2, finish)


def call(kernel, outs, scratch, scalars, args):
    vmem = pl.BlockSpec(memory_space=pltpu.VMEM)
    smem = pl.BlockSpec(memory_space=pltpu.SMEM)
    return pl.pallas_call(
        kernel,
        out_shape=outs,
        in_specs=[smem] * len(scalars) + [vmem] * len(args),
        out_specs=jax.tree.map(lambda _: vmem, outs),
        scratch_shapes=[pltpu.VMEM(shape, dtype) for dtype, shape in scratch],
        compiler_params=pltpu.CompilerParams(vmem_limit_bytes=60 << 20),
    )(*scalars, *args)


def spectrum_scratch(level):
    return [
        (F32, (rows, level.period_y, LANES))
        for rows in (level.in_x, level.in_x, level.out_x, level.out_x)
    ]


def terms_scratch(level, out_rows):
    return [
        (BF, (2, level.in_x * level.period_y, 2 * LANES)),
        (BF, (2, level.out_x * out_rows, 2 * LANES)),
    ]


def shifted(value, axis, by):
    length = lax.axis_size(axis)
    return lax.ppermute(
        value, axis, [(i, i + by) for i in range(length) if 0 <= i + by < length]
    )


def shards(charges, kernel_fine, kernel_mid, kernel_top):
    nx, ny, nz = charges.shape
    taps = kernel_fine.shape[0]
    half = taps // 2
    gx, gy = lax.axis_index("gx"), lax.axis_index("gy")
    left_x = lax.axis_size("gx") - gx
    end_y = gy == lax.axis_size("gy") - 1
    wide = half + 1

    ident = np.eye(ny)
    fine = Level(taps, nx, ny, wide, ny + 2 * wide, nz, ident, ident, np.eye(nz))
    my, mz = ny // 2, nz // 2
    to_fine = up(my)
    ended = np.diag([1.0] * my + [0.0])
    mid = Level(
        taps, nx // 2 + 1, my + 1, wide, my + 2 * wide, mz, to_fine, to_fine @ ended, up_closed(mz)
    )
    ty, tz = my // 2, mz // 2
    to_mid = np.concatenate([up(ty), np.eye(ty + 1)[-1:]], 0)
    top_ended = np.diag([1.0] * ty + [0.0])
    top = Level(
        taps,
        nx // 4 + 1,
        ty + 1,
        wide,
        ty + 2 * wide,
        tz,
        to_fine @ to_mid,
        to_fine @ to_mid @ top_ended,
        up_closed(mz) @ up_closed(tz),
    )

    cells = jnp.stack([kernel_fine, kernel_mid, kernel_top])
    cells = jnp.pad(cells, ((0, 0), (0, 0), (0, 1), (0, LANES - taps)))
    cells = cells.reshape(3, taps * 16, LANES)
    levels = (fine, mid, top)
    outs = [
        jax.ShapeDtypeStruct((taps, level.period_y, LANES), F32)
        for level in levels
        for _ in range(3)
    ]
    tables = [table for level in levels for table in (level.kernel_z, level.kernel_y)]
    spectra = call(
        functools.partial(spectra_kernel, taps),
        outs,
        [(F32, (taps * 16, 2 * LANES))],
        [],
        [cells, *tables],
    )

    fine_q = charges.astype(BF)
    fine_x = jnp.concatenate(
        [shifted(fine_q[-half:], "gx", 1), fine_q, shifted(fine_q[:wide], "gx", -1)], 0
    )
    fine_ext = jnp.concatenate(
        [shifted(fine_x[:, -wide:], "gy", 1), fine_x, shifted(fine_x[:, :wide], "gy", -1)], 1
    )

    lead = (half - 1) // 2
    rows = lead + nx // 2 + wide // 2
    down_y = np.tile(down(my, wide, ny + 2 * wide), (1, 3)).astype(BF)
    down_z = down(mz, 0, nz).T.astype(BF)
    valid = jnp.where(left_x == 1, lead + nx // 2, rows)[None].astype(jnp.int32)
    mid_q = call(
        restrict_kernel,
        jax.ShapeDtypeStruct((rows, my, mz), BF),
        [],
        [valid],
        [fine_ext, down_y, down_z],
    )
    mx = nx // 2
    reach = 2 * half + 1
    assert lead + mx >= reach and my >= 2 * wide
    mid_x = jnp.concatenate(
        [
            shifted(mid_q[lead + mx - reach : mx], "gx", 1),
            mid_q,
            shifted(mid_q[rows - mx :], "gx", -1),
        ],
        0,
    )
    mid_ext = jnp.concatenate(
        [
            shifted(mid_x[:, -2 * wide :], "gy", 1),
            mid_x,
            shifted(mid_x[:, : 2 * wide], "gy", -1),
        ],
        1,
    )

    fine_e = call(
        fine_kernel,
        jax.ShapeDtypeStruct((nx, ny, nz), F32),
        spectrum_scratch(fine) + terms_scratch(fine, ny),
        [],
        [
            fine_ext,
            *spectra[:3],
            fine.to_z,
            fine.to_y,
            fine.from_y[0],
            fine.from_z,
        ],
    )

    tx = nx // 4
    down_y = down(ty + 2 * wide, 0, my + 4 * wide)
    keep = jnp.arange(ty + 2 * wide)[:, None] < jnp.where(end_y, wide + ty, ty + 2 * wide)
    down_y = jnp.where(keep, np.tile(down_y, (1, 3)).astype(BF), 0)
    down_z = down(tz, 0, mz).T.astype(BF)
    valid = jnp.minimum(left_x * tx + half, top.in_x)[None].astype(jnp.int32)
    inside = jnp.where(left_x == 1, 0.0, 1.0)[None].astype(F32)

    def pick(pair):
        return jnp.where(end_y, pair[1], pair[0])

    return call(
        coarse_kernel,
        jax.ShapeDtypeStruct((nx, ny, nz), F32),
        spectrum_scratch(mid)
        + [(F32, (mid.out_x, ny, nz))]
        + spectrum_scratch(top)
        + [(F32, (top.out_x, ny, nz))]
        + terms_scratch(mid, ny)
        + [(BF, (top.in_x, top.period_y, tz))]
        + terms_scratch(top, ny),
        [valid, inside],
        [
            mid_ext,
            fine_e,
            down_y,
            down_z,
            *spectra[3:6],
            mid.to_z,
            mid.to_y,
            pick(mid.from_y),
            mid.from_z,
            *spectra[6:9],
            top.to_z,
            top.to_y,
            pick(top.from_y),
            top.from_z,
        ],
    )


def solution(mesh):
    placed = (P("gx", "gy", None), P(), P(), P())
    return jax.shard_map(
        shards, mesh=mesh, in_specs=placed, out_specs=P("gx", "gy", None), check_vma=False
    )
```

```python
import functools

import jax
import jax.numpy as jnp
import numpy as np
from jax import lax
from jax.experimental import pallas as pl
from jax.experimental.pallas import tpu as pltpu
from jax.sharding import PartitionSpec as P

BF = jnp.bfloat16
F32 = jnp.float32
LANES = 128


def two(matrix):
    high = np.asarray(matrix, np.float64).astype(BF)
    low = (matrix - high.astype(np.float64)).astype(BF)
    return high, low


def beside(real, imag):
    out = np.zeros((real.shape[0], 2 * LANES))
    out[:, : real.shape[1]] = real
    out[:, LANES : LANES + imag.shape[1]] = imag
    return out


def three_terms(matrix):
    high, low = two(matrix)
    return np.concatenate([high, high, low], 1)


def up(count):
    out = np.zeros((2 * count, count + 1))
    for i in range(count):
        out[2 * i, i] = 1.0
        out[2 * i + 1, i] = out[2 * i + 1, i + 1] = 0.5
    return out


def up_closed(count):
    return up(count)[:, :count]


def both_sides(table):
    size = table.shape[0]
    return [np.pad(table, ((at, LANES - size - at), (0, 0))) for at in (0, LANES - size)]


class Level:
    def __init__(self, taps, out_x, out_y, shift, period_y, size_z, rows_y, rows_y_end, cols_z):
        half = taps // 2
        self.taps, self.out_x, self.in_x = taps, out_x, out_x + taps - 1
        self.period_y, self.size_z = period_y, size_z
        period_z = size_z + half + (size_z + half) % 2
        assert period_y >= shift + out_y + half and shift >= half and period_y % 16 == 0
        freq_z = np.arange(period_z // 2 + 1)
        assert len(freq_z) <= LANES
        freq_y = np.arange(period_y)
        turn_z, turn_y = 2 * np.pi / period_z, 2 * np.pi / period_y
        angle = turn_z * np.outer(np.arange(size_z), freq_z)
        table = beside(np.cos(angle), -np.sin(angle))
        self.to_z = np.concatenate(two(table), 0)
        self.to_z_packed = [np.concatenate(two(side), 0) for side in both_sides(table)]
        angle = turn_y * np.outer(freq_y, np.arange(period_y))
        self.to_y = three_terms(np.concatenate([np.cos(angle), np.sin(angle)], 0))
        offsets = np.arange(taps) - half
        angle = turn_z * np.outer(offsets, freq_z)
        table = np.zeros((LANES, 2 * LANES))
        table[:taps] = beside(np.cos(angle), np.sin(angle))
        self.kernel_z = np.concatenate(two(table), 0)
        angle = turn_y * np.outer(freq_y, np.pad(offsets, (0, 1)))
        self.kernel_y = three_terms(np.concatenate([np.cos(angle), np.sin(angle)], 0))
        angle = turn_y * np.outer(np.arange(out_y) + shift, freq_y)
        self.from_y = [
            three_terms(
                np.concatenate([rows @ np.cos(angle), rows @ np.sin(angle)], 0) / period_y
            )
            for rows in (rows_y, rows_y_end)
        ]
        weight = np.where((freq_z == 0) | (2 * freq_z == period_z), 1.0, 2.0)[:, None] / period_z
        angle = turn_z * np.outer(freq_z, np.arange(size_z))
        table = np.zeros((2 * LANES, cols_z.shape[0]))
        table[: len(freq_z)] = (weight * np.cos(angle)) @ cols_z.T
        table[LANES : LANES + len(freq_z)] = (-weight * np.sin(angle)) @ cols_z.T
        high, low = two(table)
        self.from_z = np.concatenate([high, high, low], 0)


def down(count, first, length):
    out = np.zeros((count, length))
    for j in range(count):
        for a, w in ((-1, 0.5), (0, 1.0), (1, 0.5)):
            if 0 <= first + 2 * j + a < length:
                out[j, first + 2 * j + a] = w
    return out


def dot(a, b):
    return jnp.dot(a, b, preferred_element_type=F32)


def split(value, terms):
    out = []
    for _ in range(terms - 1):
        out.append(value.astype(BF))
        value = value - out[-1].astype(F32)
    return out + [value.astype(BF)]


def stacked(value):
    high, low = split(value, 2)
    return jnp.concatenate([high, low, high], 0)


def batches(count, size, body):
    def trip(i, _):
        first = i * size
        body([first + k for k in range(size)], first)
        return 0

    whole = count // size
    if whole > 1:
        lax.fori_loop(0, whole, trip, 0)
    else:
        whole = 0
    for first in range(whole * size, count, size):
        body(list(range(first, min(count, first + size))), first)


def rows_at(first, period, count):
    return pl.ds(first * period if isinstance(first, int) else pl.multiple_of(first * period, 16), count * period)


def to_frequencies_z(read, count, size, table, terms):
    period = terms.shape[1] // count

    def body(xs, first):
        cells = jnp.concatenate([read(x) for x in xs], 0)
        size_z = cells.shape[1]
        if size_z % LANES == 0:
            value = dot(jnp.concatenate([cells, cells], 1), table[...])
        else:
            value = dot(cells, table[:size_z]) + dot(cells, table[size_z:])
        high, low = split(value, 2)
        terms[0, rows_at(first, period, len(xs)), :] = high
        terms[1, rows_at(first, period, len(xs)), :] = low

    batches(count, size, body)


def to_frequencies_y(terms, size, to_y, real, imag):
    count, period = real.shape[:2]

    def body(xs, first):
        spreads = []
        for x in xs:
            rows = rows_at(x, period, 1)
            high, low = terms[0, rows, :], terms[1, rows, :]
            spreads.append(dot(to_y[...], jnp.concatenate([high, low, high], 0)))
        for x, spread in zip(xs, spreads):
            real[x] = spread[:period, :LANES] + spread[period:, LANES:]
            imag[x] = spread[:period, LANES:] - spread[period:, :LANES]

    batches(count, size, body)


def from_frequencies_y(real, imag, size, from_y, terms):
    count = real.shape[0]
    rows = from_y.shape[0] // 2

    def body(xs, first):
        spreads = [
            dot(from_y[...], stacked(jnp.concatenate([real[x], imag[x]], 1))) for x in xs
        ]
        for x, spread in zip(xs, spreads):
            r = spread[:rows, :LANES] - spread[rows:, LANES:]
            i = spread[rows:, :LANES] + spread[:rows, LANES:]
            high, low = split(jnp.concatenate([r, i], 1), 2)
            terms[0, rows_at(x, rows, 1), :] = high
            terms[1, rows_at(x, rows, 1), :] = low

    batches(count, size, body)


def from_frequencies_z(terms, count, size, from_z, write):
    rows = terms.shape[1] // count

    def body(xs, first):
        span = rows_at(first, rows, len(xs))
        high, low = terms[0, span, :], terms[1, span, :]
        value = dot(jnp.concatenate([high, low, high], 1), from_z[...])
        for k, x in enumerate(xs):
            write(x, value[k * rows : (k + 1) * rows])

    batches(count, size, body)


def along_x(real, imag, spectrum, out_real, out_imag, block):
    kernel_r, kernel_d, kernel_s = spectrum
    taps, period = kernel_r.shape[:2]
    out_x = out_real.shape[0]

    def body(part, _):
        rows = pl.ds(pl.multiple_of(8 * part, 8), 8)
        for start in range(0, out_x, block):
            count = min(block, out_x - start)
            sums = [[None] * 3 for _ in range(count)]
            seen = {}
            for a in range(taps):
                weights = kernel_r[a, rows, :], kernel_d[a, rows, :], kernel_s[a, rows, :]
                for i in range(count):
                    x = start + i + a
                    if x not in seen:
                        r, m = real(x, rows), imag(x, rows)
                        seen[x] = r + m, r, m
                    for k in range(3):
                        term = weights[k] * seen[x][k]
                        sums[i][k] = term if a == 0 else sums[i][k] + term
            for i in range(count):
                out_real[start + i, rows, :] = sums[i][0] - sums[i][2]
                out_imag[start + i, rows, :] = sums[i][0] + sums[i][1]
        return 0

    lax.fori_loop(0, period // 8, body, 0)


def rows_loop(count, step, body):
    def trip(i, _):
        for k in range(step):
            body(i * step + k)
        return 0

    lax.fori_loop(0, count // step, trip, 0)
    for x in range(count - count % step, count):
        body(x)


def all_terms(value):
    return jnp.concatenate(split(value, 3), 0)


def spectra_kernel(levels, *refs):
    kernels, refs = refs[:levels], refs[levels:]
    tables, outs, (padded, mid) = refs[: 2 * levels], refs[2 * levels : -2], refs[-2:]
    taps = kernels[0].shape[0]
    padded[...] = jnp.zeros(padded.shape, padded.dtype)
    for level in range(levels):
        kernel_z, kernel_y = tables[2 * level : 2 * level + 2]
        outs_here = outs[3 * level : 3 * level + 3]
        period = outs_here[0].shape[1]
        padded[:, :taps, :taps] = kernels[level][...].astype(F32)
        cells = padded[...].astype(BF).reshape(taps * padded.shape[1], LANES)
        mid[...] = dot(jnp.concatenate([cells, cells], 1), kernel_z[...])

        def body(xs, first, kernel_y=kernel_y, outs=outs_here, period=period):
            spreads = [dot(kernel_y[...], stacked(mid[rows_at(a, 16, 1), :])) for a in xs]
            for a, spread in zip(xs, spreads):
                real = spread[:period, :LANES] - spread[period:, LANES:]
                imag = spread[:period, LANES:] + spread[period:, :LANES]
                outs[0][a] = real
                outs[1][a] = imag - real
                outs[2][a] = imag + real

        batches(taps, 5, body)


def pack_kernel(
    ended, own, left, right, down_z, down_y, ordered, near, coarse, to_right, to_left, far_right, far_left, part
):
    count, size = own.shape[:2]
    side = left.shape[1]
    width = near.shape[1]
    start = side - (width - size) // 2
    window = part.shape[1]

    def body(xs, first):
        rows = []
        for x in xs:
            l, o, r = left[x], own[x], right[x]
            near[x] = jnp.concatenate([l[start:], o, r[: side - start]], 0)
            low = jnp.concatenate([l, o[: window - side]], 0)
            high = jnp.concatenate([o[size + side - window :], r], 0)
            rows.append(jnp.concatenate([low, high], 1))
        value = dot(jnp.concatenate(rows, 0), down_z[...])
        for k, x in enumerate(xs):
            part[x] = value[k * window : (k + 1) * window]

    batches(count, 4, body)
    half = down_y.shape[0] // 2
    shape = (half, LANES)
    high_lanes = lax.broadcasted_iota(jnp.int32, shape, 1) >= LANES // 2
    outside = high_lanes & (lax.broadcasted_iota(jnp.int32, shape, 0) >= half // 2)
    outside = outside & (ended[0] == 1)
    last = count // 2
    totals = []
    for i in range(last + 1):
        if i == 0:
            total = part[0] + 0.5 * part[1]
        elif i == last:
            total = 0.5 * part[count - 1]
        else:
            total = 0.5 * part[2 * i - 1] + part[2 * i] + 0.5 * part[2 * i + 1]
        totals.append(dot(down_y[...], all_terms(total)))
    for i, total in enumerate(totals):
        row = jnp.where(high_lanes, total[half:], total[:half])
        row = jnp.where(outside, 0.0, row)
        if i == 0:
            for k, term in enumerate(split(row, 3)):
                coarse[k] = term
        elif i == last:
            for k, term in enumerate(split(row, 3)):
                coarse[last + 2 + k] = term
        else:
            coarse[i + 2] = row.astype(BF)
    for out, rows in ((to_right, to_right.shape[0]), (to_left, to_left.shape[0])):
        lines = rows - coarse.shape[0] * half
        first = count - lines // width if out is to_right else 0
        for x in range(lines // width):
            out[x * width : (x + 1) * width, :] = near[first + x]
        for k in range(coarse.shape[0]):
            out[lines + k * half : lines + (k + 1) * half, :] = coarse[k]
    shift = coarse.shape[0] - far_right.shape[0]
    for k in range(far_right.shape[0]):
        far_right[k] = coarse[shift + k]
        far_left[k] = coarse[k]


def own_kernel(near, to_z, to_y, real, imag, ahead):
    to_frequencies_z(lambda x: near[x], real.shape[0], 4, to_z, ahead)
    to_frequencies_y(ahead, 4, to_y, real, imag)


def final_kernel(
    limits,
    own_real,
    own_imag,
    from_left,
    from_right,
    far_left,
    far_right,
    coarse,
    kr,
    kd,
    ks,
    to_z,
    to_y,
    from_y,
    from_z,
    mr,
    md,
    ms,
    m_low,
    m_high,
    m_to_y,
    m_from_y,
    m_from_z,
    tr,
    td,
    ts,
    t_down_y,
    t_down_z,
    t_to_z,
    t_to_y,
    t_from_y,
    t_from_z,
    out,
    side_real,
    side_imag,
    er,
    ei,
    ahead,
    back,
    mid,
    m_real,
    m_imag,
    m_er,
    m_ei,
    m_ahead,
    m_back,
    m_out,
    t_real,
    t_imag,
    t_er,
    t_ei,
    t_cells,
    t_ahead,
    t_back,
    t_out,
):
    top_rows, ended_x, close_x, ended_y = limits[0], limits[1], limits[2], limits[3]
    count, width = own_real.shape[:2]
    reach = side_real.shape[0] // 2

    def side_cells(x):
        ref, first = (from_left, x) if x < reach else (from_right, x - reach)
        return ref[first * width : (first + 1) * width, :]

    period = width
    for first in range(0, 2 * reach, 4):
        xs = list(range(first, min(2 * reach, first + 4)))
        cells = jnp.concatenate([side_cells(x) for x in xs], 0)
        value = dot(jnp.concatenate([cells, cells], 1), to_z[...])
        high, low = split(value, 2)
        ahead[0, rows_at(first, period, len(xs)), :] = high
        ahead[1, rows_at(first, period, len(xs)), :] = low
    to_frequencies_y(ahead, 7, to_y, side_real, side_imag)

    def source(own, side):
        def read(x, rows):
            if x < reach:
                return side[x, rows, :]
            if x < reach + count:
                return own[x - reach, rows, :]
            return side[x - count, rows, :]

        return read

    along_x(source(own_real, side_real), source(own_imag, side_imag), (kr, kd, ks), er, ei, 8)
    from_frequencies_y(er, ei, 4, from_y, back)

    def fine_write(x, value):
        out[x] = value

    from_frequencies_z(back, count, 4, from_z, fine_write)

    half = mid.shape[1]
    last = count // 2
    skip_left = from_left.shape[0] - coarse.shape[0] * half
    skip_right = from_right.shape[0] - coarse.shape[0] * half

    def left_row(k):
        return from_left[skip_left + k * half : skip_left + (k + 1) * half, :]

    def right_row(k):
        return from_right[skip_right + k * half : skip_right + (k + 1) * half, :]

    def added(first, second, dropped=None):
        value = sum(first(2 - k).astype(F32) for k in range(3))
        value = value + sum(second(last + 4 - k).astype(F32) for k in range(3))
        if dropped is not None:
            value = jnp.where(dropped == 1, 0.0, value)
        return value.astype(BF)

    spare = far_left.shape[0] - 3
    far_first = coarse.shape[0] - far_left.shape[0]
    rows = [far_left[k] for k in range(spare)]
    rows += [added(left_row, lambda k: far_left[k - far_first])]
    rows += [left_row(k) for k in range(3, last + 2)]
    rows += [added(lambda k: coarse[k], left_row)]
    rows += [coarse[k] for k in range(3, last + 2)]
    rows += [added(right_row, lambda k: coarse[k], ended_x)]
    rows += [right_row(k) for k in range(3, last + 2)]
    rows += [added(lambda k: far_right[k], right_row, close_x)]
    rows += [far_right[k] for k in range(3, 3 + spare)]
    for k, row in enumerate(rows):
        mid[k] = row

    skip = (mid.shape[0] - m_real.shape[0]) // 2
    m_width = m_real.shape[1]
    cut = half - m_width // 2

    def mid_z(xs, first):
        cells = jnp.concatenate([mid[x + skip] for x in xs], 0)
        cells = jnp.concatenate([cells, cells], 1)
        low, high = dot(cells, m_low[...]), dot(cells, m_high[...])
        parts = []
        for k in range(len(xs)):
            parts += [low[k * half + cut : (k + 1) * half], high[k * half : (k + 1) * half - cut]]
        high, low = split(jnp.concatenate(parts, 0), 2)
        m_ahead[0, rows_at(first, m_width, len(xs)), :] = high
        m_ahead[1, rows_at(first, m_width, len(xs)), :] = low

    batches(m_real.shape[0], 9, mid_z)
    to_frequencies_y(m_ahead, 9, m_to_y, m_real, m_imag)

    t_width = t_real.shape[1]
    inside = lax.broadcasted_iota(jnp.int32, (t_width, t_cells.shape[2]), 0)
    inside = inside < jnp.where(ended_y == 1, t_width - (t_width - last_columns(t_width, m_width)) // 2, t_width)

    def top_cells(xs, first):
        spreads = []
        for t in xs:
            total = 0.5 * mid[2 * t].astype(F32) + mid[2 * t + 1].astype(F32) + 0.5 * mid[2 * t + 2].astype(F32)
            spreads.append(dot(t_down_y[...], all_terms(total)))
        low = jnp.concatenate([spread[:t_width] for spread in spreads], 0)
        high = jnp.concatenate([spread[t_width:] for spread in spreads], 0)
        value = dot(jnp.concatenate(split(low, 3) + split(high, 3), 1), t_down_z[...])
        for k, t in enumerate(xs):
            row = jnp.where(inside, value[k * t_width : (k + 1) * t_width], 0.0)
            t_cells[t] = jnp.where(t < top_rows, row, 0.0).astype(BF)

    batches(t_real.shape[0], 7, top_cells)
    to_frequencies_z(lambda x: t_cells[x], t_real.shape[0], 7, t_to_z, t_ahead)
    to_frequencies_y(t_ahead, 7, t_to_y, t_real, t_imag)

    def plain(ref):
        return lambda x, rows: ref[x, rows, :]

    along_x(plain(m_real), plain(m_imag), (mr, md, ms), m_er, m_ei, 7)
    along_x(plain(t_real), plain(t_imag), (tr, td, ts), t_er, t_ei, 7)

    def top_write(x, value):
        t_out[x] = value

    def mid_write(x, value):
        m_out[x] = value

    from_frequencies_y(t_er, t_ei, 7, t_from_y.at[ended_y], t_back)
    from_frequencies_y(m_er, m_ei, 7, m_from_y.at[ended_y], m_back)
    from_frequencies_z(t_back, t_out.shape[0], 7, t_from_z, top_write)
    from_frequencies_z(m_back, m_out.shape[0], 7, m_from_z, mid_write)
    keep = jnp.where(ended_x == 1, 0.0, 1.0)
    top = t_out.shape[0] - 1
    t_out[top] = t_out[top] * keep
    for i in range(top):
        m_out[2 * i] += t_out[i]
        m_out[2 * i + 1] += 0.5 * (t_out[i] + t_out[i + 1])
    m_out[2 * top] = (m_out[2 * top] + t_out[top]) * keep

    def finish(i):
        out[2 * i] += m_out[i]
        out[2 * i + 1] += 0.5 * (m_out[i] + m_out[i + 1])

    rows_loop(count // 2, 2, finish)


def last_columns(t_width, m_width):
    return m_width - t_width


def call(kernel, outs, scratch, scalars, args, loose=()):
    vmem = pl.BlockSpec(memory_space=pltpu.VMEM)
    smem = pl.BlockSpec(memory_space=pltpu.SMEM)
    return pl.pallas_call(
        kernel,
        out_shape=outs,
        in_specs=[
            smem if i < len(scalars) else pl.BlockSpec(memory_space=pl.ANY) if i in loose else vmem
            for i in range(len(scalars) + len(args))
        ],
        out_specs=jax.tree.map(lambda _: vmem, outs),
        scratch_shapes=[pltpu.VMEM(shape, dtype) for dtype, shape in scratch],
        compiler_params=pltpu.CompilerParams(vmem_limit_bytes=60 << 20),
    )(*scalars, *args)


def level_scratch(level, ny, nz, extra=()):
    rows = [
        (F32, (count, level.period_y, LANES))
        for count in (level.in_x, level.in_x, level.out_x, level.out_x)
    ]
    terms = [
        (BF, (2, level.in_x * level.period_y, 2 * LANES)),
        (BF, (2, level.out_x * ny, 2 * LANES)),
    ]
    return [*rows, *extra, *terms, (F32, (level.out_x, ny, nz))]


def shifted(value, axis, by):
    length = lax.axis_size(axis)
    return lax.ppermute(
        value, axis, [(i, i + by) for i in range(length) if 0 <= i + by < length]
    )


def shards(charges, kernel_fine, kernel_mid, kernel_top):
    nx, ny, nz = charges.shape
    taps = kernel_fine.shape[0]
    half = taps // 2
    gx, gy = lax.axis_index("gx"), lax.axis_index("gy")
    left_x = lax.axis_size("gx") - gx
    end_y = gy == lax.axis_size("gy") - 1
    wide = half + 1

    ident = np.eye(ny)
    fine = Level(taps, nx, ny, wide, ny + 2 * wide, nz, ident, ident, np.eye(nz))
    my, mz = ny // 2, nz // 2
    to_fine = up(my)
    ended = np.diag([1.0] * my + [0.0])
    mid = Level(
        taps, nx // 2 + 1, my + 1, wide, my + 2 * wide, mz, to_fine, to_fine @ ended, up_closed(mz)
    )
    ty, tz = my // 2, mz // 2
    to_mid = np.concatenate([up(ty), np.eye(ty + 1)[-1:]], 0)
    top_ended = np.diag([1.0] * ty + [0.0])
    top = Level(
        taps,
        nx // 4 + 1,
        ty + 1,
        wide,
        ty + 2 * wide,
        tz,
        to_fine @ to_mid,
        to_fine @ to_mid @ top_ended,
        up_closed(mz) @ up_closed(tz),
    )

    levels = (fine, mid, top)
    outs = [
        jax.ShapeDtypeStruct((taps, level.period_y, LANES), F32)
        for level in levels
        for _ in range(3)
    ]
    tables = [table for level in levels for table in (level.kernel_z, level.kernel_y)]
    spectra = call(
        functools.partial(spectra_kernel, 3),
        outs,
        [(F32, (taps, 16, LANES)), (F32, (taps * 16, 2 * LANES))],
        [],
        [kernel_fine, kernel_mid, kernel_top, *tables],
    )

    fine_q = charges.astype(BF)
    side = ny // 2
    from_below = shifted(fine_q[:, ny - side :], "gy", 1)
    from_above = shifted(fine_q[:, :side], "gy", -1)

    window = side + ny // 2 + 16
    packed = ny // 2
    down_z = np.concatenate([np.pad(down(mz, 0, nz).T, ((0, 0), (at, mz - at))) for at in (0, mz)], 0)
    shift = ny + 2 * side - window
    down_y = np.concatenate([down(packed, 0, window), down(packed, 2 * packed - shift, window)], 0)
    mx = nx // 2
    lines = mx - 1 + 6
    reach = 2 * half + 1 - mx
    assert 0 < reach <= mx - 1 and 2 * mz == LANES == nz
    ended = end_y.astype(jnp.int32)
    shapes = [
        (nx, fine.period_y, LANES),
        (lines, packed, LANES),
        (half * fine.period_y + lines * packed, LANES),
        (half * fine.period_y + lines * packed, LANES),
        (reach + 3, packed, LANES),
        (reach + 3, packed, LANES),
    ]
    near, coarse, to_right, to_left, far_right, far_left = call(
        pack_kernel,
        [jax.ShapeDtypeStruct(shape, BF) for shape in shapes],
        [(F32, (nx, window, LANES))],
        [ended[None]],
        [
            fine_q,
            from_below,
            from_above,
            down_z.astype(BF),
            np.tile(down_y, (1, 3)).astype(BF),
            spectra[0],
        ],
        loose=(6,),
    )
    from_left = shifted(to_right, "gx", 1)
    from_right = shifted(to_left, "gx", -1)
    from_far_left = shifted(far_right, "gx", 2)
    from_far_right = shifted(far_left, "gx", -2)

    own = call(
        own_kernel,
        [jax.ShapeDtypeStruct((nx, fine.period_y, LANES), F32)] * 2,
        [(BF, (2, nx * fine.period_y, 2 * LANES))],
        [],
        [near, fine.to_z, fine.to_y],
    )

    tx = nx // 4
    wide_top = ty + 2 * wide
    t_down_y = down(wide_top, 0, 2 * packed)
    t_down_y = np.concatenate([t_down_y[:, :packed], t_down_y[:, packed:]], 0)
    t_down_z = np.concatenate(
        [np.tile(table, (3, 1)) for table in both_sides(down(tz, 0, mz).T)], 0
    )
    limits = jnp.stack(
        [
            jnp.minimum(left_x * tx + half, top.in_x),
            (left_x == 1).astype(jnp.int32),
            (left_x <= 2).astype(jnp.int32),
            ended,
        ]
    ).astype(jnp.int32)
    return call(
        final_kernel,
        jax.ShapeDtypeStruct((nx, ny, nz), F32),
        [
            (F32, (2 * half, fine.period_y, LANES)),
            (F32, (2 * half, fine.period_y, LANES)),
            (F32, (nx, fine.period_y, LANES)),
            (F32, (nx, fine.period_y, LANES)),
            (BF, (2, 2 * half * fine.period_y, 2 * LANES)),
            (BF, (2, nx * ny, 2 * LANES)),
            (BF, (3 * mx + 1 + 2 * reach, packed, LANES)),
            *level_scratch(mid, ny, nz),
            *level_scratch(top, ny, nz, [(BF, (top.in_x, top.period_y, tz))]),
        ],
        [limits],
        [
            *own,
            from_left,
            from_right,
            from_far_left,
            from_far_right,
            coarse,
            *spectra[:3],
            fine.to_z,
            fine.to_y,
            fine.from_y[0],
            fine.from_z,
            *spectra[3:6],
            *mid.to_z_packed,
            mid.to_y,
            np.stack(mid.from_y),
            mid.from_z,
            *spectra[6:],
            np.tile(t_down_y, (1, 3)).astype(BF),
            t_down_z.astype(BF),
            top.to_z,
            top.to_y,
            np.stack(top.from_y),
            top.from_z,
        ],
    )


def solution(mesh):
    placed = (P("gx", "gy", None), P(), P(), P())
    return jax.shard_map(
        shards, mesh=mesh, in_specs=placed, out_specs=P("gx", "gy", None), check_vma=False
    )
```

```python
import functools

import jax
import jax.numpy as jnp
import numpy as np
from jax import lax
from jax.experimental import pallas as pl
from jax.experimental.pallas import tpu as pltpu
from jax.sharding import PartitionSpec as P

BF = jnp.bfloat16
F32 = jnp.float32
LANES = 128


def two(matrix):
    high = np.asarray(matrix, np.float64).astype(BF)
    low = (matrix - high.astype(np.float64)).astype(BF)
    return high, low


def beside(real, imag):
    out = np.zeros((real.shape[0], 2 * LANES))
    out[:, : real.shape[1]] = real
    out[:, LANES : LANES + imag.shape[1]] = imag
    return out


def three_terms(matrix):
    high, low = two(matrix)
    return np.concatenate([high, high, low], 1)


def up(count):
    out = np.zeros((2 * count, count + 1))
    for i in range(count):
        out[2 * i, i] = 1.0
        out[2 * i + 1, i] = out[2 * i + 1, i + 1] = 0.5
    return out


def up_closed(count):
    return up(count)[:, :count]


def both_sides(table):
    size = table.shape[0]
    return [np.pad(table, ((at, LANES - size - at), (0, 0))) for at in (0, LANES - size)]


class Level:
    def __init__(self, taps, out_x, out_y, shift, period_y, size_z, rows_y, rows_y_end, cols_z):
        half = taps // 2
        self.taps, self.out_x, self.in_x = taps, out_x, out_x + taps - 1
        self.period_y, self.size_z = period_y, size_z
        period_z = size_z + half + (size_z + half) % 2
        assert period_y >= shift + out_y + half and shift >= half and period_y % 16 == 0
        freq_z = np.arange(period_z // 2 + 1)
        assert len(freq_z) <= LANES
        freq_y = np.arange(period_y)
        turn_z, turn_y = 2 * np.pi / period_z, 2 * np.pi / period_y
        angle = turn_z * np.outer(np.arange(size_z), freq_z)
        table = beside(np.cos(angle), -np.sin(angle))
        self.to_z = np.concatenate(two(table), 0)
        self.to_z_packed = [np.concatenate(two(side), 0) for side in both_sides(table)]
        angle = turn_y * np.outer(freq_y, np.arange(period_y))
        self.to_y = three_terms(np.concatenate([np.cos(angle), np.sin(angle)], 0))
        offsets = np.arange(taps) - half
        angle = turn_z * np.outer(offsets, freq_z)
        table = np.zeros((LANES, 2 * LANES))
        table[:taps] = beside(np.cos(angle), np.sin(angle))
        self.kernel_z = np.concatenate(two(table), 0)
        angle = turn_y * np.outer(freq_y, np.pad(offsets, (0, 1)))
        self.kernel_y = three_terms(np.concatenate([np.cos(angle), np.sin(angle)], 0))
        angle = turn_y * np.outer(np.arange(out_y) + shift, freq_y)
        self.from_y = [
            three_terms(
                np.concatenate([rows @ np.cos(angle), rows @ np.sin(angle)], 0) / period_y
            )
            for rows in (rows_y, rows_y_end)
        ]
        weight = np.where((freq_z == 0) | (2 * freq_z == period_z), 1.0, 2.0)[:, None] / period_z
        angle = turn_z * np.outer(freq_z, np.arange(size_z))
        table = np.zeros((2 * LANES, cols_z.shape[0]))
        table[: len(freq_z)] = (weight * np.cos(angle)) @ cols_z.T
        table[LANES : LANES + len(freq_z)] = (-weight * np.sin(angle)) @ cols_z.T
        high, low = two(table)
        self.from_z = np.concatenate([high, high, low], 0)


def down(count, first, length):
    out = np.zeros((count, length))
    for j in range(count):
        for a, w in ((-1, 0.5), (0, 1.0), (1, 0.5)):
            if 0 <= first + 2 * j + a < length:
                out[j, first + 2 * j + a] = w
    return out


def dot(a, b):
    return jnp.dot(a, b, preferred_element_type=F32)


def split(value, terms):
    out = []
    for _ in range(terms - 1):
        out.append(value.astype(BF))
        value = value - out[-1].astype(F32)
    return out + [value.astype(BF)]


def stacked(value):
    high, low = split(value, 2)
    return jnp.concatenate([high, low, high], 0)


def batches(count, size, body):
    def trip(i, _):
        first = i * size
        body([first + k for k in range(size)], first)
        return 0

    whole = count // size
    if whole > 1:
        lax.fori_loop(0, whole, trip, 0)
    else:
        whole = 0
    for first in range(whole * size, count, size):
        body(list(range(first, min(count, first + size))), first)


def rows_at(first, period, count):
    return pl.ds(first * period if isinstance(first, int) else pl.multiple_of(first * period, 16), count * period)


def to_frequencies_z(read, count, size, table, terms):
    period = terms.shape[1] // count

    def body(xs, first):
        cells = jnp.concatenate([read(x) for x in xs], 0)
        size_z = cells.shape[1]
        if size_z % LANES == 0:
            value = dot(jnp.concatenate([cells, cells], 1), table[...])
        else:
            value = dot(cells, table[:size_z]) + dot(cells, table[size_z:])
        high, low = split(value, 2)
        terms[0, rows_at(first, period, len(xs)), :] = high
        terms[1, rows_at(first, period, len(xs)), :] = low

    batches(count, size, body)


def to_frequencies_y(terms, size, to_y, real, imag):
    count, period = real.shape[:2]

    def body(xs, first):
        spreads = []
        for x in xs:
            rows = rows_at(x, period, 1)
            high, low = terms[0, rows, :], terms[1, rows, :]
            spreads.append(dot(to_y[...], jnp.concatenate([high, low, high], 0)))
        for x, spread in zip(xs, spreads):
            real[x] = spread[:period, :LANES] + spread[period:, LANES:]
            imag[x] = spread[:period, LANES:] - spread[period:, :LANES]

    batches(count, size, body)


def from_frequencies_y(real, imag, size, from_y, terms):
    count = real.shape[0]
    rows = from_y.shape[0] // 2

    def body(xs, first):
        spreads = [
            dot(from_y[...], stacked(jnp.concatenate([real[x], imag[x]], 1))) for x in xs
        ]
        for x, spread in zip(xs, spreads):
            r = spread[:rows, :LANES] - spread[rows:, LANES:]
            i = spread[rows:, :LANES] + spread[:rows, LANES:]
            high, low = split(jnp.concatenate([r, i], 1), 2)
            terms[0, rows_at(x, rows, 1), :] = high
            terms[1, rows_at(x, rows, 1), :] = low

    batches(count, size, body)


def from_frequencies_z(terms, count, size, from_z, write):
    rows = terms.shape[1] // count

    def body(xs, first):
        span = rows_at(first, rows, len(xs))
        high, low = terms[0, span, :], terms[1, span, :]
        value = dot(jnp.concatenate([high, low, high], 1), from_z[...])
        for k, x in enumerate(xs):
            write(x, value[k * rows : (k + 1) * rows])

    batches(count, size, body)


def along_x(real, imag, spectrum, out_real, out_imag, block):
    kernel_r, kernel_d, kernel_s = spectrum
    taps, period = kernel_r.shape[:2]
    out_x = out_real.shape[0]

    def body(part, _):
        rows = pl.ds(pl.multiple_of(8 * part, 8), 8)
        for start in range(0, out_x, block):
            count = min(block, out_x - start)
            sums = [[None] * 3 for _ in range(count)]
            seen = {}
            for a in range(taps):
                weights = kernel_r[a, rows, :], kernel_d[a, rows, :], kernel_s[a, rows, :]
                for i in range(count):
                    x = start + i + a
                    if x not in seen:
                        r, m = real(x, rows), imag(x, rows)
                        seen[x] = r + m, r, m
                    for k in range(3):
                        term = weights[k] * seen[x][k]
                        sums[i][k] = term if a == 0 else sums[i][k] + term
            for i in range(count):
                out_real[start + i, rows, :] = sums[i][0] - sums[i][2]
                out_imag[start + i, rows, :] = sums[i][0] + sums[i][1]
        return 0

    lax.fori_loop(0, period // 8, body, 0)


def rows_loop(count, step, body):
    def trip(i, _):
        for k in range(step):
            body(i * step + k)
        return 0

    lax.fori_loop(0, count // step, trip, 0)
    for x in range(count - count % step, count):
        body(x)


def all_terms(value):
    return jnp.concatenate(split(value, 3), 0)


def spectra_kernel(levels, *refs):
    kernels, refs = refs[:levels], refs[levels:]
    tables, outs, (padded, mid) = refs[: 2 * levels], refs[2 * levels : -2], refs[-2:]
    taps = kernels[0].shape[0]
    padded[...] = jnp.zeros(padded.shape, padded.dtype)
    for level in range(levels):
        kernel_z, kernel_y = tables[2 * level : 2 * level + 2]
        outs_here = outs[3 * level : 3 * level + 3]
        period = outs_here[0].shape[1]
        padded[:, :taps, :taps] = kernels[level][...].astype(F32)
        cells = padded[...].astype(BF).reshape(taps * padded.shape[1], LANES)
        mid[...] = dot(jnp.concatenate([cells, cells], 1), kernel_z[...])

        def body(xs, first, kernel_y=kernel_y, outs=outs_here, period=period):
            spreads = [dot(kernel_y[...], stacked(mid[rows_at(a, 16, 1), :])) for a in xs]
            for a, spread in zip(xs, spreads):
                real = spread[:period, :LANES] - spread[period:, LANES:]
                imag = spread[:period, LANES:] + spread[period:, :LANES]
                outs[0][a] = real
                outs[1][a] = imag - real
                outs[2][a] = imag + real

        batches(taps, 5, body)


def chosen(flag, first, second):
    return jnp.where(flag, first, second)


def pack_kernel(
    own, got_a, got_b, down_z, down_y, ordered, near, coarse, next_a, next_b, far_a, far_b, part
):
    count, size = own.shape[:2]
    side = got_a.shape[1]
    up_y, up_x, up_far = leads("gy", 1), leads("gx", 1), leads("gx", 2)
    ended = lax.axis_index("gy") == lax.axis_size("gy") - 1
    width = near.shape[1]
    start = side - (width - size) // 2
    window = part.shape[1]

    def body(xs, first):
        rows = []
        for x in xs:
            a, b, o = got_a[x], got_b[x], own[x].astype(BF)
            l, r = chosen(up_y, b, a), chosen(up_y, a, b)
            near[x] = jnp.concatenate([l[start:], o, r[: side - start]], 0)
            low = jnp.concatenate([l, o[: window - side]], 0)
            high = jnp.concatenate([o[size + side - window :], r], 0)
            rows.append(jnp.concatenate([low, high], 1))
        value = dot(jnp.concatenate(rows, 0), down_z[...])
        for k, x in enumerate(xs):
            part[x] = value[k * window : (k + 1) * window]

    batches(count, 4, body)
    half = down_y.shape[0] // 2
    shape = (half, LANES)
    high_lanes = lax.broadcasted_iota(jnp.int32, shape, 1) >= LANES // 2
    outside = high_lanes & (lax.broadcasted_iota(jnp.int32, shape, 0) >= half // 2)
    outside = outside & ended
    last = count // 2
    totals = []
    for i in range(last + 1):
        if i == 0:
            total = part[0] + 0.5 * part[1]
        elif i == last:
            total = 0.5 * part[count - 1]
        else:
            total = 0.5 * part[2 * i - 1] + part[2 * i] + 0.5 * part[2 * i + 1]
        totals.append(dot(down_y[...], all_terms(total)))
    for i, total in enumerate(totals):
        row = jnp.where(high_lanes, total[half:], total[:half])
        row = jnp.where(outside, 0.0, row)
        if i == 0:
            for k, term in enumerate(split(row, 3)):
                coarse[k] = term
        elif i == last:
            for k, term in enumerate(split(row, 3)):
                coarse[last + 2 + k] = term
        else:
            coarse[i + 2] = row.astype(BF)
    lines = next_a.shape[0] - coarse.shape[0] * half
    tail = count - lines // width
    far_tail = coarse.shape[0] - far_a.shape[0]
    for out, upward in ((next_a, up_x), (next_b, jnp.logical_not(up_x))):
        first = jnp.where(upward, tail, 0)
        for x in range(lines // width):
            out[x * width : (x + 1) * width, :] = near[first + x]
        for k in range(coarse.shape[0]):
            out[lines + k * half : lines + (k + 1) * half, :] = coarse[k]
    for out, upward in ((far_a, up_far), (far_b, jnp.logical_not(up_far))):
        first = jnp.where(upward, far_tail, 0)
        for k in range(far_a.shape[0]):
            out[k] = coarse[first + k]


def own_kernel(near, to_z, to_y, real, imag, ahead):
    to_frequencies_z(lambda x: near[x], real.shape[0], 4, to_z, ahead)
    to_frequencies_y(ahead, 4, to_y, real, imag)


def final_kernel(
    own_real,
    own_imag,
    next_a,
    next_b,
    far_a,
    far_b,
    coarse,
    kr,
    kd,
    ks,
    to_z,
    to_y,
    from_y,
    from_z,
    mr,
    md,
    ms,
    m_low,
    m_high,
    m_to_y,
    m_from_y,
    m_from_z,
    tr,
    td,
    ts,
    t_down_y,
    t_down_z,
    t_to_z,
    t_to_y,
    t_from_y,
    t_from_z,
    out,
    side_real,
    side_imag,
    er,
    ei,
    ahead,
    back,
    mid,
    m_real,
    m_imag,
    m_er,
    m_ei,
    m_ahead,
    m_back,
    m_out,
    t_real,
    t_imag,
    t_er,
    t_ei,
    t_cells,
    t_ahead,
    t_back,
    t_out,
):
    left_x = lax.axis_size("gx") - lax.axis_index("gx")
    ended_x, close_x = left_x == 1, left_x <= 2
    ended_y = (lax.axis_index("gy") == lax.axis_size("gy") - 1).astype(jnp.int32)
    up_x, up_far = leads("gx", 1), leads("gx", 2)
    count, width = own_real.shape[:2]
    reach = side_real.shape[0] // 2
    top_rows = left_x * (count // 4) + reach

    def from_left(at):
        return chosen(up_x, next_b[at, :], next_a[at, :])

    def from_right(at):
        return chosen(up_x, next_a[at, :], next_b[at, :])

    def far_left(k):
        return chosen(up_far, far_b[k], far_a[k])

    def far_right(k):
        return chosen(up_far, far_a[k], far_b[k])

    def side_cells(x):
        read, first = (from_left, x) if x < reach else (from_right, x - reach)
        return read(slice(first * width, (first + 1) * width))

    period = width
    for first in range(0, 2 * reach, 4):
        xs = list(range(first, min(2 * reach, first + 4)))
        cells = jnp.concatenate([side_cells(x) for x in xs], 0)
        value = dot(jnp.concatenate([cells, cells], 1), to_z[...])
        high, low = split(value, 2)
        ahead[0, rows_at(first, period, len(xs)), :] = high
        ahead[1, rows_at(first, period, len(xs)), :] = low
    to_frequencies_y(ahead, 7, to_y, side_real, side_imag)

    def source(own, side):
        def read(x, rows):
            if x < reach:
                return side[x, rows, :]
            if x < reach + count:
                return own[x - reach, rows, :]
            return side[x - count, rows, :]

        return read

    along_x(source(own_real, side_real), source(own_imag, side_imag), (kr, kd, ks), er, ei, 8)
    from_frequencies_y(er, ei, 4, from_y, back)

    def fine_write(x, value):
        out[x] = value

    from_frequencies_z(back, count, 4, from_z, fine_write)

    half = mid.shape[1]
    last = count // 2
    lines = next_a.shape[0] - coarse.shape[0] * half

    def left_row(k):
        return from_left(slice(lines + k * half, lines + (k + 1) * half))

    def right_row(k):
        return from_right(slice(lines + k * half, lines + (k + 1) * half))

    def added(first, second, dropped=None):
        value = sum(first(2 - k).astype(F32) for k in range(3))
        value = value + sum(second(last + 4 - k).astype(F32) for k in range(3))
        if dropped is not None:
            value = jnp.where(dropped, 0.0, value)
        return value.astype(BF)

    spare = far_a.shape[0] - 3
    far_first = coarse.shape[0] - far_a.shape[0]
    rows = [far_left(k) for k in range(spare)]
    rows += [added(left_row, lambda k: far_left(k - far_first))]
    rows += [left_row(k) for k in range(3, last + 2)]
    rows += [added(lambda k: coarse[k], left_row)]
    rows += [coarse[k] for k in range(3, last + 2)]
    rows += [added(right_row, lambda k: coarse[k], ended_x)]
    rows += [right_row(k) for k in range(3, last + 2)]
    rows += [added(far_right, right_row, close_x)]
    rows += [far_right(k) for k in range(3, 3 + spare)]
    for k, row in enumerate(rows):
        mid[k] = row

    skip = (mid.shape[0] - m_real.shape[0]) // 2
    m_width = m_real.shape[1]
    cut = half - m_width // 2

    def mid_z(xs, first):
        cells = jnp.concatenate([mid[x + skip] for x in xs], 0)
        cells = jnp.concatenate([cells, cells], 1)
        low, high = dot(cells, m_low[...]), dot(cells, m_high[...])
        parts = []
        for k in range(len(xs)):
            parts += [low[k * half + cut : (k + 1) * half], high[k * half : (k + 1) * half - cut]]
        high, low = split(jnp.concatenate(parts, 0), 2)
        m_ahead[0, rows_at(first, m_width, len(xs)), :] = high
        m_ahead[1, rows_at(first, m_width, len(xs)), :] = low

    batches(m_real.shape[0], 9, mid_z)
    to_frequencies_y(m_ahead, 9, m_to_y, m_real, m_imag)

    t_width = t_real.shape[1]
    inside = lax.broadcasted_iota(jnp.int32, (t_width, t_cells.shape[2]), 0)
    inside = inside < jnp.where(ended_y == 1, t_width - (t_width - last_columns(t_width, m_width)) // 2, t_width)

    def top_cells(xs, first):
        spreads = []
        for t in xs:
            total = 0.5 * mid[2 * t].astype(F32) + mid[2 * t + 1].astype(F32) + 0.5 * mid[2 * t + 2].astype(F32)
            spreads.append(dot(t_down_y[...], all_terms(total)))
        low = jnp.concatenate([spread[:t_width] for spread in spreads], 0)
        high = jnp.concatenate([spread[t_width:] for spread in spreads], 0)
        value = dot(jnp.concatenate(split(low, 3) + split(high, 3), 1), t_down_z[...])
        for k, t in enumerate(xs):
            row = jnp.where(inside, value[k * t_width : (k + 1) * t_width], 0.0)
            t_cells[t] = jnp.where(t < top_rows, row, 0.0).astype(BF)

    batches(t_real.shape[0], 7, top_cells)
    to_frequencies_z(lambda x: t_cells[x], t_real.shape[0], 7, t_to_z, t_ahead)
    to_frequencies_y(t_ahead, 7, t_to_y, t_real, t_imag)

    def plain(ref):
        return lambda x, rows: ref[x, rows, :]

    along_x(plain(m_real), plain(m_imag), (mr, md, ms), m_er, m_ei, 7)
    along_x(plain(t_real), plain(t_imag), (tr, td, ts), t_er, t_ei, 7)

    def top_write(x, value):
        t_out[x] = value

    def mid_write(x, value):
        m_out[x] = value

    from_frequencies_y(t_er, t_ei, 7, t_from_y.at[ended_y], t_back)
    from_frequencies_y(m_er, m_ei, 7, m_from_y.at[ended_y], m_back)
    from_frequencies_z(t_back, t_out.shape[0], 7, t_from_z, top_write)
    from_frequencies_z(m_back, m_out.shape[0], 7, m_from_z, mid_write)
    keep = jnp.where(ended_x, 0.0, 1.0)
    top = t_out.shape[0] - 1
    t_out[top] = t_out[top] * keep
    for i in range(top):
        m_out[2 * i] += t_out[i]
        m_out[2 * i + 1] += 0.5 * (t_out[i] + t_out[i + 1])
    m_out[2 * top] = (m_out[2 * top] + t_out[top]) * keep

    def finish(i):
        out[2 * i] += m_out[i]
        out[2 * i + 1] += 0.5 * (m_out[i] + m_out[i + 1])

    rows_loop(count // 2, 2, finish)


def last_columns(t_width, m_width):
    return m_width - t_width


def call(kernel, outs, scratch, args, mib, loose=()):
    vmem = pl.BlockSpec(memory_space=pltpu.VMEM)
    return pl.pallas_call(
        kernel,
        out_shape=outs,
        in_specs=[
            pl.BlockSpec(memory_space=pl.ANY) if i in loose else vmem for i in range(len(args))
        ],
        out_specs=jax.tree.map(lambda _: vmem, outs),
        scratch_shapes=[pltpu.VMEM(shape, dtype) for dtype, shape in scratch],
        compiler_params=pltpu.CompilerParams(vmem_limit_bytes=mib << 20),
    )(*args)


def level_scratch(level, ny, nz, extra=()):
    rows = [
        (F32, (count, level.period_y, LANES))
        for count in (level.in_x, level.in_x, level.out_x, level.out_x)
    ]
    terms = [
        (BF, (2, level.in_x * level.period_y, 2 * LANES)),
        (BF, (2, level.out_x * ny, 2 * LANES)),
    ]
    return [*rows, *extra, *terms, (F32, (level.out_x, ny, nz))]


def leads(axis, by):
    return lax.rem(lax.div(lax.axis_index(axis), by), 2) == 0


def swapped(first, second, axis, by):
    length = lax.axis_size(axis)
    outs = []
    for value, turn in ((first, 0), (second, 1)):
        up = [i for i in range(length - by) if i // by % 2 == turn]
        pairs = [(i, i + by) for i in up] + [(i + by, i) for i in up]
        outs.append(lax.ppermute(value, axis, pairs))
    return outs


def shards(charges, kernel_fine, kernel_mid, kernel_top):
    nx, ny, nz = charges.shape
    taps = kernel_fine.shape[0]
    half = taps // 2
    wide = half + 1

    ident = np.eye(ny)
    fine = Level(taps, nx, ny, wide, ny + 2 * wide, nz, ident, ident, np.eye(nz))
    my, mz = ny // 2, nz // 2
    to_fine = up(my)
    ended = np.diag([1.0] * my + [0.0])
    mid = Level(
        taps, nx // 2 + 1, my + 1, wide, my + 2 * wide, mz, to_fine, to_fine @ ended, up_closed(mz)
    )
    ty, tz = my // 2, mz // 2
    to_mid = np.concatenate([up(ty), np.eye(ty + 1)[-1:]], 0)
    top_ended = np.diag([1.0] * ty + [0.0])
    top = Level(
        taps,
        nx // 4 + 1,
        ty + 1,
        wide,
        ty + 2 * wide,
        tz,
        to_fine @ to_mid,
        to_fine @ to_mid @ top_ended,
        up_closed(mz) @ up_closed(tz),
    )

    levels = (fine, mid, top)
    outs = [
        jax.ShapeDtypeStruct((taps, level.period_y, LANES), F32)
        for level in levels
        for _ in range(3)
    ]
    tables = [table for level in levels for table in (level.kernel_z, level.kernel_y)]
    spectra = call(
        functools.partial(spectra_kernel, 3),
        outs,
        [(F32, (taps, 16, LANES)), (F32, (taps * 16, 2 * LANES))],
        [kernel_fine, kernel_mid, kernel_top, *tables],
        8,
    )

    side = ny // 2
    up_y = leads("gy", 1)
    got_a, got_b = swapped(
        *(
            lax.dynamic_slice_in_dim(charges, jnp.where(flag, side, 0), side, 1).astype(BF)
            for flag in (up_y, jnp.logical_not(up_y))
        ),
        "gy",
        1,
    )

    window = side + ny // 2 + 16
    packed = ny // 2
    down_z = np.concatenate([np.pad(down(mz, 0, nz).T, ((0, 0), (at, mz - at))) for at in (0, mz)], 0)
    shift = ny + 2 * side - window
    down_y = np.concatenate([down(packed, 0, window), down(packed, 2 * packed - shift, window)], 0)
    mx = nx // 2
    lines = mx - 1 + 6
    reach = 2 * half + 1 - mx
    assert 0 < reach <= mx - 1 and 2 * mz == LANES == nz
    shapes = [
        (nx, fine.period_y, LANES),
        (lines, packed, LANES),
        (half * fine.period_y + lines * packed, LANES),
        (half * fine.period_y + lines * packed, LANES),
        (reach + 3, packed, LANES),
        (reach + 3, packed, LANES),
    ]
    near, coarse, next_a, next_b, far_a, far_b = call(
        pack_kernel,
        [jax.ShapeDtypeStruct(shape, BF) for shape in shapes],
        [(F32, (nx, window, LANES))],
        [
            charges,
            got_a,
            got_b,
            down_z.astype(BF),
            np.tile(down_y, (1, 3)).astype(BF),
            spectra[0],
        ],
        8,
        loose=(5,),
    )
    next_a, next_b = swapped(next_a, next_b, "gx", 1)
    far_a, far_b = swapped(far_a, far_b, "gx", 2)

    own = call(
        own_kernel,
        [jax.ShapeDtypeStruct((nx, fine.period_y, LANES), F32)] * 2,
        [(BF, (2, nx * fine.period_y, 2 * LANES))],
        [near, fine.to_z, fine.to_y],
        8,
    )

    wide_top = ty + 2 * wide
    t_down_y = down(wide_top, 0, 2 * packed)
    t_down_y = np.concatenate([t_down_y[:, :packed], t_down_y[:, packed:]], 0)
    t_down_z = np.concatenate(
        [np.tile(table, (3, 1)) for table in both_sides(down(tz, 0, mz).T)], 0
    )
    return call(
        final_kernel,
        jax.ShapeDtypeStruct((nx, ny, nz), F32),
        [
            (F32, (2 * half, fine.period_y, LANES)),
            (F32, (2 * half, fine.period_y, LANES)),
            (F32, (nx, fine.period_y, LANES)),
            (F32, (nx, fine.period_y, LANES)),
            (BF, (2, 2 * half * fine.period_y, 2 * LANES)),
            (BF, (2, nx * ny, 2 * LANES)),
            (BF, (3 * mx + 1 + 2 * reach, packed, LANES)),
            *level_scratch(mid, ny, nz),
            *level_scratch(top, ny, nz, [(BF, (top.in_x, top.period_y, tz))]),
        ],
        [
            *own,
            next_a,
            next_b,
            far_a,
            far_b,
            coarse,
            *spectra[:3],
            fine.to_z,
            fine.to_y,
            fine.from_y[0],
            fine.from_z,
            *spectra[3:6],
            *mid.to_z_packed,
            mid.to_y,
            np.stack(mid.from_y),
            mid.from_z,
            *spectra[6:],
            np.tile(t_down_y, (1, 3)).astype(BF),
            t_down_z.astype(BF),
            top.to_z,
            top.to_y,
            np.stack(top.from_y),
            top.from_z,
        ],
        26,
    )


def solution(mesh):
    placed = (P("gx", "gy", None), P(), P(), P())
    return jax.shard_map(
        shards, mesh=mesh, in_specs=placed, out_specs=P("gx", "gy", None), check_vma=False
    )
```

```python
import functools

import jax
import jax.numpy as jnp
import numpy as np
from jax import lax
from jax.experimental import pallas as pl
from jax.experimental.pallas import tpu as pltpu
from jax.sharding import PartitionSpec as P

BF = jnp.bfloat16
F32 = jnp.float32
LANES = 128


def two(matrix):
    high = np.asarray(matrix, np.float64).astype(BF)
    low = (matrix - high.astype(np.float64)).astype(BF)
    return high, low


def beside(real, imag):
    out = np.zeros((real.shape[0], 2 * LANES))
    out[:, : real.shape[1]] = real
    out[:, LANES : LANES + imag.shape[1]] = imag
    return out


def three_terms(matrix):
    high, low = two(matrix)
    return np.concatenate([high, high, low], 1)


def up(count):
    out = np.zeros((2 * count, count + 1))
    for i in range(count):
        out[2 * i, i] = 1.0
        out[2 * i + 1, i] = out[2 * i + 1, i + 1] = 0.5
    return out


def up_closed(count):
    return up(count)[:, :count]


def both_sides(table):
    size = table.shape[0]
    return [np.pad(table, ((at, LANES - size - at), (0, 0))) for at in (0, LANES - size)]


class Level:
    def __init__(self, taps, out_x, out_y, shift, period_y, size_z, rows_y, rows_y_end, cols_z):
        half = taps // 2
        self.taps, self.out_x, self.in_x = taps, out_x, out_x + taps - 1
        self.period_y, self.size_z = period_y, size_z
        period_z = size_z + half + (size_z + half) % 2
        assert period_y >= shift + out_y + half and shift >= half and period_y % 16 == 0
        freq_z = np.arange(period_z // 2 + 1)
        assert len(freq_z) <= LANES
        freq_y = np.arange(period_y)
        turn_z, turn_y = 2 * np.pi / period_z, 2 * np.pi / period_y
        angle = turn_z * np.outer(np.arange(size_z), freq_z)
        table = beside(np.cos(angle), -np.sin(angle))
        self.to_z = np.concatenate(two(table), 0)
        self.to_z_packed = [np.concatenate(two(side), 0) for side in both_sides(table)]
        angle = turn_y * np.outer(freq_y, np.arange(period_y))
        self.to_y = three_terms(np.concatenate([np.cos(angle), np.sin(angle)], 0))
        offsets = np.arange(taps) - half
        angle = turn_z * np.outer(offsets, freq_z)
        table = np.zeros((LANES, 2 * LANES))
        table[:taps] = beside(np.cos(angle), np.sin(angle))
        self.kernel_z = np.concatenate(two(table), 0)
        angle = turn_y * np.outer(freq_y, np.pad(offsets, (0, 1)))
        self.kernel_y = three_terms(np.concatenate([np.cos(angle), np.sin(angle)], 0))
        angle = turn_y * np.outer(np.arange(out_y) + shift, freq_y)
        self.from_y = [
            three_terms(
                np.concatenate([rows @ np.cos(angle), rows @ np.sin(angle)], 0) / period_y
            )
            for rows in (rows_y, rows_y_end)
        ]
        weight = np.where((freq_z == 0) | (2 * freq_z == period_z), 1.0, 2.0)[:, None] / period_z
        angle = turn_z * np.outer(freq_z, np.arange(size_z))
        table = np.zeros((2 * LANES, cols_z.shape[0]))
        table[: len(freq_z)] = (weight * np.cos(angle)) @ cols_z.T
        table[LANES : LANES + len(freq_z)] = (-weight * np.sin(angle)) @ cols_z.T
        high, low = two(table)
        self.from_z = np.concatenate([high, high, low], 0)


def down(count, first, length):
    out = np.zeros((count, length))
    for j in range(count):
        for a, w in ((-1, 0.5), (0, 1.0), (1, 0.5)):
            if 0 <= first + 2 * j + a < length:
                out[j, first + 2 * j + a] = w
    return out


def dot(a, b):
    return jnp.dot(a, b, preferred_element_type=F32)


def split(value, terms):
    out = []
    for _ in range(terms - 1):
        out.append(value.astype(BF))
        value = value - out[-1].astype(F32)
    return out + [value.astype(BF)]


def stacked(value):
    high, low = split(value, 2)
    return jnp.concatenate([high, low, high], 0)


def batches(count, size, body):
    def trip(i, _):
        first = i * size
        body([first + k for k in range(size)], first)
        return 0

    whole = count // size
    if whole > 1:
        lax.fori_loop(0, whole, trip, 0)
    else:
        whole = 0
    for first in range(whole * size, count, size):
        body(list(range(first, min(count, first + size))), first)


def rows_at(first, period, count):
    return pl.ds(first * period if isinstance(first, int) else pl.multiple_of(first * period, 16), count * period)


def to_frequencies_z(read, count, size, table, terms):
    period = terms.shape[1] // count

    def body(xs, first):
        cells = jnp.concatenate([read(x) for x in xs], 0)
        size_z = cells.shape[1]
        if size_z % LANES == 0:
            value = dot(jnp.concatenate([cells, cells], 1), table[...])
        else:
            value = dot(cells, table[:size_z]) + dot(cells, table[size_z:])
        high, low = split(value, 2)
        terms[0, rows_at(first, period, len(xs)), :] = high
        terms[1, rows_at(first, period, len(xs)), :] = low

    batches(count, size, body)


def to_frequencies_y(terms, size, to_y, real, imag):
    count, period = real.shape[:2]

    def body(xs, first):
        spreads = []
        for x in xs:
            rows = rows_at(x, period, 1)
            high, low = terms[0, rows, :], terms[1, rows, :]
            spreads.append(dot(to_y[...], jnp.concatenate([high, low, high], 0)))
        for x, spread in zip(xs, spreads):
            real[x] = spread[:period, :LANES] + spread[period:, LANES:]
            imag[x] = spread[:period, LANES:] - spread[period:, :LANES]

    batches(count, size, body)


def from_frequencies_y(real, imag, size, from_y, terms):
    count = real.shape[0]
    rows = from_y.shape[0] // 2

    def body(xs, first):
        spreads = [
            dot(from_y[...], stacked(jnp.concatenate([real[x], imag[x]], 1))) for x in xs
        ]
        for x, spread in zip(xs, spreads):
            r = spread[:rows, :LANES] - spread[rows:, LANES:]
            i = spread[rows:, :LANES] + spread[:rows, LANES:]
            high, low = split(jnp.concatenate([r, i], 1), 2)
            terms[0, rows_at(x, rows, 1), :] = high
            terms[1, rows_at(x, rows, 1), :] = low

    batches(count, size, body)


def from_frequencies_z(terms, count, size, from_z, write):
    rows = terms.shape[1] // count

    def body(xs, first):
        span = rows_at(first, rows, len(xs))
        high, low = terms[0, span, :], terms[1, span, :]
        value = dot(jnp.concatenate([high, low, high], 1), from_z[...])
        for k, x in enumerate(xs):
            write(x, value[k * rows : (k + 1) * rows])

    batches(count, size, body)


def along_x(real, imag, spectrum, out_real, out_imag, block, taken=None, before=None):
    kernel_r, kernel_d, kernel_s = spectrum
    taps, period = kernel_r.shape[:2]
    out_x = out_real.shape[0]
    taken = taken or (lambda x: True)

    def body(part, _):
        rows = pl.ds(pl.multiple_of(8 * part, 8), 8)
        for start in range(0, out_x, block):
            count = min(block, out_x - start)
            sums = [[None] * 3 for _ in range(count)]
            seen = {}
            for a in range(taps):
                used = [i for i in range(count) if taken(start + i + a)]
                if used:
                    weights = kernel_r[a, rows, :], kernel_d[a, rows, :], kernel_s[a, rows, :]
                for i in used:
                    x = start + i + a
                    if x not in seen:
                        r, m = real(x, rows), imag(x, rows)
                        seen[x] = r + m, r, m
                    for k in range(3):
                        term = weights[k] * seen[x][k]
                        sums[i][k] = term if sums[i][k] is None else sums[i][k] + term
            for i in range(count):
                values = []
                if sums[i][0] is not None:
                    values.append((sums[i][0] - sums[i][2], sums[i][0] + sums[i][1]))
                if before is not None:
                    values.append((before[0][start + i, rows, :], before[1][start + i, rows, :]))
                out_real[start + i, rows, :] = sum(value[0] for value in values)
                out_imag[start + i, rows, :] = sum(value[1] for value in values)
        return 0

    lax.fori_loop(0, period // 8, body, 0)


def rows_loop(count, step, body):
    def trip(i, _):
        for k in range(step):
            body(i * step + k)
        return 0

    lax.fori_loop(0, count // step, trip, 0)
    for x in range(count - count % step, count):
        body(x)


def all_terms(value):
    return jnp.concatenate(split(value, 3), 0)


def spectra_kernel(levels, *refs):
    kernels, refs = refs[:levels], refs[levels:]
    table, outs, (padded, mid) = refs[0], refs[1:-2], refs[-2:]
    at = 0
    taps = kernels[0].shape[0]
    padded[...] = jnp.zeros(padded.shape, padded.dtype)
    for level in range(levels):
        outs_here = outs[3 * level : 3 * level + 3]
        period = outs_here[0].shape[1]
        kernel_z = table[at : at + 2 * LANES, :]
        kernel_y = table[at + 2 * LANES : at + 2 * LANES + 2 * period, : 3 * padded.shape[1]]
        at += 2 * LANES + 2 * period
        padded[:, :taps, :taps] = kernels[level][...].astype(F32)
        cells = padded[...].astype(BF).reshape(taps * padded.shape[1], LANES)
        mid[...] = dot(jnp.concatenate([cells, cells], 1), kernel_z)

        def body(xs, first, kernel_y=kernel_y, outs=outs_here, period=period):
            spreads = [dot(kernel_y, stacked(mid[rows_at(a, 16, 1), :])) for a in xs]
            for a, spread in zip(xs, spreads):
                real = spread[:period, :LANES] - spread[period:, LANES:]
                imag = spread[:period, LANES:] + spread[period:, :LANES]
                outs[0][a] = real
                outs[1][a] = imag - real
                outs[2][a] = imag + real

        batches(taps, 5, body)


def chosen(flag, first, second):
    return jnp.where(flag, first, second)


def pack_kernel(
    own, got_a, got_b, down_z, down_y, ordered, near, coarse, next_a, next_b, far_a, far_b, part
):
    count, size = own.shape[:2]
    side = got_a.shape[1]
    up_y, up_x, up_far = leads("gy", 1), leads("gx", 1), leads("gx", 2)
    ended = lax.axis_index("gy") == lax.axis_size("gy") - 1
    width = near.shape[1]
    start = side - (width - size) // 2
    window = part.shape[1]

    def body(xs, first):
        rows = []
        for x in xs:
            a, b, o = got_a[x], got_b[x], own[x].astype(BF)
            l, r = chosen(up_y, b, a), chosen(up_y, a, b)
            near[x] = jnp.concatenate([l[start:], o, r[: side - start]], 0)
            low = jnp.concatenate([l, o[: window - side]], 0)
            high = jnp.concatenate([o[size + side - window :], r], 0)
            rows.append(jnp.concatenate([low, high], 1))
        value = dot(jnp.concatenate(rows, 0), down_z[...])
        for k, x in enumerate(xs):
            part[x] = value[k * window : (k + 1) * window]

    batches(count, 4, body)
    half = down_y.shape[0] // 2
    shape = (half, LANES)
    high_lanes = lax.broadcasted_iota(jnp.int32, shape, 1) >= LANES // 2
    outside = high_lanes & (lax.broadcasted_iota(jnp.int32, shape, 0) >= half // 2)
    outside = outside & ended
    last = count // 2
    totals = []
    for i in range(last + 1):
        if i == 0:
            total = part[0] + 0.5 * part[1]
        elif i == last:
            total = 0.5 * part[count - 1]
        else:
            total = 0.5 * part[2 * i - 1] + part[2 * i] + 0.5 * part[2 * i + 1]
        totals.append(dot(down_y[...], all_terms(total)))
    for i, total in enumerate(totals):
        row = jnp.where(high_lanes, total[half:], total[:half])
        row = jnp.where(outside, 0.0, row)
        if i == 0:
            for k, term in enumerate(split(row, 3)):
                coarse[k] = term
        elif i == last:
            for k, term in enumerate(split(row, 3)):
                coarse[last + 2 + k] = term
        else:
            coarse[i + 2] = row.astype(BF)
    lines = next_a.shape[0] - coarse.shape[0] * half
    tail = count - lines // width
    far_tail = coarse.shape[0] - far_a.shape[0]
    for out, upward in ((next_a, up_x), (next_b, jnp.logical_not(up_x))):
        first = jnp.where(upward, tail, 0)
        for x in range(lines // width):
            out[x * width : (x + 1) * width, :] = near[first + x]
        for k in range(coarse.shape[0]):
            out[lines + k * half : lines + (k + 1) * half, :] = coarse[k]
    for out, upward in ((far_a, up_far), (far_b, jnp.logical_not(up_far))):
        first = jnp.where(upward, far_tail, 0)
        for k in range(far_a.shape[0]):
            out[k] = coarse[first + k]


def own_kernel(near, kr, kd, ks, to_z, to_y, out_real, out_imag, real, imag, ahead):
    count = real.shape[0]
    half = kr.shape[0] // 2
    to_frequencies_z(lambda x: near[x], count, 4, to_z, ahead)
    to_frequencies_y(ahead, 4, to_y, real, imag)
    along_x(
        lambda x, rows: real[x - half, rows, :],
        lambda x, rows: imag[x - half, rows, :],
        (kr, kd, ks),
        out_real,
        out_imag,
        8,
        lambda x: half <= x < half + count,
    )


def final_kernel(
    part_real,
    part_imag,
    next_a,
    next_b,
    far_a,
    far_b,
    coarse,
    kr,
    kd,
    ks,
    to_z,
    to_y,
    from_y,
    from_z,
    mr,
    md,
    ms,
    m_low,
    m_high,
    m_to_y,
    m_from_y,
    m_from_z,
    tr,
    td,
    ts,
    t_down_y,
    t_down_z,
    t_to_z,
    t_to_y,
    t_from_y,
    t_from_z,
    out,
    side_real,
    side_imag,
    er,
    ei,
    ahead,
    back,
    mid,
    m_real,
    m_imag,
    m_er,
    m_ei,
    m_ahead,
    m_back,
    m_out,
    t_real,
    t_imag,
    t_er,
    t_ei,
    t_cells,
    t_ahead,
    t_back,
    t_out,
):
    left_x = lax.axis_size("gx") - lax.axis_index("gx")
    ended_x, close_x = left_x == 1, left_x <= 2
    ended_y = (lax.axis_index("gy") == lax.axis_size("gy") - 1).astype(jnp.int32)
    up_x, up_far = leads("gx", 1), leads("gx", 2)
    count, width = part_real.shape[:2]
    reach = side_real.shape[0] // 2
    top_rows = left_x * (count // 4) + reach

    def from_left(at):
        return chosen(up_x, next_b[at, :], next_a[at, :])

    def from_right(at):
        return chosen(up_x, next_a[at, :], next_b[at, :])

    def far_left(k):
        return chosen(up_far, far_b[k], far_a[k])

    def far_right(k):
        return chosen(up_far, far_a[k], far_b[k])

    def side_cells(x):
        read, first = (from_left, x) if x < reach else (from_right, x - reach)
        return read(slice(first * width, (first + 1) * width))

    period = width
    for first in range(0, 2 * reach, 4):
        xs = list(range(first, min(2 * reach, first + 4)))
        cells = jnp.concatenate([side_cells(x) for x in xs], 0)
        value = dot(jnp.concatenate([cells, cells], 1), to_z[...])
        high, low = split(value, 2)
        ahead[0, rows_at(first, period, len(xs)), :] = high
        ahead[1, rows_at(first, period, len(xs)), :] = low
    to_frequencies_y(ahead, 7, to_y, side_real, side_imag)

    def source(side):
        return lambda x, rows: side[x if x < reach else x - count, rows, :]

    along_x(
        source(side_real),
        source(side_imag),
        (kr, kd, ks),
        er,
        ei,
        8,
        lambda x: x < reach or x >= reach + count,
        (part_real, part_imag),
    )
    from_frequencies_y(er, ei, 4, from_y, back)

    def fine_write(x, value):
        out[x] = value

    from_frequencies_z(back, count, 4, from_z, fine_write)

    half = mid.shape[1]
    last = count // 2
    lines = next_a.shape[0] - coarse.shape[0] * half

    def left_row(k):
        return from_left(slice(lines + k * half, lines + (k + 1) * half))

    def right_row(k):
        return from_right(slice(lines + k * half, lines + (k + 1) * half))

    def added(first, second, dropped=None):
        value = sum(first(2 - k).astype(F32) for k in range(3))
        value = value + sum(second(last + 4 - k).astype(F32) for k in range(3))
        if dropped is not None:
            value = jnp.where(dropped, 0.0, value)
        return value.astype(BF)

    spare = far_a.shape[0] - 3
    far_first = coarse.shape[0] - far_a.shape[0]
    rows = [far_left(k) for k in range(spare)]
    rows += [added(left_row, lambda k: far_left(k - far_first))]
    rows += [left_row(k) for k in range(3, last + 2)]
    rows += [added(lambda k: coarse[k], left_row)]
    rows += [coarse[k] for k in range(3, last + 2)]
    rows += [added(right_row, lambda k: coarse[k], ended_x)]
    rows += [right_row(k) for k in range(3, last + 2)]
    rows += [added(far_right, right_row, close_x)]
    rows += [far_right(k) for k in range(3, 3 + spare)]
    for k, row in enumerate(rows):
        mid[k] = row

    skip = (mid.shape[0] - m_real.shape[0]) // 2
    m_width = m_real.shape[1]
    cut = half - m_width // 2

    def mid_z(xs, first):
        cells = jnp.concatenate([mid[x + skip] for x in xs], 0)
        cells = jnp.concatenate([cells, cells], 1)
        low, high = dot(cells, m_low[...]), dot(cells, m_high[...])
        parts = []
        for k in range(len(xs)):
            parts += [low[k * half + cut : (k + 1) * half], high[k * half : (k + 1) * half - cut]]
        high, low = split(jnp.concatenate(parts, 0), 2)
        m_ahead[0, rows_at(first, m_width, len(xs)), :] = high
        m_ahead[1, rows_at(first, m_width, len(xs)), :] = low

    batches(m_real.shape[0], 9, mid_z)
    to_frequencies_y(m_ahead, 9, m_to_y, m_real, m_imag)

    t_width = t_real.shape[1]
    inside = lax.broadcasted_iota(jnp.int32, (t_width, t_cells.shape[2]), 0)
    inside = inside < jnp.where(ended_y == 1, t_width - (t_width - last_columns(t_width, m_width)) // 2, t_width)

    def top_cells(xs, first):
        spreads = []
        for t in xs:
            total = 0.5 * mid[2 * t].astype(F32) + mid[2 * t + 1].astype(F32) + 0.5 * mid[2 * t + 2].astype(F32)
            spreads.append(dot(t_down_y[...], all_terms(total)))
        low = jnp.concatenate([spread[:t_width] for spread in spreads], 0)
        high = jnp.concatenate([spread[t_width:] for spread in spreads], 0)
        value = dot(jnp.concatenate(split(low, 3) + split(high, 3), 1), t_down_z[...])
        for k, t in enumerate(xs):
            row = jnp.where(inside, value[k * t_width : (k + 1) * t_width], 0.0)
            t_cells[t] = jnp.where(t < top_rows, row, 0.0).astype(BF)

    batches(t_real.shape[0], 7, top_cells)
    to_frequencies_z(lambda x: t_cells[x], t_real.shape[0], 7, t_to_z, t_ahead)
    to_frequencies_y(t_ahead, 7, t_to_y, t_real, t_imag)

    def plain(ref):
        return lambda x, rows: ref[x, rows, :]

    along_x(plain(m_real), plain(m_imag), (mr, md, ms), m_er, m_ei, 7)
    along_x(plain(t_real), plain(t_imag), (tr, td, ts), t_er, t_ei, 7)

    def top_write(x, value):
        t_out[x] = value

    def mid_write(x, value):
        m_out[x] = value

    from_frequencies_y(t_er, t_ei, 7, t_from_y.at[ended_y], t_back)
    from_frequencies_y(m_er, m_ei, 7, m_from_y.at[ended_y], m_back)
    from_frequencies_z(t_back, t_out.shape[0], 7, t_from_z, top_write)
    from_frequencies_z(m_back, m_out.shape[0], 7, m_from_z, mid_write)
    keep = jnp.where(ended_x, 0.0, 1.0)
    top = t_out.shape[0] - 1
    t_out[top] = t_out[top] * keep
    for i in range(top):
        m_out[2 * i] += t_out[i]
        m_out[2 * i + 1] += 0.5 * (t_out[i] + t_out[i + 1])
    m_out[2 * top] = (m_out[2 * top] + t_out[top]) * keep

    def finish(i):
        out[2 * i] += m_out[i]
        out[2 * i + 1] += 0.5 * (m_out[i] + m_out[i + 1])

    rows_loop(count // 2, 2, finish)


def last_columns(t_width, m_width):
    return m_width - t_width


def call(kernel, outs, scratch, args, mib, loose=()):
    vmem = pl.BlockSpec(memory_space=pltpu.VMEM)
    return pl.pallas_call(
        kernel,
        out_shape=outs,
        in_specs=[
            pl.BlockSpec(memory_space=pl.ANY) if i in loose else vmem for i in range(len(args))
        ],
        out_specs=jax.tree.map(lambda _: vmem, outs),
        scratch_shapes=[pltpu.VMEM(shape, dtype) for dtype, shape in scratch],
        compiler_params=pltpu.CompilerParams(vmem_limit_bytes=mib << 20),
    )(*args)


def level_scratch(level, ny, nz, extra=()):
    rows = [
        (F32, (count, level.period_y, LANES))
        for count in (level.in_x, level.in_x, level.out_x, level.out_x)
    ]
    terms = [
        (BF, (2, level.in_x * level.period_y, 2 * LANES)),
        (BF, (2, level.out_x * ny, 2 * LANES)),
    ]
    return [*rows, *extra, *terms, (F32, (level.out_x, ny, nz))]


def leads(axis, by):
    return lax.rem(lax.div(lax.axis_index(axis), by), 2) == 0


def swapped(first, second, axis, by):
    length = lax.axis_size(axis)
    outs = []
    for value, turn in ((first, 0), (second, 1)):
        up = [i for i in range(length - by) if i // by % 2 == turn]
        pairs = [(i, i + by) for i in up] + [(i + by, i) for i in up]
        outs.append(lax.ppermute(value, axis, pairs))
    return outs


def shards(charges, kernel_fine, kernel_mid, kernel_top):
    nx, ny, nz = charges.shape
    taps = kernel_fine.shape[0]
    half = taps // 2
    wide = half + 1

    ident = np.eye(ny)
    fine = Level(taps, nx, ny, wide, ny + 2 * wide, nz, ident, ident, np.eye(nz))
    my, mz = ny // 2, nz // 2
    to_fine = up(my)
    ended = np.diag([1.0] * my + [0.0])
    mid = Level(
        taps, nx // 2 + 1, my + 1, wide, my + 2 * wide, mz, to_fine, to_fine @ ended, up_closed(mz)
    )
    ty, tz = my // 2, mz // 2
    to_mid = np.concatenate([up(ty), np.eye(ty + 1)[-1:]], 0)
    top_ended = np.diag([1.0] * ty + [0.0])
    top = Level(
        taps,
        nx // 4 + 1,
        ty + 1,
        wide,
        ty + 2 * wide,
        tz,
        to_fine @ to_mid,
        to_fine @ to_mid @ top_ended,
        up_closed(mz) @ up_closed(tz),
    )

    levels = (fine, mid, top)
    outs = [
        jax.ShapeDtypeStruct((taps, level.period_y, LANES), F32)
        for level in levels
        for _ in range(3)
    ]
    tables = []
    for level in levels:
        tables.append(level.kernel_z)
        tables.append(np.pad(level.kernel_y, ((0, 0), (0, 2 * LANES - level.kernel_y.shape[1]))))
    spectra = call(
        functools.partial(spectra_kernel, 3),
        outs,
        [(F32, (taps, 16, LANES)), (F32, (taps * 16, 2 * LANES))],
        [kernel_fine, kernel_mid, kernel_top, np.concatenate(tables, 0)],
        8,
    )

    side = ny // 2
    up_y = leads("gy", 1)
    got_a, got_b = swapped(
        *(
            lax.dynamic_slice_in_dim(charges, jnp.where(flag, side, 0), side, 1).astype(BF)
            for flag in (up_y, jnp.logical_not(up_y))
        ),
        "gy",
        1,
    )

    window = side + ny // 2 + 16
    packed = ny // 2
    down_z = np.concatenate([np.pad(down(mz, 0, nz).T, ((0, 0), (at, mz - at))) for at in (0, mz)], 0)
    shift = ny + 2 * side - window
    down_y = np.concatenate([down(packed, 0, window), down(packed, 2 * packed - shift, window)], 0)
    mx = nx // 2
    lines = mx - 1 + 6
    reach = 2 * half + 1 - mx
    assert 0 < reach <= mx - 1 and 2 * mz == LANES == nz
    shapes = [
        (nx, fine.period_y, LANES),
        (lines, packed, LANES),
        (half * fine.period_y + lines * packed, LANES),
        (half * fine.period_y + lines * packed, LANES),
        (reach + 3, packed, LANES),
        (reach + 3, packed, LANES),
    ]
    near, coarse, next_a, next_b, far_a, far_b = call(
        pack_kernel,
        [jax.ShapeDtypeStruct(shape, BF) for shape in shapes],
        [(F32, (nx, window, LANES))],
        [
            charges,
            got_a,
            got_b,
            down_z.astype(BF),
            np.tile(down_y, (1, 3)).astype(BF),
            spectra[0],
        ],
        8,
        loose=(5,),
    )
    next_a, next_b = swapped(next_a, next_b, "gx", 1)
    far_a, far_b = swapped(far_a, far_b, "gx", 2)

    own = call(
        own_kernel,
        [jax.ShapeDtypeStruct((nx, fine.period_y, LANES), F32)] * 2,
        [(F32, (nx, fine.period_y, LANES))] * 2 + [(BF, (2, nx * fine.period_y, 2 * LANES))],
        [near, *spectra[:3], fine.to_z, fine.to_y],
        12,
    )

    wide_top = ty + 2 * wide
    t_down_y = down(wide_top, 0, 2 * packed)
    t_down_y = np.concatenate([t_down_y[:, :packed], t_down_y[:, packed:]], 0)
    t_down_z = np.concatenate(
        [np.tile(table, (3, 1)) for table in both_sides(down(tz, 0, mz).T)], 0
    )
    return call(
        final_kernel,
        jax.ShapeDtypeStruct((nx, ny, nz), F32),
        [
            (F32, (2 * half, fine.period_y, LANES)),
            (F32, (2 * half, fine.period_y, LANES)),
            (F32, (nx, fine.period_y, LANES)),
            (F32, (nx, fine.period_y, LANES)),
            (BF, (2, 2 * half * fine.period_y, 2 * LANES)),
            (BF, (2, nx * ny, 2 * LANES)),
            (BF, (3 * mx + 1 + 2 * reach, packed, LANES)),
            *level_scratch(mid, ny, nz),
            *level_scratch(top, ny, nz, [(BF, (top.in_x, top.period_y, tz))]),
        ],
        [
            *own,
            next_a,
            next_b,
            far_a,
            far_b,
            coarse,
            *spectra[:3],
            fine.to_z,
            fine.to_y,
            fine.from_y[0],
            fine.from_z,
            *spectra[3:6],
            *mid.to_z_packed,
            mid.to_y,
            np.stack(mid.from_y),
            mid.from_z,
            *spectra[6:],
            np.tile(t_down_y, (1, 3)).astype(BF),
            t_down_z.astype(BF),
            top.to_z,
            top.to_y,
            np.stack(top.from_y),
            top.from_z,
        ],
        26,
    )


def solution(mesh):
    placed = (P("gx", "gy", None), P(), P(), P())
    return jax.shard_map(
        shards, mesh=mesh, in_specs=placed, out_specs=P("gx", "gy", None), check_vma=False
    )
```

```python
import functools

import jax
import jax.numpy as jnp
import numpy as np
from jax import lax
from jax.experimental import pallas as pl
from jax.experimental.pallas import tpu as pltpu
from jax.sharding import PartitionSpec as P

BF = jnp.bfloat16
F32 = jnp.float32
LANES = 128


def two(matrix):
    high = np.asarray(matrix, np.float64).astype(BF)
    low = (matrix - high.astype(np.float64)).astype(BF)
    return high, low


def three_terms(matrix):
    high, low = two(matrix)
    return np.concatenate([high, high, low], 1)


def terms_below(matrix):
    high, low = two(matrix)
    return np.concatenate([high, high, low], 0)


def up(count):
    out = np.zeros((2 * count, count + 1))
    for i in range(count):
        out[2 * i, i] = 1.0
        out[2 * i + 1, i] = out[2 * i + 1, i + 1] = 0.5
    return out


def up_closed(count):
    return up(count)[:, :count]


def both_sides(table):
    size = table.shape[0]
    return [np.pad(table, ((at, LANES - size - at), (0, 0))) for at in (0, LANES - size)]


class Level:
    def __init__(self, taps, out_x, out_y, shift, window, size_z, rows_y, rows_y_end, cols_z):
        half = taps // 2
        self.taps, self.out_x, self.in_x = taps, out_x, out_x + taps - 1
        period_y = out_y + 2 * half + (out_y + 1) % 2
        period_z = size_z + half
        self.freq = (period_y + 1) // 2
        self.main = min(LANES, period_z)
        self.left = period_z - self.main
        assert self.freq % 8 == 0 and self.left <= 8 and self.freq <= LANES
        self.rows = self.freq + (8 if self.left else 0)
        turn_z, turn_y = 2 * np.pi / period_z, 2 * np.pi / period_y
        freq_y, freq_z = np.arange(self.freq), np.arange(period_z)

        cells = np.arange(window)
        needed = (cells >= shift - half) & (cells < shift + out_y + half)
        angle = turn_y * np.outer(freq_y, cells)
        self.table_y = np.concatenate([np.cos(angle), -np.sin(angle)], 0) * needed
        self.to_y = np.concatenate(two(self.table_y), 1)
        self.table_z = self.columns(turn_z * np.outer(np.arange(size_z), freq_z))
        self.to_z = terms_below(self.table_z)

        offsets = np.arange(taps) - half
        angle = turn_y * np.outer(freq_y, offsets)
        table = np.zeros((2 * self.freq, 16))
        table[:, :taps] = np.concatenate([np.cos(angle), np.sin(angle)], 0)
        self.kernel_y = np.concatenate(two(table), 1)
        table = self.columns(turn_z * np.outer(offsets, freq_z))
        table = terms_below(np.pad(table, ((0, 16 - taps), (0, 0))))
        self.kernel_z = np.pad(table, ((0, LANES - 48), (0, 0)))

        angle = turn_z * np.outer(freq_z, np.arange(size_z))
        table = np.concatenate([np.cos(angle) @ cols_z.T, np.sin(angle) @ cols_z.T], 1) / period_z
        lanes = np.zeros((LANES * (2 if self.left else 1), table.shape[1]))
        lanes[: self.main] = table[: self.main]
        if self.left:
            for group in range(self.freq // 8):
                at = LANES + 8 * group
                lanes[at : at + self.left] = table[self.main :]
        self.from_z = terms_below(lanes)
        weight = np.where(freq_y == 0, 1.0, 2.0) / period_y
        angle = turn_y * np.outer(np.arange(out_y) + shift, freq_y)
        wave = np.concatenate([weight * np.cos(angle), -weight * np.sin(angle)], 1)
        self.from_y = [three_terms(rows @ wave) for rows in (rows_y, rows_y_end)]

    def columns(self, angle):
        out = []
        for start, stop in ((0, self.main), (self.main, self.main + self.left)):
            for wave in (np.cos(angle[:, start:stop]), np.sin(angle[:, start:stop])):
                table = np.zeros((angle.shape[0], LANES))
                for group in range(1 if start == 0 else self.freq // 8):
                    table[:, 8 * group : 8 * group + stop - start] = wave
                out.append(table)
            if not self.left:
                break
        return np.concatenate(out, 1)


def down(count, first, length):
    out = np.zeros((count, length))
    for j in range(count):
        for a, w in ((-1, 0.5), (0, 1.0), (1, 0.5)):
            if 0 <= first + 2 * j + a < length:
                out[j, first + 2 * j + a] = w
    return out


def dot(a, b):
    return jnp.dot(a, b, preferred_element_type=F32)


def split(value, terms):
    out = []
    for _ in range(terms - 1):
        out.append(value.astype(BF))
        value = value - out[-1].astype(F32)
    return out + [value.astype(BF)]


def side_by_side(value):
    high, low = split(value, 2)
    return jnp.concatenate([high, low, high], 1)


def fold(value):
    groups = value.shape[0] // 8
    lane = lax.broadcasted_iota(jnp.int32, (8, LANES), 1)
    out = value[8 * (groups - 1) :]
    for group in range(groups - 2, -1, -1):
        out = jnp.where(lane < 8 * (group + 1), value[8 * group : 8 * (group + 1)], out)
    return out


def unfold(value, groups):
    lane = lax.broadcasted_iota(jnp.int32, (8, LANES), 1)
    return jnp.concatenate(
        [
            jnp.where((lane >= 8 * group) & (lane < 8 * (group + 1)), value, 0.0)
            for group in range(groups)
        ],
        0,
    )


def joined(spread, sign):
    freq = spread.shape[0] // 2
    outs = []
    for at in range(0, spread.shape[1], 2 * LANES):
        rc, rs = spread[:freq, at : at + LANES], spread[:freq, at + LANES : at + 2 * LANES]
        ic, js = spread[freq:, at : at + LANES], spread[freq:, at + LANES : at + 2 * LANES]
        if at:
            rc, rs, ic, js = fold(rc), fold(rs), fold(ic), fold(js)
        outs.append((rc + js, ic - rs) if sign > 0 else (rc - js, ic + rs))
    return [jnp.concatenate([out[k] for out in outs], 0) for k in range(2)]


def batches(count, size, body):
    def trip(i, _):
        first = i * size
        body([first + k for k in range(size)], first)
        return 0

    whole = count // size
    if whole > 1:
        lax.fori_loop(0, whole, trip, 0)
    else:
        whole = 0
    for first in range(whole * size, count, size):
        body(list(range(first, min(count, first + size))), first)


def rows_at(first, period, count):
    return pl.ds(first * period if isinstance(first, int) else pl.multiple_of(first * period, 16), count * period)


def store_terms(terms, first, rows, values):
    high, low = split(jnp.concatenate(values, 0), 2)
    terms[0, rows_at(first, rows, len(values)), :] = high
    terms[1, rows_at(first, rows, len(values)), :] = low


def to_frequencies_y(read, count, size, to_y, terms, packed=False):
    rows = terms.shape[1] // count

    def body(xs, first):
        values = []
        for k in range(0, len(xs), 2):
            cells = [read(x) for x in xs[k : k + 2]]
            width = cells[0].shape[1]
            if width % LANES == 0:
                cells = [jnp.concatenate(cells, 1)]
            for part in cells:
                spread = dot(to_y[...], jnp.concatenate([part, part], 0))
                for at in range(0, spread.shape[1], width):
                    value = spread[:, at : at + width]
                    if packed:
                        low_lanes = lax.broadcasted_iota(jnp.int32, (rows, LANES), 1) < LANES // 2
                        value = jnp.where(low_lanes, value[:rows], value[rows:])
                    values.append(value)
        store_terms(terms, first, rows, values)

    batches(count, size, body)


def to_frequencies_z(terms, size, to_z, real, imag):
    count = real.shape[0]
    rows = terms.shape[1] // count

    def body(xs, first):
        span = rows_at(first, rows, len(xs))
        high, low = terms[0, span, :], terms[1, span, :]
        width = high.shape[1]
        if width % LANES == 0:
            spread = dot(jnp.concatenate([high, low, high], 1), to_z[...])
        else:
            spread = dot(high, to_z[:width]) + dot(low, to_z[width : 2 * width])
            spread = spread + dot(high, to_z[2 * width :])
        for k, x in enumerate(xs):
            real[x], imag[x] = joined(spread[k * rows : (k + 1) * rows], 1)

    batches(count, size, body)


def from_frequencies_z(real, imag, size, from_z, terms):
    count = real.shape[0]
    rows = terms.shape[1] // count
    freq = rows // 2

    def body(xs, first):
        lines = []
        for x in xs:
            for ref in (real, imag):
                value = ref[x]
                main = value[:freq]
                if value.shape[0] > freq:
                    main = jnp.concatenate([main, unfold(value[freq:], freq // 8)], 1)
                lines.append(main)
        spread = dot(side_by_side(jnp.concatenate(lines, 0)), from_z[...])
        half = spread.shape[1] // 2
        values = []
        for k in range(len(xs)):
            r = spread[k * rows : k * rows + freq]
            i = spread[k * rows + freq : (k + 1) * rows]
            values += [r[:, :half] - i[:, half:], r[:, half:] + i[:, :half]]
        high, low = split(jnp.concatenate(values, 0), 2)
        terms[0, rows_at(first, rows, len(xs)), :] = high
        terms[1, rows_at(first, rows, len(xs)), :] = low

    batches(count, size, body)


def from_frequencies_y(terms, count, size, from_y, write):
    rows = terms.shape[1] // count

    def body(xs, first):
        for k in range(0, len(xs), 2):
            parts = []
            for x in xs[k : k + 2]:
                span = rows_at(x, rows, 1)
                high, low = terms[0, span, :], terms[1, span, :]
                parts.append(jnp.concatenate([high, low, high], 0))
            value = dot(from_y[...], jnp.concatenate(parts, 1))
            width = parts[0].shape[1]
            for j, x in enumerate(xs[k : k + 2]):
                write(x, value[:, j * width : (j + 1) * width])

    batches(count, size, body)


def along_x(real, imag, spectrum, out_real, out_imag, block, taken=None, before=None):
    kernel_r, kernel_d, kernel_s = spectrum
    taps, period = kernel_r.shape[:2]
    out_x = out_real.shape[0]
    taken = taken or (lambda x: True)

    def body(part, _):
        rows = pl.ds(pl.multiple_of(8 * part, 8), 8)
        for start in range(0, out_x, block):
            count = min(block, out_x - start)
            sums = [[None] * 3 for _ in range(count)]
            seen = {}
            for a in range(taps):
                used = [i for i in range(count) if taken(start + i + a)]
                if used:
                    weights = kernel_r[a, rows, :], kernel_d[a, rows, :], kernel_s[a, rows, :]
                for i in used:
                    x = start + i + a
                    if x not in seen:
                        r, m = real(x, rows), imag(x, rows)
                        seen[x] = r + m, r, m
                    for k in range(3):
                        term = weights[k] * seen[x][k]
                        sums[i][k] = term if sums[i][k] is None else sums[i][k] + term
            for i in range(count):
                values = []
                if sums[i][0] is not None:
                    values.append((sums[i][0] - sums[i][2], sums[i][0] + sums[i][1]))
                if before is not None:
                    values.append((before[0][start + i, rows, :], before[1][start + i, rows, :]))
                out_real[start + i, rows, :] = sum(value[0] for value in values)
                out_imag[start + i, rows, :] = sum(value[1] for value in values)
        return 0

    lax.fori_loop(0, period // 8, body, 0)


def rows_loop(count, step, body):
    def trip(i, _):
        for k in range(step):
            body(i * step + k)
        return 0

    lax.fori_loop(0, count // step, trip, 0)
    for x in range(count - count % step, count):
        body(x)


def all_terms(value):
    return jnp.concatenate(split(value, 3), 0)


def spectra_kernel(sizes, *refs):
    kernels, table, outs, (padded, lines) = refs[0], refs[1], refs[2:-2], refs[-2:]
    levels, taps = kernels.shape[:2]
    padded[...] = jnp.zeros(padded.shape, padded.dtype)
    at_z = 0
    for level in range(levels):
        outs_here = outs[3 * level : 3 * level + 3]
        rows, columns, row, lane = sizes[level]
        kernel_y = table[row : row + rows, lane : lane + 32]
        kernel_z = table[:, at_z : at_z + columns]
        at_z += columns
        for at in (0, 16, 32):
            padded[:, :taps, at : at + taps] = kernels[level].astype(F32)
        cells = jnp.concatenate([padded[a].astype(BF) for a in range(taps)], 1)
        spread = dot(kernel_y, jnp.concatenate([cells, cells], 0))
        lane = lax.broadcasted_iota(jnp.int32, (rows, LANES), 1)
        middle = (lane >= 16) & (lane < 32)
        for a in range(taps):
            high, low = (term.astype(F32) for term in split(spread[:, a * LANES : (a + 1) * LANES], 2))
            lines[a * rows : (a + 1) * rows, :] = jnp.where(middle, low, high).astype(BF)

        def body(xs, first, rows=rows, kernel_z=kernel_z, outs=outs_here):
            spread = dot(lines[rows_at(first, rows, len(xs)), :], kernel_z)
            for k, a in enumerate(xs):
                real, imag = joined(spread[k * rows : (k + 1) * rows], -1)
                outs[0][a] = real
                outs[1][a] = imag - real
                outs[2][a] = imag + real

        batches(taps, 5, body)


def chosen(flag, first, second):
    return jnp.where(flag, first, second)


def pack_kernel(
    own, got_a, got_b, down_z, down_y, ordered, near, coarse, next_a, next_b, far_a, far_b, part
):
    count, size = own.shape[:2]
    side = got_a.shape[1]
    up_y, up_x, up_far = leads("gy", 1), leads("gx", 1), leads("gx", 2)
    ended = lax.axis_index("gy") == lax.axis_size("gy") - 1
    width = near.shape[1]
    start = side - (width - size) // 2
    window = part.shape[1]

    def body(xs, first):
        rows = []
        for x in xs:
            a, b, o = got_a[x], got_b[x], own[x].astype(BF)
            l, r = chosen(up_y, b, a), chosen(up_y, a, b)
            near[x] = jnp.concatenate([l[start:], o, r[: side - start]], 0)
            low = jnp.concatenate([l, o[: window - side]], 0)
            high = jnp.concatenate([o[size + side - window :], r], 0)
            rows.append(jnp.concatenate([low, high], 1))
        value = dot(jnp.concatenate(rows, 0), down_z[...])
        for k, x in enumerate(xs):
            part[x] = value[k * window : (k + 1) * window]

    batches(count, 4, body)
    half = down_y.shape[0] // 2
    shape = (half, LANES)
    high_lanes = lax.broadcasted_iota(jnp.int32, shape, 1) >= LANES // 2
    outside = high_lanes & (lax.broadcasted_iota(jnp.int32, shape, 0) >= half // 2)
    outside = outside & ended
    last = count // 2
    totals = []
    for i in range(last + 1):
        if i == 0:
            total = part[0] + 0.5 * part[1]
        elif i == last:
            total = 0.5 * part[count - 1]
        else:
            total = 0.5 * part[2 * i - 1] + part[2 * i] + 0.5 * part[2 * i + 1]
        totals.append(dot(down_y[...], all_terms(total)))
    for i, total in enumerate(totals):
        row = jnp.where(high_lanes, total[half:], total[:half])
        row = jnp.where(outside, 0.0, row)
        if i == 0:
            for k, term in enumerate(split(row, 3)):
                coarse[k] = term
        elif i == last:
            for k, term in enumerate(split(row, 3)):
                coarse[last + 2 + k] = term
        else:
            coarse[i + 2] = row.astype(BF)
    lines = next_a.shape[0] - coarse.shape[0] * half
    tail = count - lines // width
    far_tail = coarse.shape[0] - far_a.shape[0]
    for out, upward in ((next_a, up_x), (next_b, jnp.logical_not(up_x))):
        first = jnp.where(upward, tail, 0)
        for x in range(lines // width):
            out[x * width : (x + 1) * width, :] = near[first + x]
        for k in range(coarse.shape[0]):
            out[lines + k * half : lines + (k + 1) * half, :] = coarse[k]
    for out, upward in ((far_a, up_far), (far_b, jnp.logical_not(up_far))):
        first = jnp.where(upward, far_tail, 0)
        for k in range(far_a.shape[0]):
            out[k] = coarse[first + k]


def own_kernel(near, to_y, to_z, real, imag, ahead):
    count = real.shape[0]
    to_frequencies_y(lambda x: near[x], count, 8, to_y, ahead)
    to_frequencies_z(ahead, 4, to_z, real, imag)


def own_sum_kernel(real, imag, kr, kd, ks, out_real, out_imag):
    count = real.shape[0]
    half = kr.shape[0] // 2
    along_x(
        lambda x, rows: real[x - half, rows, :],
        lambda x, rows: imag[x - half, rows, :],
        (kr, kd, ks),
        out_real,
        out_imag,
        8,
        lambda x: half <= x < half + count,
    )


def final_kernel(
    t_columns,
    part_real,
    part_imag,
    next_a,
    next_b,
    far_a,
    far_b,
    coarse,
    kr,
    kd,
    ks,
    to_y,
    to_z,
    from_z,
    from_y,
    mr,
    md,
    ms,
    m_to_y,
    m_to_z,
    m_from_z,
    m_from_y,
    tr,
    td,
    ts,
    t_down_y,
    t_down_z,
    t_to_y,
    t_to_z,
    t_from_z,
    t_from_y,
    out,
    side_real,
    side_imag,
    er,
    ei,
    ahead,
    back,
    mid,
    m_real,
    m_imag,
    m_er,
    m_ei,
    m_ahead,
    m_back,
    m_out,
    t_real,
    t_imag,
    t_er,
    t_ei,
    t_cells,
    t_ahead,
    t_back,
    t_out,
):
    left_x = lax.axis_size("gx") - lax.axis_index("gx")
    ended_x, close_x = left_x == 1, left_x <= 2
    ended_y = (lax.axis_index("gy") == lax.axis_size("gy") - 1).astype(jnp.int32)
    up_x, up_far = leads("gx", 1), leads("gx", 2)
    count = part_real.shape[0]
    width = to_y.shape[1] // 2
    reach = side_real.shape[0] // 2
    top_rows = left_x * (count // 4) + reach

    def from_left(at):
        return chosen(up_x, next_b[at, :], next_a[at, :])

    def from_right(at):
        return chosen(up_x, next_a[at, :], next_b[at, :])

    def far_left(k):
        return chosen(up_far, far_b[k], far_a[k])

    def far_right(k):
        return chosen(up_far, far_a[k], far_b[k])

    def side_cells(x):
        read, first = (from_left, x) if x < reach else (from_right, x - reach)
        return read(slice(first * width, (first + 1) * width))

    for first in range(0, 2 * reach, 2):
        xs = [first, first + 1]
        cells = jnp.concatenate([side_cells(x) for x in xs], 1)
        spread = dot(to_y[...], jnp.concatenate([cells, cells], 0))
        store_terms(ahead, first, to_y.shape[0], [spread[:, :LANES], spread[:, LANES:]])
    to_frequencies_z(ahead, 7, to_z, side_real, side_imag)

    def source(side):
        return lambda x, rows: side[x if x < reach else x - count, rows, :]

    along_x(
        source(side_real),
        source(side_imag),
        (kr, kd, ks),
        er,
        ei,
        8,
        lambda x: x < reach or x >= reach + count,
        (part_real, part_imag),
    )
    from_frequencies_z(er, ei, 4, from_z, back)

    def fine_write(x, value):
        out[x] = value

    from_frequencies_y(back, count, 8, from_y, fine_write)

    half = mid.shape[1]
    last = count // 2
    lines = next_a.shape[0] - coarse.shape[0] * half

    def left_row(k):
        return from_left(slice(lines + k * half, lines + (k + 1) * half))

    def right_row(k):
        return from_right(slice(lines + k * half, lines + (k + 1) * half))

    def added(first, second, dropped=None):
        value = sum(first(2 - k).astype(F32) for k in range(3))
        value = value + sum(second(last + 4 - k).astype(F32) for k in range(3))
        if dropped is not None:
            value = jnp.where(dropped, 0.0, value)
        return value.astype(BF)

    spare = far_a.shape[0] - 3
    far_first = coarse.shape[0] - far_a.shape[0]
    rows = [far_left(k) for k in range(spare)]
    rows += [added(left_row, lambda k: far_left(k - far_first))]
    rows += [left_row(k) for k in range(3, last + 2)]
    rows += [added(lambda k: coarse[k], left_row)]
    rows += [coarse[k] for k in range(3, last + 2)]
    rows += [added(right_row, lambda k: coarse[k], ended_x)]
    rows += [right_row(k) for k in range(3, last + 2)]
    rows += [added(far_right, right_row, close_x)]
    rows += [far_right(k) for k in range(3, 3 + spare)]
    for k, row in enumerate(rows):
        mid[k] = row

    skip = (mid.shape[0] - m_real.shape[0]) // 2
    to_frequencies_y(lambda x: mid[x + skip], m_real.shape[0], 9, m_to_y, m_ahead, True)
    to_frequencies_z(m_ahead, 9, m_to_z, m_real, m_imag)

    t_width = t_cells.shape[1]
    spare = (t_width - t_columns) // 2
    inside = lax.broadcasted_iota(jnp.int32, (t_width, t_cells.shape[2]), 0)
    inside = inside < jnp.where(ended_y == 1, t_width - spare, t_width)

    def top_cells(xs, first):
        spreads = []
        for t in xs:
            total = 0.5 * mid[2 * t].astype(F32) + mid[2 * t + 1].astype(F32) + 0.5 * mid[2 * t + 2].astype(F32)
            spreads.append(dot(t_down_y[...], all_terms(total)))
        low = jnp.concatenate([spread[:t_width] for spread in spreads], 0)
        high = jnp.concatenate([spread[t_width:] for spread in spreads], 0)
        value = dot(jnp.concatenate(split(low, 3) + split(high, 3), 1), t_down_z[...])
        for k, t in enumerate(xs):
            row = jnp.where(inside, value[k * t_width : (k + 1) * t_width], 0.0)
            t_cells[t] = jnp.where(t < top_rows, row, 0.0).astype(BF)

    batches(t_real.shape[0], 7, top_cells)
    to_frequencies_y(lambda x: t_cells[x], t_real.shape[0], 7, t_to_y, t_ahead)
    to_frequencies_z(t_ahead, 7, t_to_z, t_real, t_imag)

    def plain(ref):
        return lambda x, rows: ref[x, rows, :]

    along_x(plain(m_real), plain(m_imag), (mr, md, ms), m_er, m_ei, 7)
    along_x(plain(t_real), plain(t_imag), (tr, td, ts), t_er, t_ei, 7)

    def top_write(x, value):
        t_out[x] = value

    def mid_write(x, value):
        m_out[x] = value

    from_frequencies_z(t_er, t_ei, 7, t_from_z, t_back)
    from_frequencies_z(m_er, m_ei, 7, m_from_z, m_back)
    from_frequencies_y(t_back, t_out.shape[0], 7, t_from_y.at[ended_y], top_write)
    from_frequencies_y(m_back, m_out.shape[0], 7, m_from_y.at[ended_y], mid_write)
    keep = jnp.where(ended_x, 0.0, 1.0)
    top = t_out.shape[0] - 1
    t_out[top] = t_out[top] * keep
    for i in range(top):
        m_out[2 * i] += t_out[i]
        m_out[2 * i + 1] += 0.5 * (t_out[i] + t_out[i + 1])
    m_out[2 * top] = (m_out[2 * top] + t_out[top]) * keep

    def finish(i):
        out[2 * i] += m_out[i]
        out[2 * i + 1] += 0.5 * (m_out[i] + m_out[i + 1])

    rows_loop(count // 2, 2, finish)


def call(kernel, outs, scratch, args, mib, loose=()):
    vmem = pl.BlockSpec(memory_space=pltpu.VMEM)
    return pl.pallas_call(
        kernel,
        out_shape=outs,
        in_specs=[
            pl.BlockSpec(memory_space=pl.ANY) if i in loose else vmem for i in range(len(args))
        ],
        out_specs=jax.tree.map(lambda _: vmem, outs),
        scratch_shapes=[pltpu.VMEM(shape, dtype) for dtype, shape in scratch],
        compiler_params=pltpu.CompilerParams(vmem_limit_bytes=mib << 20),
    )(*args)


def level_scratch(level, ny, nz, lanes, extra=()):
    rows = [
        (F32, (count, level.rows, LANES))
        for count in (level.in_x, level.in_x, level.out_x, level.out_x)
    ]
    terms = [
        (BF, (2, level.in_x * 2 * level.freq, lanes)),
        (BF, (2, level.out_x * 2 * level.freq, nz)),
    ]
    return [*rows, *extra, *terms, (F32, (level.out_x, ny, nz))]


def leads(axis, by):
    return lax.rem(lax.div(lax.axis_index(axis), by), 2) == 0


def swapped(first, second, axis, by):
    length = lax.axis_size(axis)
    outs = []
    for value, turn in ((first, 0), (second, 1)):
        up = [i for i in range(length - by) if i // by % 2 == turn]
        pairs = [(i, i + by) for i in up] + [(i + by, i) for i in up]
        outs.append(lax.ppermute(value, axis, pairs))
    return outs


def block(charges, kernel_fine, kernel_mid, kernel_top):
    nx, ny, nz = charges.shape
    taps = kernel_fine.shape[0]
    half = taps // 2
    wide = half + 1

    ident = np.eye(ny)
    width = ny + 2 * wide
    fine = Level(taps, nx, ny, wide, width, nz, ident, ident, np.eye(nz))
    my, mz = ny // 2, nz // 2
    to_fine = up(my)
    ended = np.diag([1.0] * my + [0.0])
    mid = Level(
        taps, nx // 2 + 1, my + 1, ny // 4, ny, mz, to_fine, to_fine @ ended, up_closed(mz)
    )
    ty, tz = my // 2, mz // 2
    to_mid = np.concatenate([up(ty), np.eye(ty + 1)[-1:]], 0)
    top_ended = np.diag([1.0] * ty + [0.0])
    top = Level(
        taps,
        nx // 4 + 1,
        ty + 1,
        wide,
        ty + 2 * wide,
        tz,
        to_fine @ to_mid,
        to_fine @ to_mid @ top_ended,
        up_closed(mz) @ up_closed(tz),
    )

    levels = (fine, mid, top)
    outs = [
        jax.ShapeDtypeStruct((taps, level.rows, LANES), F32)
        for level in levels
        for _ in range(3)
    ]
    table = np.concatenate([level.kernel_z for level in levels], 1)
    sizes = []
    for level, other in ((fine, None), (mid, None), (top, mid)):
        rows, columns = level.kernel_y.shape[0], level.kernel_z.shape[1]
        row, lane = 48 + (other.kernel_y.shape[0] if other else 0), 0 if level is fine else LANES
        assert row + rows <= LANES
        table[row : row + rows, lane : lane + 32] = level.kernel_y
        sizes.append((rows, columns, row, lane))
    spectra = call(
        functools.partial(spectra_kernel, sizes),
        outs,
        [(F32, (taps, 16, LANES)), (BF, (taps * 2 * fine.freq, LANES))],
        [jnp.stack([kernel_fine, kernel_mid, kernel_top]), table],
        8,
    )

    side = ny // 2
    up_y = leads("gy", 1)
    got_a, got_b = swapped(
        *(
            lax.dynamic_slice_in_dim(charges, jnp.where(flag, side, 0), side, 1).astype(BF)
            for flag in (up_y, jnp.logical_not(up_y))
        ),
        "gy",
        1,
    )

    window = side + ny // 2 + 16
    packed = ny // 2
    down_z = np.concatenate([np.pad(down(mz, 0, nz).T, ((0, 0), (at, mz - at))) for at in (0, mz)], 0)
    shift = ny + 2 * side - window
    down_y = np.concatenate([down(packed, 0, window), down(packed, 2 * packed - shift, window)], 0)
    mx = nx // 2
    lines = mx - 1 + 6
    reach = 2 * half + 1 - mx
    assert 0 < reach <= mx - 1 and 2 * mz == LANES == nz
    shapes = [
        (nx, width, LANES),
        (lines, packed, LANES),
        (half * width + lines * packed, LANES),
        (half * width + lines * packed, LANES),
        (reach + 3, packed, LANES),
        (reach + 3, packed, LANES),
    ]
    near, coarse, next_a, next_b, far_a, far_b = call(
        pack_kernel,
        [jax.ShapeDtypeStruct(shape, BF) for shape in shapes],
        [(F32, (nx, window, LANES))],
        [
            charges,
            got_a,
            got_b,
            down_z.astype(BF),
            np.tile(down_y, (1, 3)).astype(BF),
            spectra[0],
        ],
        8,
        loose=(5,),
    )
    far_a, far_b = swapped(far_a, far_b, "gx", 2)
    next_a, next_b = swapped(next_a, next_b, "gx", 1)

    spectrum = [jax.ShapeDtypeStruct((nx, fine.rows, LANES), F32)] * 2
    own = call(
        own_kernel,
        spectrum,
        [(BF, (2, nx * 2 * fine.freq, nz))],
        [near, fine.to_y, fine.to_z],
        10,
    )
    own = call(own_sum_kernel, spectrum, [], [*own, *spectra[:3]], 8)

    wide_top = ty + 2 * wide
    t_down_y = down(wide_top, 0, 2 * packed)
    t_down_y = np.concatenate([t_down_y[:, :packed], t_down_y[:, packed:]], 0)
    t_down_z = np.concatenate(
        [np.tile(table, (3, 1)) for table in both_sides(down(tz, 0, mz).T)], 0
    )
    return call(
        functools.partial(final_kernel, ty),
        jax.ShapeDtypeStruct((nx, ny, nz), F32),
        [
            (F32, (2 * half, fine.rows, LANES)),
            (F32, (2 * half, fine.rows, LANES)),
            (F32, (nx, fine.rows, LANES)),
            (F32, (nx, fine.rows, LANES)),
            (BF, (2, 2 * half * 2 * fine.freq, nz)),
            (BF, (2, nx * 2 * fine.freq, nz)),
            (BF, (3 * mx + 1 + 2 * reach, packed, LANES)),
            *level_scratch(mid, ny, nz, LANES),
            *level_scratch(top, ny, nz, tz, [(BF, (top.in_x, wide_top, tz))]),
        ],
        [
            *own,
            next_a,
            next_b,
            far_a,
            far_b,
            coarse,
            *spectra[:3],
            fine.to_y,
            fine.to_z,
            fine.from_z,
            fine.from_y[0],
            *spectra[3:6],
            np.concatenate([np.concatenate(two(mid.table_y[:, at : at + packed]), 1) for at in (0, packed)], 0),
            terms_below(np.tile(mid.table_z, (2, 1))),
            mid.from_z,
            np.stack(mid.from_y),
            *spectra[6:],
            np.tile(t_down_y, (1, 3)).astype(BF),
            t_down_z.astype(BF),
            top.to_y,
            top.to_z,
            top.from_z,
            np.stack(top.from_y),
        ],
        26,
    )


def solution(mesh):
    placed = (P("gx", "gy", None), P(), P(), P())
    return jax.shard_map(
        block, mesh=mesh, in_specs=placed, out_specs=P("gx", "gy", None), check_vma=False
    )
```

```python
import functools

import jax
import jax.numpy as jnp
import numpy as np
from jax import lax
from jax.experimental import pallas as pl
from jax.experimental.pallas import tpu as pltpu
from jax.sharding import PartitionSpec as P

BF = jnp.bfloat16
F32 = jnp.float32
LANES = 128


def two(matrix):
    high = np.asarray(matrix, np.float64).astype(BF)
    low = (matrix - high.astype(np.float64)).astype(BF)
    return high, low


def three_terms(matrix):
    high, low = two(matrix)
    return np.concatenate([high, high, low], 1)


def terms_below(matrix):
    high, low = two(matrix)
    return np.concatenate([high, high, low], 0)


def up(count):
    out = np.zeros((2 * count, count + 1))
    for i in range(count):
        out[2 * i, i] = 1.0
        out[2 * i + 1, i] = out[2 * i + 1, i + 1] = 0.5
    return out


def up_closed(count):
    return up(count)[:, :count]


def both_sides(table):
    size = table.shape[0]
    return [np.pad(table, ((at, LANES - size - at), (0, 0))) for at in (0, LANES - size)]


class Level:
    def __init__(self, taps, out_x, out_y, shift, window, size_z, rows_y, rows_y_end, cols_z):
        half = taps // 2
        self.taps, self.out_x, self.in_x = taps, out_x, out_x + taps - 1
        period_y = out_y + 2 * half + (out_y + 1) % 2
        period_z = size_z + half
        self.freq = (period_y + 1) // 2
        self.main = min(LANES, period_z)
        self.left = period_z - self.main
        assert self.freq % 8 == 0 and self.left <= 8 and self.freq <= LANES
        self.rows = self.freq + (8 if self.left else 0)
        turn_z, turn_y = 2 * np.pi / period_z, 2 * np.pi / period_y
        freq_y, freq_z = np.arange(self.freq), np.arange(period_z)

        cells = np.arange(window)
        needed = (cells >= shift - half) & (cells < shift + out_y + half)
        angle = turn_y * np.outer(freq_y, cells)
        self.table_y = np.concatenate([np.cos(angle), -np.sin(angle)], 0) * needed
        self.to_y = np.concatenate(two(self.table_y), 1)
        self.table_z = self.columns(turn_z * np.outer(np.arange(size_z), freq_z))
        self.to_z = terms_below(self.table_z)

        offsets = np.arange(taps) - half
        angle = turn_y * np.outer(freq_y, offsets)
        table = np.zeros((2 * self.freq, 16))
        table[:, :taps] = np.concatenate([np.cos(angle), np.sin(angle)], 0)
        self.kernel_y = np.concatenate(two(table), 1)
        table = self.columns(turn_z * np.outer(offsets, freq_z))
        table = terms_below(np.pad(table, ((0, 16 - taps), (0, 0))))
        self.kernel_z = np.pad(table, ((0, LANES - 48), (0, 0)))

        angle = turn_z * np.outer(freq_z, np.arange(size_z))
        table = np.concatenate([np.cos(angle) @ cols_z.T, np.sin(angle) @ cols_z.T], 1) / period_z
        lanes = np.zeros((LANES * (2 if self.left else 1), table.shape[1]))
        lanes[: self.main] = table[: self.main]
        if self.left:
            for group in range(self.freq // 8):
                at = LANES + 8 * group
                lanes[at : at + self.left] = table[self.main :]
        self.from_z = terms_below(lanes)
        weight = np.where(freq_y == 0, 1.0, 2.0) / period_y
        angle = turn_y * np.outer(np.arange(out_y) + shift, freq_y)
        wave = np.concatenate([weight * np.cos(angle), -weight * np.sin(angle)], 1)
        self.from_y = [three_terms(rows @ wave) for rows in (rows_y, rows_y_end)]

    def columns(self, angle):
        out = []
        for start, stop in ((0, self.main), (self.main, self.main + self.left)):
            for wave in (np.cos(angle[:, start:stop]), np.sin(angle[:, start:stop])):
                table = np.zeros((angle.shape[0], LANES))
                for group in range(1 if start == 0 else self.freq // 8):
                    table[:, 8 * group : 8 * group + stop - start] = wave
                out.append(table)
            if not self.left:
                break
        return np.concatenate(out, 1)


def down(count, first, length):
    out = np.zeros((count, length))
    for j in range(count):
        for a, w in ((-1, 0.5), (0, 1.0), (1, 0.5)):
            if 0 <= first + 2 * j + a < length:
                out[j, first + 2 * j + a] = w
    return out


def dot(a, b):
    return jnp.dot(a, b, preferred_element_type=F32)


def split(value, terms):
    out = []
    for _ in range(terms - 1):
        out.append(value.astype(BF))
        value = value - out[-1].astype(F32)
    return out + [value.astype(BF)]


def side_by_side(value):
    high, low = split(value, 2)
    return jnp.concatenate([high, low, high], 1)


def fold(value):
    groups = value.shape[0] // 8
    lane = lax.broadcasted_iota(jnp.int32, (8, LANES), 1)
    out = value[8 * (groups - 1) :]
    for group in range(groups - 2, -1, -1):
        out = jnp.where(lane < 8 * (group + 1), value[8 * group : 8 * (group + 1)], out)
    return out


def unfold(value, groups):
    lane = lax.broadcasted_iota(jnp.int32, (8, LANES), 1)
    return jnp.concatenate(
        [
            jnp.where((lane >= 8 * group) & (lane < 8 * (group + 1)), value, 0.0)
            for group in range(groups)
        ],
        0,
    )


def joined(spread, sign):
    freq = spread.shape[0] // 2
    outs = []
    for at in range(0, spread.shape[1], 2 * LANES):
        rc, rs = spread[:freq, at : at + LANES], spread[:freq, at + LANES : at + 2 * LANES]
        ic, js = spread[freq:, at : at + LANES], spread[freq:, at + LANES : at + 2 * LANES]
        if at:
            rc, rs, ic, js = fold(rc), fold(rs), fold(ic), fold(js)
        outs.append((rc + js, ic - rs) if sign > 0 else (rc - js, ic + rs))
    return [jnp.concatenate([out[k] for out in outs], 0) for k in range(2)]


def batches(count, size, body):
    for first in range(0, count, size):
        body(list(range(first, min(count, first + size))), first)


def rows_at(first, period, count):
    return pl.ds(first * period if isinstance(first, int) else pl.multiple_of(first * period, 16), count * period)


def store_terms(terms, first, rows, values):
    high, low = split(jnp.concatenate(values, 0), 2)
    terms[0, rows_at(first, rows, len(values)), :] = high
    terms[1, rows_at(first, rows, len(values)), :] = low


def to_frequencies_y(read, count, size, to_y, terms, packed=False):
    rows = terms.shape[1] // count

    def body(xs, first):
        values = []
        for k in range(0, len(xs), 2):
            cells = [read(x) for x in xs[k : k + 2]]
            width = cells[0].shape[1]
            if width % LANES == 0:
                cells = [jnp.concatenate(cells, 1)]
            for part in cells:
                spread = dot(to_y[...], jnp.concatenate([part, part], 0))
                for at in range(0, spread.shape[1], width):
                    value = spread[:, at : at + width]
                    if packed:
                        low_lanes = lax.broadcasted_iota(jnp.int32, (rows, LANES), 1) < LANES // 2
                        value = jnp.where(low_lanes, value[:rows], value[rows:])
                    values.append(value)
        store_terms(terms, first, rows, values)

    batches(count, size, body)


def to_frequencies_z(terms, size, to_z, real, imag):
    count = real.shape[0]
    rows = terms.shape[1] // count

    def body(xs, first):
        span = rows_at(first, rows, len(xs))
        high, low = terms[0, span, :], terms[1, span, :]
        width = high.shape[1]
        if width % LANES == 0:
            spread = dot(jnp.concatenate([high, low, high], 1), to_z[...])
        else:
            spread = dot(high, to_z[:width]) + dot(low, to_z[width : 2 * width])
            spread = spread + dot(high, to_z[2 * width :])
        for k, x in enumerate(xs):
            real[x], imag[x] = joined(spread[k * rows : (k + 1) * rows], 1)

    batches(count, size, body)


def from_frequencies_z(real, imag, size, from_z, terms):
    count = real.shape[0]
    rows = terms.shape[1] // count
    freq = rows // 2

    def body(xs, first):
        lines = []
        for x in xs:
            for ref in (real, imag):
                value = ref[x]
                main = value[:freq]
                if value.shape[0] > freq:
                    main = jnp.concatenate([main, unfold(value[freq:], freq // 8)], 1)
                lines.append(main)
        spread = dot(side_by_side(jnp.concatenate(lines, 0)), from_z[...])
        half = spread.shape[1] // 2
        values = []
        for k in range(len(xs)):
            r = spread[k * rows : k * rows + freq]
            i = spread[k * rows + freq : (k + 1) * rows]
            values += [r[:, :half] - i[:, half:], r[:, half:] + i[:, :half]]
        high, low = split(jnp.concatenate(values, 0), 2)
        terms[0, rows_at(first, rows, len(xs)), :] = high
        terms[1, rows_at(first, rows, len(xs)), :] = low

    batches(count, size, body)


def from_frequencies_y(terms, count, size, from_y, write):
    rows = terms.shape[1] // count

    def body(xs, first):
        for k in range(0, len(xs), 2):
            parts = []
            for x in xs[k : k + 2]:
                span = rows_at(x, rows, 1)
                high, low = terms[0, span, :], terms[1, span, :]
                parts.append(jnp.concatenate([high, low, high], 0))
            value = dot(from_y[...], jnp.concatenate(parts, 1))
            width = parts[0].shape[1]
            for j, x in enumerate(xs[k : k + 2]):
                write(x, value[:, j * width : (j + 1) * width])

    batches(count, size, body)


def along_x(real, imag, spectrum, out_real, out_imag, block, taken=None, before=None):
    kernel_r, kernel_d, kernel_s = spectrum
    taps, period = kernel_r.shape[:2]
    out_x = out_real.shape[0]
    taken = taken or (lambda x: True)

    def body(part, _):
        rows = pl.ds(pl.multiple_of(8 * part, 8), 8)
        for start in range(0, out_x, block):
            count = min(block, out_x - start)
            sums = [[None] * 3 for _ in range(count)]
            seen = {}
            for a in range(taps):
                used = [i for i in range(count) if taken(start + i + a)]
                if used:
                    weights = kernel_r[a, rows, :], kernel_d[a, rows, :], kernel_s[a, rows, :]
                for i in used:
                    x = start + i + a
                    if x not in seen:
                        r, m = real(x, rows), imag(x, rows)
                        seen[x] = r + m, r, m
                    for k in range(3):
                        term = weights[k] * seen[x][k]
                        sums[i][k] = term if sums[i][k] is None else sums[i][k] + term
            for i in range(count):
                values = []
                if sums[i][0] is not None:
                    values.append((sums[i][0] - sums[i][2], sums[i][0] + sums[i][1]))
                if before is not None:
                    values.append((before[0][start + i, rows, :], before[1][start + i, rows, :]))
                out_real[start + i, rows, :] = sum(value[0] for value in values)
                out_imag[start + i, rows, :] = sum(value[1] for value in values)
        return 0

    lax.fori_loop(0, period // 8, body, 0)


def rows_loop(count, step, body):
    def trip(i, _):
        for k in range(step):
            body(i * step + k)
        return 0

    lax.fori_loop(0, count // step, trip, 0)
    for x in range(count - count % step, count):
        body(x)


def all_terms(value):
    return jnp.concatenate(split(value, 3), 0)


def spectra_kernel(sizes, *refs):
    kernels, table, outs, (padded, lines) = refs[0], refs[1], refs[2:-2], refs[-2:]
    levels, taps = kernels.shape[:2]
    padded[...] = jnp.zeros(padded.shape, padded.dtype)
    at_z = 0
    for level in range(levels):
        outs_here = outs[3 * level : 3 * level + 3]
        rows, columns, row, lane = sizes[level]
        kernel_y = table[row : row + rows, lane : lane + 32]
        kernel_z = table[:, at_z : at_z + columns]
        at_z += columns
        for at in (0, 16, 32):
            padded[:, :taps, at : at + taps] = kernels[level].astype(F32)
        cells = jnp.concatenate([padded[a].astype(BF) for a in range(taps)], 1)
        spread = dot(kernel_y, jnp.concatenate([cells, cells], 0))
        lane = lax.broadcasted_iota(jnp.int32, (rows, LANES), 1)
        middle = (lane >= 16) & (lane < 32)
        for a in range(taps):
            high, low = (term.astype(F32) for term in split(spread[:, a * LANES : (a + 1) * LANES], 2))
            lines[a * rows : (a + 1) * rows, :] = jnp.where(middle, low, high).astype(BF)

        def body(xs, first, rows=rows, kernel_z=kernel_z, outs=outs_here):
            spread = dot(lines[rows_at(first, rows, len(xs)), :], kernel_z)
            for k, a in enumerate(xs):
                real, imag = joined(spread[k * rows : (k + 1) * rows], -1)
                outs[0][a] = real
                outs[1][a] = imag - real
                outs[2][a] = imag + real

        batches(taps, 5, body)


def chosen(flag, first, second):
    return jnp.where(flag, first, second)


def pack_kernel(
    own, got_a, got_b, down_z, down_y, ordered, near, coarse, next_a, next_b, far_a, far_b, part
):
    count, size = own.shape[:2]
    side = got_a.shape[1]
    up_y, up_x, up_far = leads("gy", 1), leads("gx", 1), leads("gx", 2)
    ended = lax.axis_index("gy") == lax.axis_size("gy") - 1
    width = near.shape[1]
    start = side - (width - size) // 2
    window = part.shape[1]

    def body(xs, first):
        rows = []
        for x in xs:
            a, b, o = got_a[x], got_b[x], own[x].astype(BF)
            l, r = chosen(up_y, b, a), chosen(up_y, a, b)
            near[x] = jnp.concatenate([l[start:], o, r[: side - start]], 0)
            low = jnp.concatenate([l, o[: window - side]], 0)
            high = jnp.concatenate([o[size + side - window :], r], 0)
            rows.append(jnp.concatenate([low, high], 1))
        value = dot(jnp.concatenate(rows, 0), down_z[...])
        for k, x in enumerate(xs):
            part[x] = value[k * window : (k + 1) * window]

    batches(count, 4, body)
    half = down_y.shape[0] // 2
    shape = (half, LANES)
    high_lanes = lax.broadcasted_iota(jnp.int32, shape, 1) >= LANES // 2
    outside = high_lanes & (lax.broadcasted_iota(jnp.int32, shape, 0) >= half // 2)
    outside = outside & ended
    last = count // 2
    totals = []
    for i in range(last + 1):
        if i == 0:
            total = part[0] + 0.5 * part[1]
        elif i == last:
            total = 0.5 * part[count - 1]
        else:
            total = 0.5 * part[2 * i - 1] + part[2 * i] + 0.5 * part[2 * i + 1]
        totals.append(dot(down_y[...], all_terms(total)))
    for i, total in enumerate(totals):
        row = jnp.where(high_lanes, total[half:], total[:half])
        row = jnp.where(outside, 0.0, row)
        if i == 0:
            for k, term in enumerate(split(row, 3)):
                coarse[k] = term
        elif i == last:
            for k, term in enumerate(split(row, 3)):
                coarse[last + 2 + k] = term
        else:
            coarse[i + 2] = row.astype(BF)
    lines = next_a.shape[0] - coarse.shape[0] * half
    tail = count - lines // width
    far_tail = coarse.shape[0] - far_a.shape[0]
    for out, upward in ((next_a, up_x), (next_b, jnp.logical_not(up_x))):
        first = jnp.where(upward, tail, 0)
        for x in range(lines // width):
            out[x * width : (x + 1) * width, :] = near[first + x]
        for k in range(coarse.shape[0]):
            out[lines + k * half : lines + (k + 1) * half, :] = coarse[k]
    for out, upward in ((far_a, up_far), (far_b, jnp.logical_not(up_far))):
        first = jnp.where(upward, far_tail, 0)
        for k in range(far_a.shape[0]):
            out[k] = coarse[first + k]


def own_kernel(near, to_y, to_z, real, imag, ahead):
    count = real.shape[0]
    to_frequencies_y(lambda x: near[x], count, 8, to_y, ahead)
    to_frequencies_z(ahead, 4, to_z, real, imag)


def own_sum_kernel(real, imag, kr, kd, ks, out_real, out_imag):
    count = real.shape[0]
    half = kr.shape[0] // 2
    along_x(
        lambda x, rows: real[x - half, rows, :],
        lambda x, rows: imag[x - half, rows, :],
        (kr, kd, ks),
        out_real,
        out_imag,
        8,
        lambda x: half <= x < half + count,
    )


def final_kernel(
    t_columns,
    part_real,
    part_imag,
    next_a,
    next_b,
    far_a,
    far_b,
    coarse,
    kr,
    kd,
    ks,
    to_y,
    to_z,
    from_z,
    from_y,
    mr,
    md,
    ms,
    m_to_y,
    m_to_z,
    m_from_z,
    m_from_y,
    tr,
    td,
    ts,
    t_down_y,
    t_down_z,
    t_to_y,
    t_to_z,
    t_from_z,
    t_from_y,
    out,
    side_real,
    side_imag,
    er,
    ei,
    ahead,
    back,
    mid,
    m_real,
    m_imag,
    m_er,
    m_ei,
    m_ahead,
    m_back,
    m_out,
    t_real,
    t_imag,
    t_er,
    t_ei,
    t_cells,
    t_ahead,
    t_back,
    t_out,
):
    left_x = lax.axis_size("gx") - lax.axis_index("gx")
    ended_x, close_x = left_x == 1, left_x <= 2
    ended_y = (lax.axis_index("gy") == lax.axis_size("gy") - 1).astype(jnp.int32)
    up_x, up_far = leads("gx", 1), leads("gx", 2)
    count = part_real.shape[0]
    width = to_y.shape[1] // 2
    reach = side_real.shape[0] // 2
    top_rows = left_x * (count // 4) + reach

    def from_left(at):
        return chosen(up_x, next_b[at, :], next_a[at, :])

    def from_right(at):
        return chosen(up_x, next_a[at, :], next_b[at, :])

    def far_left(k):
        return chosen(up_far, far_b[k], far_a[k])

    def far_right(k):
        return chosen(up_far, far_a[k], far_b[k])

    def side_cells(x):
        read, first = (from_left, x) if x < reach else (from_right, x - reach)
        return read(slice(first * width, (first + 1) * width))

    for first in range(0, 2 * reach, 2):
        xs = [first, first + 1]
        cells = jnp.concatenate([side_cells(x) for x in xs], 1)
        spread = dot(to_y[...], jnp.concatenate([cells, cells], 0))
        store_terms(ahead, first, to_y.shape[0], [spread[:, :LANES], spread[:, LANES:]])
    to_frequencies_z(ahead, 7, to_z, side_real, side_imag)

    def source(side):
        return lambda x, rows: side[x if x < reach else x - count, rows, :]

    along_x(
        source(side_real),
        source(side_imag),
        (kr, kd, ks),
        er,
        ei,
        8,
        lambda x: x < reach or x >= reach + count,
        (part_real, part_imag),
    )
    from_frequencies_z(er, ei, 4, from_z, back)

    def fine_write(x, value):
        out[x] = value

    from_frequencies_y(back, count, 8, from_y, fine_write)

    half = mid.shape[1]
    last = count // 2
    lines = next_a.shape[0] - coarse.shape[0] * half

    def left_row(k):
        return from_left(slice(lines + k * half, lines + (k + 1) * half))

    def right_row(k):
        return from_right(slice(lines + k * half, lines + (k + 1) * half))

    def added(first, second, dropped=None):
        value = sum(first(2 - k).astype(F32) for k in range(3))
        value = value + sum(second(last + 4 - k).astype(F32) for k in range(3))
        if dropped is not None:
            value = jnp.where(dropped, 0.0, value)
        return value.astype(BF)

    spare = far_a.shape[0] - 3
    far_first = coarse.shape[0] - far_a.shape[0]
    rows = [far_left(k) for k in range(spare)]
    rows += [added(left_row, lambda k: far_left(k - far_first))]
    rows += [left_row(k) for k in range(3, last + 2)]
    rows += [added(lambda k: coarse[k], left_row)]
    rows += [coarse[k] for k in range(3, last + 2)]
    rows += [added(right_row, lambda k: coarse[k], ended_x)]
    rows += [right_row(k) for k in range(3, last + 2)]
    rows += [added(far_right, right_row, close_x)]
    rows += [far_right(k) for k in range(3, 3 + spare)]
    for k, row in enumerate(rows):
        mid[k] = row

    skip = (mid.shape[0] - m_real.shape[0]) // 2
    to_frequencies_y(lambda x: mid[x + skip], m_real.shape[0], 9, m_to_y, m_ahead, True)
    to_frequencies_z(m_ahead, 9, m_to_z, m_real, m_imag)

    t_width = t_cells.shape[1]
    spare = (t_width - t_columns) // 2
    inside = lax.broadcasted_iota(jnp.int32, (t_width, t_cells.shape[2]), 0)
    inside = inside < jnp.where(ended_y == 1, t_width - spare, t_width)

    def top_cells(xs, first):
        spreads = []
        for t in xs:
            total = 0.5 * mid[2 * t].astype(F32) + mid[2 * t + 1].astype(F32) + 0.5 * mid[2 * t + 2].astype(F32)
            spreads.append(dot(t_down_y[...], all_terms(total)))
        low = jnp.concatenate([spread[:t_width] for spread in spreads], 0)
        high = jnp.concatenate([spread[t_width:] for spread in spreads], 0)
        value = dot(jnp.concatenate(split(low, 3) + split(high, 3), 1), t_down_z[...])
        for k, t in enumerate(xs):
            row = jnp.where(inside, value[k * t_width : (k + 1) * t_width], 0.0)
            t_cells[t] = jnp.where(t < top_rows, row, 0.0).astype(BF)

    batches(t_real.shape[0], 7, top_cells)
    to_frequencies_y(lambda x: t_cells[x], t_real.shape[0], 7, t_to_y, t_ahead)
    to_frequencies_z(t_ahead, 7, t_to_z, t_real, t_imag)

    def plain(ref):
        return lambda x, rows: ref[x, rows, :]

    along_x(plain(m_real), plain(m_imag), (mr, md, ms), m_er, m_ei, 7)
    along_x(plain(t_real), plain(t_imag), (tr, td, ts), t_er, t_ei, 7)

    def top_write(x, value):
        t_out[x] = value

    def mid_write(x, value):
        m_out[x] = value

    from_frequencies_z(t_er, t_ei, 7, t_from_z, t_back)
    from_frequencies_z(m_er, m_ei, 7, m_from_z, m_back)
    from_frequencies_y(t_back, t_out.shape[0], 7, t_from_y.at[ended_y], top_write)
    from_frequencies_y(m_back, m_out.shape[0], 7, m_from_y.at[ended_y], mid_write)
    keep = jnp.where(ended_x, 0.0, 1.0)
    top = t_out.shape[0] - 1
    t_out[top] = t_out[top] * keep
    for i in range(top):
        m_out[2 * i] += t_out[i]
        m_out[2 * i + 1] += 0.5 * (t_out[i] + t_out[i + 1])
    m_out[2 * top] = (m_out[2 * top] + t_out[top]) * keep

    def finish(i):
        out[2 * i] += m_out[i]
        out[2 * i + 1] += 0.5 * (m_out[i] + m_out[i + 1])

    rows_loop(count // 2, 2, finish)


def call(kernel, outs, scratch, args, mib, loose=()):
    vmem = pl.BlockSpec(memory_space=pltpu.VMEM)
    return pl.pallas_call(
        kernel,
        out_shape=outs,
        in_specs=[
            pl.BlockSpec(memory_space=pl.ANY) if i in loose else vmem for i in range(len(args))
        ],
        out_specs=jax.tree.map(lambda _: vmem, outs),
        scratch_shapes=[pltpu.VMEM(shape, dtype) for dtype, shape in scratch],
        compiler_params=pltpu.CompilerParams(vmem_limit_bytes=mib << 20),
    )(*args)


def level_scratch(level, ny, nz, lanes, extra=()):
    rows = [
        (F32, (count, level.rows, LANES))
        for count in (level.in_x, level.in_x, level.out_x, level.out_x)
    ]
    terms = [
        (BF, (2, level.in_x * 2 * level.freq, lanes)),
        (BF, (2, level.out_x * 2 * level.freq, nz)),
    ]
    return [*rows, *extra, *terms, (F32, (level.out_x, ny, nz))]


def leads(axis, by):
    return lax.rem(lax.div(lax.axis_index(axis), by), 2) == 0


def swapped(first, second, axis, by):
    length = lax.axis_size(axis)
    outs = []
    for value, turn in ((first, 0), (second, 1)):
        up = [i for i in range(length - by) if i // by % 2 == turn]
        pairs = [(i, i + by) for i in up] + [(i + by, i) for i in up]
        outs.append(lax.ppermute(value, axis, pairs))
    return outs


def block(charges, kernel_fine, kernel_mid, kernel_top):
    nx, ny, nz = charges.shape
    taps = kernel_fine.shape[0]
    half = taps // 2
    wide = half + 1

    ident = np.eye(ny)
    width = ny + 2 * wide
    fine = Level(taps, nx, ny, wide, width, nz, ident, ident, np.eye(nz))
    my, mz = ny // 2, nz // 2
    to_fine = up(my)
    ended = np.diag([1.0] * my + [0.0])
    mid = Level(
        taps, nx // 2 + 1, my + 1, ny // 4, ny, mz, to_fine, to_fine @ ended, up_closed(mz)
    )
    ty, tz = my // 2, mz // 2
    to_mid = np.concatenate([up(ty), np.eye(ty + 1)[-1:]], 0)
    top_ended = np.diag([1.0] * ty + [0.0])
    top = Level(
        taps,
        nx // 4 + 1,
        ty + 1,
        wide,
        ty + 2 * wide,
        tz,
        to_fine @ to_mid,
        to_fine @ to_mid @ top_ended,
        up_closed(mz) @ up_closed(tz),
    )

    levels = (fine, mid, top)
    outs = [
        jax.ShapeDtypeStruct((taps, level.rows, LANES), F32)
        for level in levels
        for _ in range(3)
    ]
    table = np.concatenate([level.kernel_z for level in levels], 1)
    sizes = []
    for level, other in ((fine, None), (mid, None), (top, mid)):
        rows, columns = level.kernel_y.shape[0], level.kernel_z.shape[1]
        row, lane = 48 + (other.kernel_y.shape[0] if other else 0), 0 if level is fine else LANES
        assert row + rows <= LANES
        table[row : row + rows, lane : lane + 32] = level.kernel_y
        sizes.append((rows, columns, row, lane))
    spectra = call(
        functools.partial(spectra_kernel, sizes),
        outs,
        [(F32, (taps, 16, LANES)), (BF, (taps * 2 * fine.freq, LANES))],
        [jnp.stack([kernel_fine, kernel_mid, kernel_top]), table],
        8,
    )

    side = ny // 2
    up_y = leads("gy", 1)
    got_a, got_b = swapped(
        *(
            lax.dynamic_slice_in_dim(charges, jnp.where(flag, side, 0), side, 1).astype(BF)
            for flag in (up_y, jnp.logical_not(up_y))
        ),
        "gy",
        1,
    )

    window = side + ny // 2 + 16
    packed = ny // 2
    down_z = np.concatenate([np.pad(down(mz, 0, nz).T, ((0, 0), (at, mz - at))) for at in (0, mz)], 0)
    shift = ny + 2 * side - window
    down_y = np.concatenate([down(packed, 0, window), down(packed, 2 * packed - shift, window)], 0)
    mx = nx // 2
    lines = mx - 1 + 6
    reach = 2 * half + 1 - mx
    assert 0 < reach <= mx - 1 and 2 * mz == LANES == nz
    shapes = [
        (nx, width, LANES),
        (lines, packed, LANES),
        (half * width + lines * packed, LANES),
        (half * width + lines * packed, LANES),
        (reach + 3, packed, LANES),
        (reach + 3, packed, LANES),
    ]
    near, coarse, next_a, next_b, far_a, far_b = call(
        pack_kernel,
        [jax.ShapeDtypeStruct(shape, BF) for shape in shapes],
        [(F32, (nx, window, LANES))],
        [
            charges,
            got_a,
            got_b,
            down_z.astype(BF),
            np.tile(down_y, (1, 3)).astype(BF),
            spectra[0],
        ],
        8,
        loose=(5,),
    )
    far_a, far_b = swapped(far_a, far_b, "gx", 2)
    next_a, next_b = swapped(next_a, next_b, "gx", 1)

    spectrum = [jax.ShapeDtypeStruct((nx, fine.rows, LANES), F32)] * 2
    own = call(
        own_kernel,
        spectrum,
        [(BF, (2, nx * 2 * fine.freq, nz))],
        [near, fine.to_y, fine.to_z],
        10,
    )
    own = call(own_sum_kernel, spectrum, [], [*own, *spectra[:3]], 8)

    wide_top = ty + 2 * wide
    t_down_y = down(wide_top, 0, 2 * packed)
    t_down_y = np.concatenate([t_down_y[:, :packed], t_down_y[:, packed:]], 0)
    t_down_z = np.concatenate(
        [np.tile(table, (3, 1)) for table in both_sides(down(tz, 0, mz).T)], 0
    )
    return call(
        functools.partial(final_kernel, ty),
        jax.ShapeDtypeStruct((nx, ny, nz), F32),
        [
            (F32, (2 * half, fine.rows, LANES)),
            (F32, (2 * half, fine.rows, LANES)),
            (F32, (nx, fine.rows, LANES)),
            (F32, (nx, fine.rows, LANES)),
            (BF, (2, 2 * half * 2 * fine.freq, nz)),
            (BF, (2, nx * 2 * fine.freq, nz)),
            (BF, (3 * mx + 1 + 2 * reach, packed, LANES)),
            *level_scratch(mid, ny, nz, LANES),
            *level_scratch(top, ny, nz, tz, [(BF, (top.in_x, wide_top, tz))]),
        ],
        [
            *own,
            next_a,
            next_b,
            far_a,
            far_b,
            coarse,
            *spectra[:3],
            fine.to_y,
            fine.to_z,
            fine.from_z,
            fine.from_y[0],
            *spectra[3:6],
            np.concatenate([np.concatenate(two(mid.table_y[:, at : at + packed]), 1) for at in (0, packed)], 0),
            terms_below(np.tile(mid.table_z, (2, 1))),
            mid.from_z,
            np.stack(mid.from_y),
            *spectra[6:],
            np.tile(t_down_y, (1, 3)).astype(BF),
            t_down_z.astype(BF),
            top.to_y,
            top.to_z,
            top.from_z,
            np.stack(top.from_y),
        ],
        26,
    )


def solution(mesh):
    placed = (P("gx", "gy", None), P(), P(), P())
    return jax.shard_map(
        block, mesh=mesh, in_specs=placed, out_specs=P("gx", "gy", None), check_vma=False
    )
```

```python
import functools

import jax
import jax.numpy as jnp
import numpy as np
from jax import lax
from jax.experimental import pallas as pl
from jax.experimental.pallas import tpu as pltpu
from jax.sharding import PartitionSpec as P

BF = jnp.bfloat16
F32 = jnp.float32
LANES = 128
BLOCK = 8
PARTS = 2
TERMS = 3


def two(matrix):
    high = np.asarray(matrix, np.float64).astype(BF)
    low = (matrix - high.astype(np.float64)).astype(BF)
    return high, low


def three_terms(matrix):
    high, low = two(matrix)
    return np.concatenate([high, high, low], 1)


def terms_below(matrix):
    high, low = two(matrix)
    return np.concatenate([high, high, low], 0)


def up(count):
    out = np.zeros((2 * count, count + 1))
    for i in range(count):
        out[2 * i, i] = 1.0
        out[2 * i + 1, i] = out[2 * i + 1, i + 1] = 0.5
    return out


def up_closed(count):
    return up(count)[:, :count]


def both_sides(table):
    size = table.shape[0]
    return [np.pad(table, ((at, LANES - size - at), (0, 0))) for at in (0, LANES - size)]


class Level:
    def __init__(self, taps, out_x, out_y, shift, window, size_z, rows_y, rows_y_end, cols_z):
        half = taps // 2
        self.taps, self.out_x, self.in_x = taps, out_x, out_x + taps - 1
        period_y = out_y + 2 * half + (out_y + 1) % 2
        period_z = size_z + half
        self.freq = (period_y + 1) // 2
        self.main = min(LANES, period_z)
        self.left = period_z - self.main
        assert self.freq % 8 == 0 and self.left <= 8 and self.freq <= LANES
        self.rows = self.freq + (8 if self.left else 0)
        turn_z, turn_y = 2 * np.pi / period_z, 2 * np.pi / period_y
        freq_y, freq_z = np.arange(self.freq), np.arange(period_z)

        cells = np.arange(window)
        needed = (cells >= shift - half) & (cells < shift + out_y + half)
        angle = turn_y * np.outer(freq_y, cells)
        self.table_y = np.concatenate([np.cos(angle), -np.sin(angle)], 0) * needed
        self.to_y = np.concatenate(two(self.table_y), 1)
        self.table_z = self.columns(turn_z * np.outer(np.arange(size_z), freq_z))
        self.to_z = terms_below(self.table_z)

        offsets = np.arange(taps) - half
        angle = turn_y * np.outer(freq_y, offsets)
        table = np.zeros((2 * self.freq, 16))
        table[:, :taps] = np.concatenate([np.cos(angle), np.sin(angle)], 0)
        self.kernel_y = np.concatenate(two(table), 1)
        table = self.columns(turn_z * np.outer(offsets, freq_z))
        table = terms_below(np.pad(table, ((0, 16 - taps), (0, 0))))
        self.kernel_z = np.pad(table, ((0, LANES - 48), (0, 0)))

        angle = turn_z * np.outer(freq_z, np.arange(size_z))
        table = np.concatenate([np.cos(angle) @ cols_z.T, np.sin(angle) @ cols_z.T], 1) / period_z
        lanes = np.zeros((LANES * (2 if self.left else 1), table.shape[1]))
        lanes[: self.main] = table[: self.main]
        if self.left:
            for group in range(self.freq // 8):
                at = LANES + 8 * group
                lanes[at : at + self.left] = table[self.main :]
        self.from_z = terms_below(lanes)
        weight = np.where(freq_y == 0, 1.0, 2.0) / period_y
        angle = turn_y * np.outer(np.arange(out_y) + shift, freq_y)
        wave = np.concatenate([weight * np.cos(angle), -weight * np.sin(angle)], 1)
        self.from_y = [three_terms(rows @ wave) for rows in (rows_y, rows_y_end)]

    def columns(self, angle):
        out = []
        for start, stop in ((0, self.main), (self.main, self.main + self.left)):
            for wave in (np.cos(angle[:, start:stop]), np.sin(angle[:, start:stop])):
                table = np.zeros((angle.shape[0], LANES))
                for group in range(1 if start == 0 else self.freq // 8):
                    table[:, 8 * group : 8 * group + stop - start] = wave
                out.append(table)
            if not self.left:
                break
        return np.concatenate(out, 1)


def down(count, first, length):
    out = np.zeros((count, length))
    for j in range(count):
        for a, w in ((-1, 0.5), (0, 1.0), (1, 0.5)):
            if 0 <= first + 2 * j + a < length:
                out[j, first + 2 * j + a] = w
    return out


def dot(a, b):
    return jnp.dot(a, b, preferred_element_type=F32)


def split(value, terms):
    out = []
    for _ in range(terms - 1):
        out.append(value.astype(BF))
        value = value - out[-1].astype(F32)
    return out + [value.astype(BF)]


def side_by_side(value):
    high, low = split(value, 2)
    return jnp.concatenate([high, low, high], 1)


def fold(value):
    groups = value.shape[0] // 8
    lane = lax.broadcasted_iota(jnp.int32, (8, LANES), 1)
    out = value[8 * (groups - 1) :]
    for group in range(groups - 2, -1, -1):
        out = jnp.where(lane < 8 * (group + 1), value[8 * group : 8 * (group + 1)], out)
    return out


def unfold(value, groups):
    lane = lax.broadcasted_iota(jnp.int32, (8, LANES), 1)
    return jnp.concatenate(
        [
            jnp.where((lane >= 8 * group) & (lane < 8 * (group + 1)), value, 0.0)
            for group in range(groups)
        ],
        0,
    )


def joined(spread, sign):
    freq = spread.shape[0] // 2
    outs = []
    for at in range(0, spread.shape[1], 2 * LANES):
        rc, rs = spread[:freq, at : at + LANES], spread[:freq, at + LANES : at + 2 * LANES]
        ic, js = spread[freq:, at : at + LANES], spread[freq:, at + LANES : at + 2 * LANES]
        if at:
            rc, rs, ic, js = fold(rc), fold(rs), fold(ic), fold(js)
        outs.append((rc + js, ic - rs) if sign > 0 else (rc - js, ic + rs))
    return [jnp.concatenate([out[k] for out in outs], 0) for k in range(2)]


def batches(count, size, body):
    for first in range(0, count, size):
        body(list(range(first, min(count, first + size))), first)


def rows_at(first, period, count):
    return pl.ds(first * period if isinstance(first, int) else pl.multiple_of(first * period, 16), count * period)


def store_terms(terms, first, rows, values):
    high, low = split(jnp.concatenate(values, 0), 2)
    terms[0, rows_at(first, rows, len(values)), :] = high
    terms[1, rows_at(first, rows, len(values)), :] = low


def to_frequencies_y(read, count, size, to_y, terms, packed=False):
    rows = terms.shape[1] // count

    def body(xs, first):
        values = []
        for k in range(0, len(xs), 2):
            cells = [read(x) for x in xs[k : k + 2]]
            width = cells[0].shape[1]
            if width % LANES == 0:
                cells = [jnp.concatenate(cells, 1)]
            for part in cells:
                spread = dot(to_y[...], jnp.concatenate([part, part], 0))
                for at in range(0, spread.shape[1], width):
                    value = spread[:, at : at + width]
                    if packed:
                        low_lanes = lax.broadcasted_iota(jnp.int32, (rows, LANES), 1) < LANES // 2
                        value = jnp.where(low_lanes, value[:rows], value[rows:])
                    values.append(value)
        store_terms(terms, first, rows, values)

    batches(count, size, body)


def to_frequencies_z(terms, size, to_z, real, imag):
    count = real.shape[0]
    rows = terms.shape[1] // count

    def body(xs, first):
        span = rows_at(first, rows, len(xs))
        high, low = terms[0, span, :], terms[1, span, :]
        width = high.shape[1]
        if width % LANES == 0:
            spread = dot(jnp.concatenate([high, low, high], 1), to_z[...])
        else:
            spread = dot(high, to_z[:width]) + dot(low, to_z[width : 2 * width])
            spread = spread + dot(high, to_z[2 * width :])
        for k, x in enumerate(xs):
            real[x], imag[x] = joined(spread[k * rows : (k + 1) * rows], 1)

    batches(count, size, body)


def from_frequencies_z(real, imag, size, from_z, terms):
    count = real.shape[0]
    rows = terms.shape[1] // count
    freq = rows // 2

    def body(xs, first):
        lines = []
        for x in xs:
            for ref in (real, imag):
                value = ref[x]
                main = value[:freq]
                if value.shape[0] > freq:
                    main = jnp.concatenate([main, unfold(value[freq:], freq // 8)], 1)
                lines.append(main)
        spread = dot(side_by_side(jnp.concatenate(lines, 0)), from_z[...])
        half = spread.shape[1] // 2
        values = []
        for k in range(len(xs)):
            r = spread[k * rows : k * rows + freq]
            i = spread[k * rows + freq : (k + 1) * rows]
            values += [r[:, :half] - i[:, half:], r[:, half:] + i[:, :half]]
        high, low = split(jnp.concatenate(values, 0), 2)
        terms[0, rows_at(first, rows, len(xs)), :] = high
        terms[1, rows_at(first, rows, len(xs)), :] = low

    batches(count, size, body)


def from_frequencies_y(terms, count, size, from_y, write):
    rows = terms.shape[1] // count

    def body(xs, first):
        for k in range(0, len(xs), 2):
            parts = []
            for x in xs[k : k + 2]:
                span = rows_at(x, rows, 1)
                high, low = terms[0, span, :], terms[1, span, :]
                parts.append(jnp.concatenate([high, low, high], 0))
            value = dot(from_y[...], jnp.concatenate(parts, 1))
            width = parts[0].shape[1]
            for j, x in enumerate(xs[k : k + 2]):
                write(x, value[:, j * width : (j + 1) * width])

    batches(count, size, body)


def along_x(real, imag, spectrum, out_real, out_imag, block, outputs=None, taken=None, before=None):
    kernel_r, kernel_d, kernel_s = spectrum
    taps, period = kernel_r.shape[:2]
    outputs = outputs or list(range(out_real.shape[0]))
    taken = taken or (lambda x: True)

    def body(part, _):
        rows = pl.ds(pl.multiple_of(8 * part, 8), 8)
        for start in range(0, len(outputs), block):
            wanted = outputs[start : start + block]
            sums = [[None] * 3 for _ in wanted]
            seen = {}
            for a in range(taps):
                used = [i for i, out in enumerate(wanted) if taken(out + a)]
                if used:
                    weights = kernel_r[a, rows, :], kernel_d[a, rows, :], kernel_s[a, rows, :]
                for i in used:
                    x = wanted[i] + a
                    if x not in seen:
                        r, m = real(x, rows), imag(x, rows)
                        seen[x] = r + m, r, m
                    for k in range(3):
                        term = weights[k] * seen[x][k]
                        sums[i][k] = term if sums[i][k] is None else sums[i][k] + term
            for i, out in enumerate(wanted):
                value = sums[i][0] - sums[i][2], sums[i][0] + sums[i][1]
                if before is not None:
                    value = value[0] + before[0][out, rows, :], value[1] + before[1][out, rows, :]
                out_real[start + i, rows, :] = value[0]
                out_imag[start + i, rows, :] = value[1]
        return 0

    lax.fori_loop(0, period // 8, body, 0)


def rows_loop(count, step, body):
    def trip(i, _):
        for k in range(step):
            body(i * step + k)
        return 0

    lax.fori_loop(0, count // step, trip, 0)
    for x in range(count - count % step, count):
        body(x)


def all_terms(value):
    return jnp.concatenate(split(value, TERMS), 0)


def spectra_kernel(sizes, *refs):
    kernels, table, outs, (padded, lines) = refs[0], refs[1], refs[2:-2], refs[-2:]
    levels, taps = kernels.shape[:2]
    padded[...] = jnp.zeros(padded.shape, padded.dtype)
    at_z = 0
    for level in range(levels):
        outs_here = outs[3 * level : 3 * level + 3]
        rows, columns, row, lane = sizes[level]
        kernel_y = table[row : row + rows, lane : lane + 32]
        kernel_z = table[:, at_z : at_z + columns]
        at_z += columns
        for at in (0, 16, 32):
            padded[:, :taps, at : at + taps] = kernels[level].astype(F32)
        cells = jnp.concatenate([padded[a].astype(BF) for a in range(taps)], 1)
        spread = dot(kernel_y, jnp.concatenate([cells, cells], 0))
        lane = lax.broadcasted_iota(jnp.int32, (rows, LANES), 1)
        middle = (lane >= 16) & (lane < 32)
        for a in range(taps):
            high, low = (term.astype(F32) for term in split(spread[:, a * LANES : (a + 1) * LANES], 2))
            lines[a * rows : (a + 1) * rows, :] = jnp.where(middle, low, high).astype(BF)

        def body(xs, first, rows=rows, kernel_z=kernel_z, outs=outs_here):
            spread = dot(lines[rows_at(first, rows, len(xs)), :], kernel_z)
            for k, a in enumerate(xs):
                real, imag = joined(spread[k * rows : (k + 1) * rows], -1)
                outs[0][a] = real
                outs[1][a] = imag - real
                outs[2][a] = imag + real

        batches(taps, 5, body)


def chosen(flag, first, second):
    return jnp.where(flag, first, second)


def pack_kernel(
    own, got_a, got_b, down_z, down_y, ordered, near, coarse, next_a, next_b, far_a, far_b, part
):
    count, size = own.shape[:2]
    side = got_a.shape[1]
    up_y, up_x, up_far = leads("gy", 1), leads("gx", 1), leads("gx", 2)
    ended = lax.axis_index("gy") == lax.axis_size("gy") - 1
    width = near.shape[1]
    start = side - (width - size) // 2
    window = part.shape[1]

    def body(xs, first):
        rows = []
        for x in xs:
            a, b, o = got_a[x], got_b[x], own[x].astype(BF)
            l, r = chosen(up_y, b, a), chosen(up_y, a, b)
            near[x] = jnp.concatenate([l[start:], o, r[: side - start]], 0)
            low = jnp.concatenate([l, o[: window - side]], 0)
            high = jnp.concatenate([o[size + side - window :], r], 0)
            rows.append(jnp.concatenate([low, high], 1))
        value = dot(jnp.concatenate(rows, 0), down_z[...])
        for k, x in enumerate(xs):
            part[x] = value[k * window : (k + 1) * window]

    batches(count, 4, body)
    half = down_y.shape[0] // 2
    shape = (half, LANES)
    high_lanes = lax.broadcasted_iota(jnp.int32, shape, 1) >= LANES // 2
    outside = high_lanes & (lax.broadcasted_iota(jnp.int32, shape, 0) >= half // 2)
    outside = outside & ended
    last = count // 2
    totals = []
    for i in range(last + 1):
        if i == 0:
            total = part[0] + 0.5 * part[1]
        elif i == last:
            total = 0.5 * part[count - 1]
        else:
            total = 0.5 * part[2 * i - 1] + part[2 * i] + 0.5 * part[2 * i + 1]
        totals.append(dot(down_y[...], all_terms(total)))
    for i, total in enumerate(totals):
        row = jnp.where(high_lanes, total[half:], total[:half])
        row = jnp.where(outside, 0.0, row)
        if i == 0:
            for k, term in enumerate(split(row, PARTS)):
                coarse[k] = term
        elif i == last:
            for k, term in enumerate(split(row, PARTS)):
                coarse[last + PARTS - 1 + k] = term
        else:
            coarse[i + PARTS - 1] = row.astype(BF)
    lines = next_a.shape[0] - coarse.shape[0] * half
    tail = count - lines // width
    far_tail = coarse.shape[0] - far_a.shape[0]
    for out, upward in ((next_a, up_x), (next_b, jnp.logical_not(up_x))):
        first = jnp.where(upward, tail, 0)
        for x in range(lines // width):
            out[x * width : (x + 1) * width, :] = near[first + x]
        for k in range(coarse.shape[0]):
            out[lines + k * half : lines + (k + 1) * half, :] = coarse[k]
    for out, upward in ((far_a, up_far), (far_b, jnp.logical_not(up_far))):
        first = jnp.where(upward, far_tail, 0)
        for k in range(far_a.shape[0]):
            out[k] = coarse[first + k]


def own_kernel(near, to_y, to_z, real, imag, ahead):
    count = real.shape[0]
    to_frequencies_y(lambda x: near[x], count, 8, to_y, ahead)
    to_frequencies_z(ahead, 4, to_z, real, imag)


def own_sum_kernel(real, imag, kr, kd, ks, from_z, from_y, out_real, out_imag, whole, back):
    count = real.shape[0]
    half = kr.shape[0] // 2
    along_x(
        lambda x, rows: real[x - half, rows, :],
        lambda x, rows: imag[x - half, rows, :],
        (kr, kd, ks),
        out_real,
        out_imag,
        BLOCK,
        None,
        lambda x: half <= x < half + count,
    )
    inner = slice(half, count - half)

    def write(x, value):
        whole[x] = value

    from_frequencies_z(out_real.at[inner], out_imag.at[inner], 4, from_z, back)
    from_frequencies_y(back, whole.shape[0], 8, from_y, write)


def final_kernel(
    t_columns,
    part_real,
    part_imag,
    whole,
    next_a,
    next_b,
    far_a,
    far_b,
    coarse,
    kr,
    kd,
    ks,
    to_y,
    to_z,
    from_z,
    from_y,
    mr,
    md,
    ms,
    m_to_y,
    m_to_z,
    m_from_z,
    m_from_y,
    tr,
    td,
    ts,
    t_down_y,
    t_down_z,
    t_to_y,
    t_to_z,
    t_from_z,
    t_from_y,
    out,
    side_real,
    side_imag,
    er,
    ei,
    ahead,
    back,
    mid,
    m_real,
    m_imag,
    m_er,
    m_ei,
    m_ahead,
    m_back,
    m_out,
    t_real,
    t_imag,
    t_er,
    t_ei,
    t_cells,
    t_ahead,
    t_back,
    t_out,
):
    left_x = lax.axis_size("gx") - lax.axis_index("gx")
    ended_x, close_x = left_x == 1, left_x <= 2
    ended_y = (lax.axis_index("gy") == lax.axis_size("gy") - 1).astype(jnp.int32)
    up_x, up_far = leads("gx", 1), leads("gx", 2)
    count = part_real.shape[0]
    width = to_y.shape[1] // 2
    reach = side_real.shape[0] // 2
    top_rows = left_x * (count // 4) + reach

    def from_left(at):
        return chosen(up_x, next_b[at, :], next_a[at, :])

    def from_right(at):
        return chosen(up_x, next_a[at, :], next_b[at, :])

    def far_left(k):
        return chosen(up_far, far_b[k], far_a[k])

    def far_right(k):
        return chosen(up_far, far_a[k], far_b[k])

    def side_cells(x):
        read, first = (from_left, x) if x < reach else (from_right, x - reach)
        return read(slice(first * width, (first + 1) * width))

    for first in range(0, 2 * reach, 2):
        xs = [first, first + 1]
        cells = jnp.concatenate([side_cells(x) for x in xs], 1)
        spread = dot(to_y[...], jnp.concatenate([cells, cells], 0))
        store_terms(ahead, first, to_y.shape[0], [spread[:, :LANES], spread[:, LANES:]])
    to_frequencies_z(ahead, 7, to_z, side_real, side_imag)

    def source(side):
        return lambda x, rows: side[x if x < reach else x - count, rows, :]

    edges = list(range(reach)) + list(range(count - reach, count))
    along_x(
        source(side_real),
        source(side_imag),
        (kr, kd, ks),
        er,
        ei,
        reach,
        edges,
        lambda x: x < reach or x >= reach + count,
        (part_real, part_imag),
    )
    from_frequencies_z(er, ei, 4, from_z, back)

    def fine_write(x, value):
        out[edges[x]] = value

    from_frequencies_y(back, len(edges), 8, from_y, fine_write)
    for x in range(whole.shape[0]):
        out[reach + x] = whole[x]

    half = mid.shape[1]
    last = count // 2
    lines = next_a.shape[0] - coarse.shape[0] * half

    def left_row(k):
        return from_left(slice(lines + k * half, lines + (k + 1) * half))

    def right_row(k):
        return from_right(slice(lines + k * half, lines + (k + 1) * half))

    def added(first, second, dropped=None):
        value = sum(first(PARTS - 1 - k).astype(F32) for k in range(PARTS))
        value = value + sum(second(last + 2 * PARTS - 2 - k).astype(F32) for k in range(PARTS))
        if dropped is not None:
            value = jnp.where(dropped, 0.0, value)
        return value.astype(BF)

    spare = far_a.shape[0] - PARTS
    far_first = coarse.shape[0] - far_a.shape[0]
    rows = [far_left(k) for k in range(spare)]
    rows += [added(left_row, lambda k: far_left(k - far_first))]
    rows += [left_row(k) for k in range(PARTS, last - 1 + PARTS)]
    rows += [added(lambda k: coarse[k], left_row)]
    rows += [coarse[k] for k in range(PARTS, last - 1 + PARTS)]
    rows += [added(right_row, lambda k: coarse[k], ended_x)]
    rows += [right_row(k) for k in range(PARTS, last - 1 + PARTS)]
    rows += [added(far_right, right_row, close_x)]
    rows += [far_right(k) for k in range(PARTS, PARTS + spare)]
    for k, row in enumerate(rows):
        mid[k] = row

    skip = (mid.shape[0] - m_real.shape[0]) // 2
    to_frequencies_y(lambda x: mid[x + skip], m_real.shape[0], 9, m_to_y, m_ahead, True)
    to_frequencies_z(m_ahead, 9, m_to_z, m_real, m_imag)

    t_width = t_cells.shape[1]
    spare = (t_width - t_columns) // 2
    inside = lax.broadcasted_iota(jnp.int32, (t_width, t_cells.shape[2]), 0)
    inside = inside < jnp.where(ended_y == 1, t_width - spare, t_width)

    def top_cells(xs, first):
        spreads = []
        for t in xs:
            total = 0.5 * mid[2 * t].astype(F32) + mid[2 * t + 1].astype(F32) + 0.5 * mid[2 * t + 2].astype(F32)
            spreads.append(dot(t_down_y[...], all_terms(total)))
        low = jnp.concatenate([spread[:t_width] for spread in spreads], 0)
        high = jnp.concatenate([spread[t_width:] for spread in spreads], 0)
        value = dot(jnp.concatenate(split(low, TERMS) + split(high, TERMS), 1), t_down_z[...])
        for k, t in enumerate(xs):
            row = jnp.where(inside, value[k * t_width : (k + 1) * t_width], 0.0)
            t_cells[t] = jnp.where(t < top_rows, row, 0.0).astype(BF)

    batches(t_real.shape[0], 7, top_cells)
    to_frequencies_y(lambda x: t_cells[x], t_real.shape[0], 7, t_to_y, t_ahead)
    to_frequencies_z(t_ahead, 7, t_to_z, t_real, t_imag)

    def plain(ref):
        return lambda x, rows: ref[x, rows, :]

    along_x(plain(m_real), plain(m_imag), (mr, md, ms), m_er, m_ei, 7)
    along_x(plain(t_real), plain(t_imag), (tr, td, ts), t_er, t_ei, 7)

    def top_write(x, value):
        t_out[x] = value

    def mid_write(x, value):
        m_out[x] = value

    from_frequencies_z(t_er, t_ei, 7, t_from_z, t_back)
    from_frequencies_z(m_er, m_ei, 7, m_from_z, m_back)
    from_frequencies_y(t_back, t_out.shape[0], 7, t_from_y.at[ended_y], top_write)
    from_frequencies_y(m_back, m_out.shape[0], 7, m_from_y.at[ended_y], mid_write)
    keep = jnp.where(ended_x, 0.0, 1.0)
    top = t_out.shape[0] - 1
    t_out[top] = t_out[top] * keep
    for i in range(top):
        m_out[2 * i] += t_out[i]
        m_out[2 * i + 1] += 0.5 * (t_out[i] + t_out[i + 1])
    m_out[2 * top] = (m_out[2 * top] + t_out[top]) * keep

    def finish(i):
        out[2 * i] += m_out[i]
        out[2 * i + 1] += 0.5 * (m_out[i] + m_out[i + 1])

    rows_loop(count // 2, 2, finish)


def call(kernel, outs, scratch, args, mib, loose=()):
    vmem = pl.BlockSpec(memory_space=pltpu.VMEM)
    return pl.pallas_call(
        kernel,
        out_shape=outs,
        in_specs=[
            pl.BlockSpec(memory_space=pl.ANY) if i in loose else vmem for i in range(len(args))
        ],
        out_specs=jax.tree.map(lambda _: vmem, outs),
        scratch_shapes=[pltpu.VMEM(shape, dtype) for dtype, shape in scratch],
        compiler_params=pltpu.CompilerParams(vmem_limit_bytes=mib << 20),
    )(*args)


def level_scratch(level, ny, nz, lanes, extra=()):
    rows = [
        (F32, (count, level.rows, LANES))
        for count in (level.in_x, level.in_x, level.out_x, level.out_x)
    ]
    terms = [
        (BF, (2, level.in_x * 2 * level.freq, lanes)),
        (BF, (2, level.out_x * 2 * level.freq, nz)),
    ]
    return [*rows, *extra, *terms, (F32, (level.out_x, ny, nz))]


def leads(axis, by):
    return lax.rem(lax.div(lax.axis_index(axis), by), 2) == 0


def swapped(first, second, axis, by):
    length = lax.axis_size(axis)
    outs = []
    for value, turn in ((first, 0), (second, 1)):
        up = [i for i in range(length - by) if i // by % 2 == turn]
        pairs = [(i, i + by) for i in up] + [(i + by, i) for i in up]
        outs.append(lax.ppermute(value, axis, pairs))
    return outs


def block(charges, kernel_fine, kernel_mid, kernel_top):
    nx, ny, nz = charges.shape
    taps = kernel_fine.shape[0]
    half = taps // 2
    wide = half + 1

    ident = np.eye(ny)
    width = ny + 2 * wide
    fine = Level(taps, nx, ny, wide, width, nz, ident, ident, np.eye(nz))
    my, mz = ny // 2, nz // 2
    to_fine = up(my)
    ended = np.diag([1.0] * my + [0.0])
    mid = Level(
        taps, nx // 2 + 1, my + 1, ny // 4, ny, mz, to_fine, to_fine @ ended, up_closed(mz)
    )
    ty, tz = my // 2, mz // 2
    to_mid = np.concatenate([up(ty), np.eye(ty + 1)[-1:]], 0)
    top_ended = np.diag([1.0] * ty + [0.0])
    top = Level(
        taps,
        nx // 4 + 1,
        ty + 1,
        wide,
        ty + 2 * wide,
        tz,
        to_fine @ to_mid,
        to_fine @ to_mid @ top_ended,
        up_closed(mz) @ up_closed(tz),
    )

    levels = (fine, mid, top)
    outs = [
        jax.ShapeDtypeStruct((taps, level.rows, LANES), F32)
        for level in levels
        for _ in range(3)
    ]
    table = np.concatenate([level.kernel_z for level in levels], 1)
    sizes = []
    for level, other in ((fine, None), (mid, None), (top, mid)):
        rows, columns = level.kernel_y.shape[0], level.kernel_z.shape[1]
        row, lane = 48 + (other.kernel_y.shape[0] if other else 0), 0 if level is fine else LANES
        assert row + rows <= LANES
        table[row : row + rows, lane : lane + 32] = level.kernel_y
        sizes.append((rows, columns, row, lane))
    spectra = call(
        functools.partial(spectra_kernel, sizes),
        outs,
        [(F32, (taps, 16, LANES)), (BF, (taps * 2 * fine.freq, LANES))],
        [jnp.stack([kernel_fine, kernel_mid, kernel_top]), table],
        8,
    )

    side = ny // 2
    up_y = leads("gy", 1)
    got_a, got_b = swapped(
        *(
            lax.dynamic_slice_in_dim(charges, jnp.where(flag, side, 0), side, 1).astype(BF)
            for flag in (up_y, jnp.logical_not(up_y))
        ),
        "gy",
        1,
    )

    window = side + ny // 2 + 16
    packed = ny // 2
    down_z = np.concatenate([np.pad(down(mz, 0, nz).T, ((0, 0), (at, mz - at))) for at in (0, mz)], 0)
    shift = ny + 2 * side - window
    down_y = np.concatenate([down(packed, 0, window), down(packed, 2 * packed - shift, window)], 0)
    mx = nx // 2
    lines = mx - 1 + 2 * PARTS
    reach = 2 * half + 1 - mx
    assert 0 < reach <= mx - 1 and 2 * mz == LANES == nz
    shapes = [
        (nx, width, LANES),
        (lines, packed, LANES),
        (half * width + lines * packed, LANES),
        (half * width + lines * packed, LANES),
        (reach + PARTS, packed, LANES),
        (reach + PARTS, packed, LANES),
    ]
    near, coarse, next_a, next_b, far_a, far_b = call(
        pack_kernel,
        [jax.ShapeDtypeStruct(shape, BF) for shape in shapes],
        [(F32, (nx, window, LANES))],
        [
            charges,
            got_a,
            got_b,
            down_z.astype(BF),
            np.tile(down_y, (1, TERMS)).astype(BF),
            spectra[0],
        ],
        8,
        loose=(5,),
    )
    far_a, far_b = swapped(far_a, far_b, "gx", 2)
    next_a, next_b = swapped(next_a, next_b, "gx", 1)

    spectrum = [jax.ShapeDtypeStruct((nx, fine.rows, LANES), F32)] * 2
    own = call(
        own_kernel,
        spectrum,
        [(BF, (2, nx * 2 * fine.freq, nz))],
        [near, fine.to_y, fine.to_z],
        10,
    )
    inner = nx - 2 * half
    own = call(
        own_sum_kernel,
        [*spectrum, jax.ShapeDtypeStruct((inner, ny, nz), F32)],
        [(BF, (2, inner * 2 * fine.freq, nz))],
        [*own, *spectra[:3], fine.from_z, fine.from_y[0]],
        10,
    )

    wide_top = ty + 2 * wide
    t_down_y = down(wide_top, 0, 2 * packed)
    t_down_y = np.concatenate([t_down_y[:, :packed], t_down_y[:, packed:]], 0)
    t_down_z = np.concatenate(
        [np.tile(table, (TERMS, 1)) for table in both_sides(down(tz, 0, mz).T)], 0
    )
    return call(
        functools.partial(final_kernel, ty),
        jax.ShapeDtypeStruct((nx, ny, nz), F32),
        [
            (F32, (2 * half, fine.rows, LANES)),
            (F32, (2 * half, fine.rows, LANES)),
            (F32, (2 * half, fine.rows, LANES)),
            (F32, (2 * half, fine.rows, LANES)),
            (BF, (2, 2 * half * 2 * fine.freq, nz)),
            (BF, (2, 2 * half * 2 * fine.freq, nz)),
            (BF, (3 * mx + 1 + 2 * reach, packed, LANES)),
            *level_scratch(mid, ny, nz, LANES),
            *level_scratch(top, ny, nz, tz, [(BF, (top.in_x, wide_top, tz))]),
        ],
        [
            *own,
            next_a,
            next_b,
            far_a,
            far_b,
            coarse,
            *spectra[:3],
            fine.to_y,
            fine.to_z,
            fine.from_z,
            fine.from_y[0],
            *spectra[3:6],
            np.concatenate([np.concatenate(two(mid.table_y[:, at : at + packed]), 1) for at in (0, packed)], 0),
            terms_below(np.tile(mid.table_z, (2, 1))),
            mid.from_z,
            np.stack(mid.from_y),
            *spectra[6:],
            np.tile(t_down_y, (1, TERMS)).astype(BF),
            t_down_z.astype(BF),
            top.to_y,
            top.to_z,
            top.from_z,
            np.stack(top.from_y),
        ],
        26,
    )


def solution(mesh):
    placed = (P("gx", "gy", None), P(), P(), P())
    return jax.shard_map(
        block, mesh=mesh, in_specs=placed, out_specs=P("gx", "gy", None), check_vma=False
    )
```

```python
import functools

import jax
import jax.numpy as jnp
import numpy as np
from jax import lax
from jax.experimental import pallas as pl
from jax.experimental.pallas import tpu as pltpu
from jax.sharding import PartitionSpec as P

BF = jnp.bfloat16
F32 = jnp.float32
LANES = 128
BLOCK = 8
PARTS = 2
TERMS = 3


def two(matrix):
    high = np.asarray(matrix, np.float64).astype(BF)
    low = (matrix - high.astype(np.float64)).astype(BF)
    return high, low


def three_terms(matrix):
    high, low = two(matrix)
    return np.concatenate([high, high, low], 1)


def terms_below(matrix):
    high, low = two(matrix)
    return np.concatenate([high, high, low], 0)


def up(count):
    out = np.zeros((2 * count, count + 1))
    for i in range(count):
        out[2 * i, i] = 1.0
        out[2 * i + 1, i] = out[2 * i + 1, i + 1] = 0.5
    return out


def up_closed(count):
    return up(count)[:, :count]


def both_sides(table):
    size = table.shape[0]
    return [np.pad(table, ((at, LANES - size - at), (0, 0))) for at in (0, LANES - size)]


class Level:
    def __init__(self, taps, out_x, out_y, shift, window, size_z, rows_y, rows_y_end, cols_z):
        half = taps // 2
        self.taps, self.out_x, self.in_x = taps, out_x, out_x + taps - 1
        period_y = out_y + 2 * half + (out_y + 1) % 2
        period_z = size_z + half
        self.freq = (period_y + 1) // 2
        self.main = min(LANES, period_z)
        self.left = period_z - self.main
        assert self.freq % 8 == 0 and self.left <= 8 and self.freq <= LANES
        self.rows = self.freq + (8 if self.left else 0)
        turn_z, turn_y = 2 * np.pi / period_z, 2 * np.pi / period_y
        freq_y, freq_z = np.arange(self.freq), np.arange(period_z)

        cells = np.arange(window)
        needed = (cells >= shift - half) & (cells < shift + out_y + half)
        angle = turn_y * np.outer(freq_y, cells)
        self.table_y = np.concatenate([np.cos(angle), -np.sin(angle)], 0) * needed
        self.to_y = np.concatenate(two(self.table_y), 1)
        self.table_z = self.columns(turn_z * np.outer(np.arange(size_z), freq_z))
        self.to_z = terms_below(self.table_z)

        offsets = np.arange(taps) - half
        angle = turn_y * np.outer(freq_y, offsets)
        table = np.zeros((2 * self.freq, 16))
        table[:, :taps] = np.concatenate([np.cos(angle), np.sin(angle)], 0)
        self.kernel_y = np.concatenate(two(table), 1)
        table = self.columns(turn_z * np.outer(offsets, freq_z))
        table = terms_below(np.pad(table, ((0, 16 - taps), (0, 0))))
        self.kernel_z = np.pad(table, ((0, LANES - 48), (0, 0)))

        angle = turn_z * np.outer(freq_z, np.arange(size_z))
        table = np.concatenate([np.cos(angle) @ cols_z.T, np.sin(angle) @ cols_z.T], 1) / period_z
        lanes = np.zeros((LANES * (2 if self.left else 1), table.shape[1]))
        lanes[: self.main] = table[: self.main]
        if self.left:
            for group in range(self.freq // 8):
                at = LANES + 8 * group
                lanes[at : at + self.left] = table[self.main :]
        self.from_z = terms_below(lanes)
        weight = np.where(freq_y == 0, 1.0, 2.0) / period_y
        angle = turn_y * np.outer(np.arange(out_y) + shift, freq_y)
        wave = np.concatenate([weight * np.cos(angle), -weight * np.sin(angle)], 1)
        self.from_y = [three_terms(rows @ wave) for rows in (rows_y, rows_y_end)]

    def columns(self, angle):
        out = []
        for start, stop in ((0, self.main), (self.main, self.main + self.left)):
            for wave in (np.cos(angle[:, start:stop]), np.sin(angle[:, start:stop])):
                table = np.zeros((angle.shape[0], LANES))
                for group in range(1 if start == 0 else self.freq // 8):
                    table[:, 8 * group : 8 * group + stop - start] = wave
                out.append(table)
            if not self.left:
                break
        return np.concatenate(out, 1)


def down(count, first, length):
    out = np.zeros((count, length))
    for j in range(count):
        for a, w in ((-1, 0.5), (0, 1.0), (1, 0.5)):
            if 0 <= first + 2 * j + a < length:
                out[j, first + 2 * j + a] = w
    return out


def dot(a, b):
    return jnp.dot(a, b, preferred_element_type=F32)


def split(value, terms):
    out = []
    for _ in range(terms - 1):
        out.append(value.astype(BF))
        value = value - out[-1].astype(F32)
    return out + [value.astype(BF)]


def side_by_side(value):
    high, low = split(value, 2)
    return jnp.concatenate([high, low, high], 1)


def fold(value):
    groups = value.shape[0] // 8
    lane = lax.broadcasted_iota(jnp.int32, (8, LANES), 1)
    out = value[8 * (groups - 1) :]
    for group in range(groups - 2, -1, -1):
        out = jnp.where(lane < 8 * (group + 1), value[8 * group : 8 * (group + 1)], out)
    return out


def unfold(value, groups):
    lane = lax.broadcasted_iota(jnp.int32, (8, LANES), 1)
    return jnp.concatenate(
        [
            jnp.where((lane >= 8 * group) & (lane < 8 * (group + 1)), value, 0.0)
            for group in range(groups)
        ],
        0,
    )


def joined(spread, sign):
    freq = spread.shape[0] // 2
    outs = []
    for at in range(0, spread.shape[1], 2 * LANES):
        rc, rs = spread[:freq, at : at + LANES], spread[:freq, at + LANES : at + 2 * LANES]
        ic, js = spread[freq:, at : at + LANES], spread[freq:, at + LANES : at + 2 * LANES]
        if at:
            rc, rs, ic, js = fold(rc), fold(rs), fold(ic), fold(js)
        outs.append((rc + js, ic - rs) if sign > 0 else (rc - js, ic + rs))
    return [jnp.concatenate([out[k] for out in outs], 0) for k in range(2)]


def batches(count, size, body):
    for first in range(0, count, size):
        body(list(range(first, min(count, first + size))), first)


def rows_at(first, period, count):
    return pl.ds(first * period if isinstance(first, int) else pl.multiple_of(first * period, 16), count * period)


def store_terms(terms, first, rows, values):
    high, low = split(jnp.concatenate(values, 0), 2)
    terms[0, rows_at(first, rows, len(values)), :] = high
    terms[1, rows_at(first, rows, len(values)), :] = low


def to_frequencies_y(read, count, size, to_y, terms, packed=False):
    rows = terms.shape[1] // count

    def body(xs, first):
        values = []
        for k in range(0, len(xs), 2):
            cells = [read(x) for x in xs[k : k + 2]]
            width = cells[0].shape[1]
            if width % LANES == 0:
                cells = [jnp.concatenate(cells, 1)]
            for part in cells:
                spread = dot(to_y[...], jnp.concatenate([part, part], 0))
                for at in range(0, spread.shape[1], width):
                    value = spread[:, at : at + width]
                    if packed:
                        low_lanes = lax.broadcasted_iota(jnp.int32, (rows, LANES), 1) < LANES // 2
                        value = jnp.where(low_lanes, value[:rows], value[rows:])
                    values.append(value)
        store_terms(terms, first, rows, values)

    batches(count, size, body)


def to_frequencies_z(terms, size, to_z, real, imag):
    count = real.shape[0]
    rows = terms.shape[1] // count

    def body(xs, first):
        span = rows_at(first, rows, len(xs))
        high, low = terms[0, span, :], terms[1, span, :]
        width = high.shape[1]
        if width % LANES == 0:
            spread = dot(jnp.concatenate([high, low, high], 1), to_z[...])
        else:
            spread = dot(high, to_z[:width]) + dot(low, to_z[width : 2 * width])
            spread = spread + dot(high, to_z[2 * width :])
        for k, x in enumerate(xs):
            real[x], imag[x] = joined(spread[k * rows : (k + 1) * rows], 1)

    batches(count, size, body)


def from_frequencies_z(real, imag, size, from_z, terms):
    count = real.shape[0]
    rows = terms.shape[1] // count
    freq = rows // 2

    def body(xs, first):
        lines = []
        for x in xs:
            for ref in (real, imag):
                value = ref[x]
                main = value[:freq]
                if value.shape[0] > freq:
                    main = jnp.concatenate([main, unfold(value[freq:], freq // 8)], 1)
                lines.append(main)
        spread = dot(side_by_side(jnp.concatenate(lines, 0)), from_z[...])
        half = spread.shape[1] // 2
        values = []
        for k in range(len(xs)):
            r = spread[k * rows : k * rows + freq]
            i = spread[k * rows + freq : (k + 1) * rows]
            values += [r[:, :half] - i[:, half:], r[:, half:] + i[:, :half]]
        high, low = split(jnp.concatenate(values, 0), 2)
        terms[0, rows_at(first, rows, len(xs)), :] = high
        terms[1, rows_at(first, rows, len(xs)), :] = low

    batches(count, size, body)


def from_frequencies_y(terms, count, size, from_y, write):
    rows = terms.shape[1] // count

    def body(xs, first):
        for k in range(0, len(xs), 2):
            parts = []
            for x in xs[k : k + 2]:
                span = rows_at(x, rows, 1)
                high, low = terms[0, span, :], terms[1, span, :]
                parts.append(jnp.concatenate([high, low, high], 0))
            value = dot(from_y[...], jnp.concatenate(parts, 1))
            width = parts[0].shape[1]
            for j, x in enumerate(xs[k : k + 2]):
                write(x, value[:, j * width : (j + 1) * width])

    batches(count, size, body)


def along_x(real, imag, spectrum, out_real, out_imag, block, outputs=None, taken=None, before=None):
    kernel_r, kernel_d, kernel_s = spectrum
    taps, period = kernel_r.shape[:2]
    outputs = outputs or list(range(out_real.shape[0]))
    taken = taken or (lambda x: True)

    def body(part):
        rows = slice(8 * part, 8 * part + 8)
        for start in range(0, len(outputs), block):
            wanted = outputs[start : start + block]
            sums = [[None] * 3 for _ in wanted]
            seen = {}
            for a in range(taps):
                used = [i for i, out in enumerate(wanted) if taken(out + a)]
                if used:
                    weights = kernel_r[a, rows, :], kernel_d[a, rows, :], kernel_s[a, rows, :]
                for i in used:
                    x = wanted[i] + a
                    if x not in seen:
                        r, m = real(x, rows), imag(x, rows)
                        seen[x] = r + m, r, m
                    for k in range(3):
                        term = weights[k] * seen[x][k]
                        sums[i][k] = term if sums[i][k] is None else sums[i][k] + term
            for i, out in enumerate(wanted):
                value = sums[i][0] - sums[i][2], sums[i][0] + sums[i][1]
                if before is not None:
                    value = value[0] + before[0][out, rows, :], value[1] + before[1][out, rows, :]
                out_real[start + i, rows, :] = value[0]
                out_imag[start + i, rows, :] = value[1]

    for part in range(period // 8):
        body(part)


def rows_loop(count, step, body):
    def trip(i, _):
        for k in range(step):
            body(i * step + k)
        return 0

    lax.fori_loop(0, count // step, trip, 0)
    for x in range(count - count % step, count):
        body(x)


def all_terms(value):
    return jnp.concatenate(split(value, TERMS), 0)


def spectra_kernel(sizes, *refs):
    kernels, table, outs, (padded, lines) = refs[0], refs[1], refs[2:-2], refs[-2:]
    levels, taps = kernels.shape[:2]
    padded[...] = jnp.zeros(padded.shape, padded.dtype)
    at_z = 0
    for level in range(levels):
        outs_here = outs[3 * level : 3 * level + 3]
        rows, columns, row, lane = sizes[level]
        kernel_y = table[row : row + rows, lane : lane + 32]
        kernel_z = table[:, at_z : at_z + columns]
        at_z += columns
        for at in (0, 16, 32):
            padded[:, :taps, at : at + taps] = kernels[level].astype(F32)
        cells = jnp.concatenate([padded[a].astype(BF) for a in range(taps)], 1)
        spread = dot(kernel_y, jnp.concatenate([cells, cells], 0))
        lane = lax.broadcasted_iota(jnp.int32, (rows, LANES), 1)
        middle = (lane >= 16) & (lane < 32)
        for a in range(taps):
            high, low = (term.astype(F32) for term in split(spread[:, a * LANES : (a + 1) * LANES], 2))
            lines[a * rows : (a + 1) * rows, :] = jnp.where(middle, low, high).astype(BF)

        def body(xs, first, rows=rows, kernel_z=kernel_z, outs=outs_here):
            spread = dot(lines[rows_at(first, rows, len(xs)), :], kernel_z)
            for k, a in enumerate(xs):
                real, imag = joined(spread[k * rows : (k + 1) * rows], -1)
                outs[0][a] = real
                outs[1][a] = imag - real
                outs[2][a] = imag + real

        batches(taps, 5, body)


def chosen(flag, first, second):
    return jnp.where(flag, first, second)


def pack_kernel(
    own, got_a, got_b, down_z, down_y, ordered, near, coarse, next_a, next_b, far_a, far_b, part
):
    count, size = own.shape[:2]
    side = got_a.shape[1]
    up_y, up_x, up_far = leads("gy", 1), leads("gx", 1), leads("gx", 2)
    ended = lax.axis_index("gy") == lax.axis_size("gy") - 1
    width = near.shape[1]
    start = side - (width - size) // 2
    window = part.shape[1]

    def body(xs, first):
        rows = []
        for x in xs:
            a, b, o = got_a[x], got_b[x], own[x].astype(BF)
            l, r = chosen(up_y, b, a), chosen(up_y, a, b)
            near[x] = jnp.concatenate([l[start:], o, r[: side - start]], 0)
            low = jnp.concatenate([l, o[: window - side]], 0)
            high = jnp.concatenate([o[size + side - window :], r], 0)
            rows.append(jnp.concatenate([low, high], 1))
        value = dot(jnp.concatenate(rows, 0), down_z[...])
        for k, x in enumerate(xs):
            part[x] = value[k * window : (k + 1) * window]

    batches(count, 4, body)
    half = down_y.shape[0] // 2
    shape = (half, LANES)
    high_lanes = lax.broadcasted_iota(jnp.int32, shape, 1) >= LANES // 2
    outside = high_lanes & (lax.broadcasted_iota(jnp.int32, shape, 0) >= half // 2)
    outside = outside & ended
    last = count // 2
    totals = []
    for i in range(last + 1):
        if i == 0:
            total = part[0] + 0.5 * part[1]
        elif i == last:
            total = 0.5 * part[count - 1]
        else:
            total = 0.5 * part[2 * i - 1] + part[2 * i] + 0.5 * part[2 * i + 1]
        totals.append(dot(down_y[...], all_terms(total)))
    for i, total in enumerate(totals):
        row = jnp.where(high_lanes, total[half:], total[:half])
        row = jnp.where(outside, 0.0, row)
        if i == 0:
            for k, term in enumerate(split(row, PARTS)):
                coarse[k] = term
        elif i == last:
            for k, term in enumerate(split(row, PARTS)):
                coarse[last + PARTS - 1 + k] = term
        else:
            coarse[i + PARTS - 1] = row.astype(BF)
    lines = next_a.shape[0] - coarse.shape[0] * half
    tail = count - lines // width
    far_tail = coarse.shape[0] - far_a.shape[0]
    for out, upward in ((next_a, up_x), (next_b, jnp.logical_not(up_x))):
        first = jnp.where(upward, tail, 0)
        for x in range(lines // width):
            out[x * width : (x + 1) * width, :] = near[first + x]
        for k in range(coarse.shape[0]):
            out[lines + k * half : lines + (k + 1) * half, :] = coarse[k]
    for out, upward in ((far_a, up_far), (far_b, jnp.logical_not(up_far))):
        first = jnp.where(upward, far_tail, 0)
        for k in range(far_a.shape[0]):
            out[k] = coarse[first + k]


def own_kernel(near, to_y, to_z, real, imag, ahead):
    count = real.shape[0]
    to_frequencies_y(lambda x: near[x], count, 8, to_y, ahead)
    to_frequencies_z(ahead, 4, to_z, real, imag)


def own_sum_kernel(
    real,
    imag,
    coarse,
    kr,
    kd,
    ks,
    from_z,
    from_y,
    mr,
    md,
    ms,
    m_to_y,
    m_to_z,
    out_real,
    out_imag,
    whole,
    m_part_real,
    m_part_imag,
    back,
    m_real,
    m_imag,
    m_ahead,
):
    count = real.shape[0]
    half = kr.shape[0] // 2
    along_x(
        lambda x, rows: real[x - half, rows, :],
        lambda x, rows: imag[x - half, rows, :],
        (kr, kd, ks),
        out_real,
        out_imag,
        BLOCK,
        None,
        lambda x: half <= x < half + count,
    )
    lines = m_real.shape[0]
    first = half + 1
    to_frequencies_y(lambda k: coarse[k + PARTS], lines, 6, m_to_y, m_ahead, True)
    to_frequencies_z(m_ahead, 6, m_to_z, m_real, m_imag)
    along_x(
        lambda x, rows: m_real[x - first, rows, :],
        lambda x, rows: m_imag[x - first, rows, :],
        (mr, md, ms),
        m_part_real,
        m_part_imag,
        7,
        None,
        lambda x: first <= x < first + lines,
    )
    inner = slice(half, count - half)

    def write(x, value):
        whole[x] = value

    from_frequencies_z(out_real.at[inner], out_imag.at[inner], 4, from_z, back)
    from_frequencies_y(back, whole.shape[0], 8, from_y, write)


def final_kernel(
    t_columns,
    part_real,
    part_imag,
    whole,
    m_part_real,
    m_part_imag,
    next_a,
    next_b,
    far_a,
    far_b,
    coarse,
    kr,
    kd,
    ks,
    to_y,
    to_z,
    from_z,
    from_y,
    mr,
    md,
    ms,
    m_to_y,
    m_to_z,
    m_from_z,
    m_from_y,
    tr,
    td,
    ts,
    t_down_y,
    t_down_z,
    t_to_y,
    t_to_z,
    t_from_z,
    t_from_y,
    out,
    side_real,
    side_imag,
    er,
    ei,
    ahead,
    back,
    mid,
    m_real,
    m_imag,
    m_er,
    m_ei,
    m_ahead,
    m_back,
    m_out,
    t_real,
    t_imag,
    t_er,
    t_ei,
    t_cells,
    t_ahead,
    t_back,
    t_out,
):
    left_x = lax.axis_size("gx") - lax.axis_index("gx")
    ended_x, close_x = left_x == 1, left_x <= 2
    ended_y = (lax.axis_index("gy") == lax.axis_size("gy") - 1).astype(jnp.int32)
    up_x, up_far = leads("gx", 1), leads("gx", 2)
    count = part_real.shape[0]
    width = to_y.shape[1] // 2
    reach = side_real.shape[0] // 2
    top_rows = left_x * (count // 4) + reach

    def from_left(at):
        return chosen(up_x, next_b[at, :], next_a[at, :])

    def from_right(at):
        return chosen(up_x, next_a[at, :], next_b[at, :])

    def far_left(k):
        return chosen(up_far, far_b[k], far_a[k])

    def far_right(k):
        return chosen(up_far, far_a[k], far_b[k])

    def side_cells(x):
        read, first = (from_left, x) if x < reach else (from_right, x - reach)
        return read(slice(first * width, (first + 1) * width))

    for first in range(0, 2 * reach, 2):
        xs = [first, first + 1]
        cells = jnp.concatenate([side_cells(x) for x in xs], 1)
        spread = dot(to_y[...], jnp.concatenate([cells, cells], 0))
        store_terms(ahead, first, to_y.shape[0], [spread[:, :LANES], spread[:, LANES:]])
    to_frequencies_z(ahead, 7, to_z, side_real, side_imag)

    def source(side):
        return lambda x, rows: side[x if x < reach else x - count, rows, :]

    edges = list(range(reach)) + list(range(count - reach, count))
    along_x(
        source(side_real),
        source(side_imag),
        (kr, kd, ks),
        er,
        ei,
        reach,
        edges,
        lambda x: x < reach or x >= reach + count,
        (part_real, part_imag),
    )
    from_frequencies_z(er, ei, 4, from_z, back)

    def fine_write(x, value):
        out[edges[x]] = value

    from_frequencies_y(back, len(edges), 8, from_y, fine_write)
    for x in range(whole.shape[0]):
        out[reach + x] = whole[x]

    half = mid.shape[1]
    last = count // 2
    lines = next_a.shape[0] - coarse.shape[0] * half

    def left_row(k):
        return from_left(slice(lines + k * half, lines + (k + 1) * half))

    def right_row(k):
        return from_right(slice(lines + k * half, lines + (k + 1) * half))

    def added(first, second, dropped=None):
        value = sum(first(PARTS - 1 - k).astype(F32) for k in range(PARTS))
        value = value + sum(second(last + 2 * PARTS - 2 - k).astype(F32) for k in range(PARTS))
        if dropped is not None:
            value = jnp.where(dropped, 0.0, value)
        return value.astype(BF)

    spare = far_a.shape[0] - PARTS
    far_first = coarse.shape[0] - far_a.shape[0]
    rows = [far_left(k) for k in range(spare)]
    rows += [added(left_row, lambda k: far_left(k - far_first))]
    rows += [left_row(k) for k in range(PARTS, last - 1 + PARTS)]
    rows += [added(lambda k: coarse[k], left_row)]
    rows += [coarse[k] for k in range(PARTS, last - 1 + PARTS)]
    rows += [added(right_row, lambda k: coarse[k], ended_x)]
    rows += [right_row(k) for k in range(PARTS, last - 1 + PARTS)]
    rows += [added(far_right, right_row, close_x)]
    rows += [far_right(k) for k in range(PARTS, PARTS + spare)]
    for k, row in enumerate(rows):
        mid[k] = row

    own_lines = last - 1
    m_rows = m_real.shape[0] + own_lines
    skip = (mid.shape[0] - m_rows) // 2
    sides = [x for x in range(m_rows) if not reach < x <= reach + own_lines]
    to_frequencies_y(lambda k: mid[sides[k] + skip], len(sides), 8, m_to_y, m_ahead, True)
    to_frequencies_z(m_ahead, 8, m_to_z, m_real, m_imag)

    t_width = t_cells.shape[1]
    spare = (t_width - t_columns) // 2
    inside = lax.broadcasted_iota(jnp.int32, (t_width, t_cells.shape[2]), 0)
    inside = inside < jnp.where(ended_y == 1, t_width - spare, t_width)

    def top_cells(xs, first):
        spreads = []
        for t in xs:
            total = 0.5 * mid[2 * t].astype(F32) + mid[2 * t + 1].astype(F32) + 0.5 * mid[2 * t + 2].astype(F32)
            spreads.append(dot(t_down_y[...], all_terms(total)))
        low = jnp.concatenate([spread[:t_width] for spread in spreads], 0)
        high = jnp.concatenate([spread[t_width:] for spread in spreads], 0)
        value = dot(jnp.concatenate(split(low, TERMS) + split(high, TERMS), 1), t_down_z[...])
        for k, t in enumerate(xs):
            row = jnp.where(inside, value[k * t_width : (k + 1) * t_width], 0.0)
            t_cells[t] = jnp.where(t < top_rows, row, 0.0).astype(BF)

    batches(t_real.shape[0], 7, top_cells)
    to_frequencies_y(lambda x: t_cells[x], t_real.shape[0], 7, t_to_y, t_ahead)
    to_frequencies_z(t_ahead, 7, t_to_z, t_real, t_imag)

    def plain(ref):
        return lambda x, rows: ref[x, rows, :]

    along_x(
        lambda x, rows: m_real[sides.index(x), rows, :],
        lambda x, rows: m_imag[sides.index(x), rows, :],
        (mr, md, ms),
        m_er,
        m_ei,
        7,
        None,
        lambda x: x in sides,
        (m_part_real, m_part_imag),
    )
    along_x(plain(t_real), plain(t_imag), (tr, td, ts), t_er, t_ei, 7)

    def top_write(x, value):
        t_out[x] = value

    def mid_write(x, value):
        m_out[x] = value

    from_frequencies_z(t_er, t_ei, 7, t_from_z, t_back)
    from_frequencies_z(m_er, m_ei, 7, m_from_z, m_back)
    from_frequencies_y(t_back, t_out.shape[0], 7, t_from_y.at[ended_y], top_write)
    from_frequencies_y(m_back, m_out.shape[0], 7, m_from_y.at[ended_y], mid_write)
    keep = jnp.where(ended_x, 0.0, 1.0)
    top = t_out.shape[0] - 1
    t_out[top] = t_out[top] * keep
    for i in range(top):
        m_out[2 * i] += t_out[i]
        m_out[2 * i + 1] += 0.5 * (t_out[i] + t_out[i + 1])
    m_out[2 * top] = (m_out[2 * top] + t_out[top]) * keep

    def finish(i):
        out[2 * i] += m_out[i]
        out[2 * i + 1] += 0.5 * (m_out[i] + m_out[i + 1])

    rows_loop(count // 2, 2, finish)


def call(kernel, outs, scratch, args, mib, loose=()):
    vmem = pl.BlockSpec(memory_space=pltpu.VMEM)
    return pl.pallas_call(
        kernel,
        out_shape=outs,
        in_specs=[
            pl.BlockSpec(memory_space=pl.ANY) if i in loose else vmem for i in range(len(args))
        ],
        out_specs=jax.tree.map(lambda _: vmem, outs),
        scratch_shapes=[pltpu.VMEM(shape, dtype) for dtype, shape in scratch],
        compiler_params=pltpu.CompilerParams(vmem_limit_bytes=mib << 20),
    )(*args)


def level_scratch(level, in_x, ny, nz, lanes, extra=()):
    rows = [
        (F32, (count, level.rows, LANES))
        for count in (in_x, in_x, level.out_x, level.out_x)
    ]
    terms = [
        (BF, (2, in_x * 2 * level.freq, lanes)),
        (BF, (2, level.out_x * 2 * level.freq, nz)),
    ]
    return [*rows, *extra, *terms, (F32, (level.out_x, ny, nz))]


def leads(axis, by):
    return lax.rem(lax.div(lax.axis_index(axis), by), 2) == 0


def swapped(first, second, axis, by):
    length = lax.axis_size(axis)
    outs = []
    for value, turn in ((first, 0), (second, 1)):
        up = [i for i in range(length - by) if i // by % 2 == turn]
        pairs = [(i, i + by) for i in up] + [(i + by, i) for i in up]
        outs.append(lax.ppermute(value, axis, pairs))
    return outs


def block(charges, kernel_fine, kernel_mid, kernel_top):
    nx, ny, nz = charges.shape
    taps = kernel_fine.shape[0]
    half = taps // 2
    wide = half + 1

    ident = np.eye(ny)
    width = ny + 2 * wide
    fine = Level(taps, nx, ny, wide, width, nz, ident, ident, np.eye(nz))
    my, mz = ny // 2, nz // 2
    to_fine = up(my)
    ended = np.diag([1.0] * my + [0.0])
    mid = Level(
        taps, nx // 2 + 1, my + 1, ny // 4, ny, mz, to_fine, to_fine @ ended, up_closed(mz)
    )
    ty, tz = my // 2, mz // 2
    to_mid = np.concatenate([up(ty), np.eye(ty + 1)[-1:]], 0)
    top_ended = np.diag([1.0] * ty + [0.0])
    top = Level(
        taps,
        nx // 4 + 1,
        ty + 1,
        wide,
        ty + 2 * wide,
        tz,
        to_fine @ to_mid,
        to_fine @ to_mid @ top_ended,
        up_closed(mz) @ up_closed(tz),
    )

    levels = (fine, mid, top)
    outs = [
        jax.ShapeDtypeStruct((taps, level.rows, LANES), F32)
        for level in levels
        for _ in range(3)
    ]
    table = np.concatenate([level.kernel_z for level in levels], 1)
    sizes = []
    for level, other in ((fine, None), (mid, None), (top, mid)):
        rows, columns = level.kernel_y.shape[0], level.kernel_z.shape[1]
        row, lane = 48 + (other.kernel_y.shape[0] if other else 0), 0 if level is fine else LANES
        assert row + rows <= LANES
        table[row : row + rows, lane : lane + 32] = level.kernel_y
        sizes.append((rows, columns, row, lane))
    spectra = call(
        functools.partial(spectra_kernel, sizes),
        outs,
        [(F32, (taps, 16, LANES)), (BF, (taps * 2 * fine.freq, LANES))],
        [jnp.stack([kernel_fine, kernel_mid, kernel_top]), table],
        8,
    )

    side = ny // 2
    up_y = leads("gy", 1)
    got_a, got_b = swapped(
        *(
            lax.dynamic_slice_in_dim(charges, jnp.where(flag, side, 0), side, 1).astype(BF)
            for flag in (up_y, jnp.logical_not(up_y))
        ),
        "gy",
        1,
    )

    window = side + ny // 2 + 16
    packed = ny // 2
    down_z = np.concatenate([np.pad(down(mz, 0, nz).T, ((0, 0), (at, mz - at))) for at in (0, mz)], 0)
    shift = ny + 2 * side - window
    down_y = np.concatenate([down(packed, 0, window), down(packed, 2 * packed - shift, window)], 0)
    mx = nx // 2
    lines = mx - 1 + 2 * PARTS
    reach = 2 * half + 1 - mx
    assert 0 < reach <= mx - 1 and 2 * mz == LANES == nz
    shapes = [
        (nx, width, LANES),
        (lines, packed, LANES),
        (half * width + lines * packed, LANES),
        (half * width + lines * packed, LANES),
        (reach + PARTS, packed, LANES),
        (reach + PARTS, packed, LANES),
    ]
    near, coarse, next_a, next_b, far_a, far_b = call(
        pack_kernel,
        [jax.ShapeDtypeStruct(shape, BF) for shape in shapes],
        [(F32, (nx, window, LANES))],
        [
            charges,
            got_a,
            got_b,
            down_z.astype(BF),
            np.tile(down_y, (1, TERMS)).astype(BF),
            spectra[0],
        ],
        8,
        loose=(5,),
    )
    far_a, far_b = swapped(far_a, far_b, "gx", 2)
    next_a, next_b = swapped(next_a, next_b, "gx", 1)

    parts = [np.concatenate(two(mid.table_y[:, at : at + packed]), 1) for at in (0, packed)]
    mid_to_y = np.concatenate(parts, 0)
    mid_to_z = terms_below(np.tile(mid.table_z, (2, 1)))
    spectrum = [jax.ShapeDtypeStruct((nx, fine.rows, LANES), F32)] * 2
    own = call(
        own_kernel,
        spectrum,
        [(BF, (2, nx * 2 * fine.freq, nz))],
        [near, fine.to_y, fine.to_z],
        10,
    )
    inner = nx - 2 * half
    own = call(
        own_sum_kernel,
        [
            *spectrum,
            jax.ShapeDtypeStruct((inner, ny, nz), F32),
            *[jax.ShapeDtypeStruct((mid.out_x, mid.rows, LANES), F32)] * 2,
        ],
        [
            (BF, (2, inner * 2 * fine.freq, nz)),
            *[(F32, (mx - 1, mid.rows, LANES))] * 2,
            (BF, (2, (mx - 1) * 2 * mid.freq, LANES)),
        ],
        [
            *own,
            coarse,
            *spectra[:3],
            fine.from_z,
            fine.from_y[0],
            *spectra[3:6],
            mid_to_y,
            mid_to_z,
        ],
        10,
    )

    wide_top = ty + 2 * wide
    t_down_y = down(wide_top, 0, 2 * packed)
    t_down_y = np.concatenate([t_down_y[:, :packed], t_down_y[:, packed:]], 0)
    t_down_z = np.concatenate(
        [np.tile(table, (TERMS, 1)) for table in both_sides(down(tz, 0, mz).T)], 0
    )
    return call(
        functools.partial(final_kernel, ty),
        jax.ShapeDtypeStruct((nx, ny, nz), F32),
        [
            (F32, (2 * half, fine.rows, LANES)),
            (F32, (2 * half, fine.rows, LANES)),
            (F32, (2 * half, fine.rows, LANES)),
            (F32, (2 * half, fine.rows, LANES)),
            (BF, (2, 2 * half * 2 * fine.freq, nz)),
            (BF, (2, 2 * half * 2 * fine.freq, nz)),
            (BF, (3 * mx + 1 + 2 * reach, packed, LANES)),
            *level_scratch(mid, mid.in_x - mx + 1, ny, nz, LANES),
            *level_scratch(top, top.in_x, ny, nz, tz, [(BF, (top.in_x, wide_top, tz))]),
        ],
        [
            *own,
            next_a,
            next_b,
            far_a,
            far_b,
            coarse,
            *spectra[:3],
            fine.to_y,
            fine.to_z,
            fine.from_z,
            fine.from_y[0],
            *spectra[3:6],
            mid_to_y,
            mid_to_z,
            mid.from_z,
            np.stack(mid.from_y),
            *spectra[6:],
            np.tile(t_down_y, (1, TERMS)).astype(BF),
            t_down_z.astype(BF),
            top.to_y,
            top.to_z,
            top.from_z,
            np.stack(top.from_y),
        ],
        26,
    )


def solution(mesh):
    placed = (P("gx", "gy", None), P(), P(), P())
    return jax.shard_map(
        block, mesh=mesh, in_specs=placed, out_specs=P("gx", "gy", None), check_vma=False
    )
```

```python
import functools

import jax
import jax.numpy as jnp
import numpy as np
from jax import lax
from jax.experimental import pallas as pl
from jax.experimental.pallas import tpu as pltpu
from jax.sharding import PartitionSpec as P

BF = jnp.bfloat16
F32 = jnp.float32
LANES = 128
BLOCK = 8
PARTS = 2
TERMS = 2


def two(matrix):
    high = np.asarray(matrix, np.float64).astype(BF)
    low = (matrix - high.astype(np.float64)).astype(BF)
    return high, low


def three_terms(matrix):
    high, low = two(matrix)
    return np.concatenate([high, high, low], 1)


def terms_below(matrix):
    high, low = two(matrix)
    return np.concatenate([high, high, low], 0)


def up(count):
    out = np.zeros((2 * count, count + 1))
    for i in range(count):
        out[2 * i, i] = 1.0
        out[2 * i + 1, i] = out[2 * i + 1, i + 1] = 0.5
    return out


def up_closed(count):
    return up(count)[:, :count]


def both_sides(table):
    size = table.shape[0]
    return [np.pad(table, ((at, LANES - size - at), (0, 0))) for at in (0, LANES - size)]


class Level:
    def __init__(self, taps, out_x, out_y, shift, window, size_z, rows_y, rows_y_end, cols_z):
        half = taps // 2
        self.taps, self.out_x, self.in_x = taps, out_x, out_x + taps - 1
        period_y = out_y + 2 * half + (out_y + 1) % 2
        period_z = size_z + half
        self.freq = (period_y + 1) // 2
        self.main = min(LANES, period_z)
        self.left = period_z - self.main
        assert self.freq % 8 == 0 and self.left <= 8 and self.freq <= LANES
        self.rows = self.freq + (8 if self.left else 0)
        turn_z, turn_y = 2 * np.pi / period_z, 2 * np.pi / period_y
        freq_y, freq_z = np.arange(self.freq), np.arange(period_z)

        cells = np.arange(window)
        needed = (cells >= shift - half) & (cells < shift + out_y + half)
        angle = turn_y * np.outer(freq_y, cells)
        self.table_y = np.concatenate([np.cos(angle), -np.sin(angle)], 0) * needed
        self.to_y = np.concatenate(two(self.table_y), 1)
        self.table_z = self.columns(turn_z * np.outer(np.arange(size_z), freq_z))
        self.to_z = terms_below(self.table_z)

        offsets = np.arange(taps) - half
        angle = turn_y * np.outer(freq_y, offsets)
        table = np.zeros((2 * self.freq, 16))
        table[:, :taps] = np.concatenate([np.cos(angle), np.sin(angle)], 0)
        self.kernel_y = np.concatenate(two(table), 1)
        table = self.columns(turn_z * np.outer(offsets, freq_z))
        table = terms_below(np.pad(table, ((0, 16 - taps), (0, 0))))
        self.kernel_z = np.pad(table, ((0, LANES - 48), (0, 0)))

        angle = turn_z * np.outer(freq_z, np.arange(size_z))
        table = np.concatenate([np.cos(angle) @ cols_z.T, np.sin(angle) @ cols_z.T], 1) / period_z
        lanes = np.zeros((LANES * (2 if self.left else 1), table.shape[1]))
        lanes[: self.main] = table[: self.main]
        if self.left:
            for group in range(self.freq // 8):
                at = LANES + 8 * group
                lanes[at : at + self.left] = table[self.main :]
        self.from_z = terms_below(lanes)
        weight = np.where(freq_y == 0, 1.0, 2.0) / period_y
        angle = turn_y * np.outer(np.arange(out_y) + shift, freq_y)
        wave = np.concatenate([weight * np.cos(angle), -weight * np.sin(angle)], 1)
        self.from_y = [three_terms(rows @ wave) for rows in (rows_y, rows_y_end)]

    def columns(self, angle):
        out = []
        for start, stop in ((0, self.main), (self.main, self.main + self.left)):
            for wave in (np.cos(angle[:, start:stop]), np.sin(angle[:, start:stop])):
                table = np.zeros((angle.shape[0], LANES))
                for group in range(1 if start == 0 else self.freq // 8):
                    table[:, 8 * group : 8 * group + stop - start] = wave
                out.append(table)
            if not self.left:
                break
        return np.concatenate(out, 1)


def down(count, first, length):
    out = np.zeros((count, length))
    for j in range(count):
        for a, w in ((-1, 0.5), (0, 1.0), (1, 0.5)):
            if 0 <= first + 2 * j + a < length:
                out[j, first + 2 * j + a] = w
    return out


def dot(a, b):
    return jnp.dot(a, b, preferred_element_type=F32)


def split(value, terms):
    out = []
    for _ in range(terms - 1):
        out.append(value.astype(BF))
        value = value - out[-1].astype(F32)
    return out + [value.astype(BF)]


def side_by_side(value):
    high, low = split(value, 2)
    return jnp.concatenate([high, low, high], 1)


def fold(value):
    groups = value.shape[0] // 8
    lane = lax.broadcasted_iota(jnp.int32, (8, LANES), 1)
    out = value[8 * (groups - 1) :]
    for group in range(groups - 2, -1, -1):
        out = jnp.where(lane < 8 * (group + 1), value[8 * group : 8 * (group + 1)], out)
    return out


def unfold(value, groups):
    lane = lax.broadcasted_iota(jnp.int32, (8, LANES), 1)
    return jnp.concatenate(
        [
            jnp.where((lane >= 8 * group) & (lane < 8 * (group + 1)), value, 0.0)
            for group in range(groups)
        ],
        0,
    )


def joined(spread, sign):
    freq = spread.shape[0] // 2
    outs = []
    for at in range(0, spread.shape[1], 2 * LANES):
        rc, rs = spread[:freq, at : at + LANES], spread[:freq, at + LANES : at + 2 * LANES]
        ic, js = spread[freq:, at : at + LANES], spread[freq:, at + LANES : at + 2 * LANES]
        if at:
            rc, rs, ic, js = fold(rc), fold(rs), fold(ic), fold(js)
        outs.append((rc + js, ic - rs) if sign > 0 else (rc - js, ic + rs))
    return [jnp.concatenate([out[k] for out in outs], 0) for k in range(2)]


def batches(count, size, body):
    for first in range(0, count, size):
        body(list(range(first, min(count, first + size))), first)


def rows_at(first, period, count):
    return pl.ds(first * period if isinstance(first, int) else pl.multiple_of(first * period, 16), count * period)


def store_terms(terms, first, rows, values):
    high, low = split(jnp.concatenate(values, 0), 2)
    terms[0, rows_at(first, rows, len(values)), :] = high
    terms[1, rows_at(first, rows, len(values)), :] = low


def to_frequencies_y(read, count, size, to_y, terms, packed=False):
    rows = terms.shape[1] // count

    def body(xs, first):
        values = []
        for k in range(0, len(xs), 2):
            cells = [read(x) for x in xs[k : k + 2]]
            width = cells[0].shape[1]
            if width % LANES == 0:
                cells = [jnp.concatenate(cells, 1)]
            for part in cells:
                spread = dot(to_y[...], jnp.concatenate([part, part], 0))
                for at in range(0, spread.shape[1], width):
                    value = spread[:, at : at + width]
                    if packed:
                        low_lanes = lax.broadcasted_iota(jnp.int32, (rows, LANES), 1) < LANES // 2
                        value = jnp.where(low_lanes, value[:rows], value[rows:])
                    values.append(value)
        store_terms(terms, first, rows, values)

    batches(count, size, body)


def to_frequencies_z(terms, size, to_z, real, imag):
    count = real.shape[0]
    rows = terms.shape[1] // count

    def body(xs, first):
        span = rows_at(first, rows, len(xs))
        high, low = terms[0, span, :], terms[1, span, :]
        width = high.shape[1]
        if width % LANES == 0:
            spread = dot(jnp.concatenate([high, low, high], 1), to_z[...])
        else:
            spread = dot(high, to_z[:width]) + dot(low, to_z[width : 2 * width])
            spread = spread + dot(high, to_z[2 * width :])
        for k, x in enumerate(xs):
            real[x], imag[x] = joined(spread[k * rows : (k + 1) * rows], 1)

    batches(count, size, body)


def from_frequencies_z(real, imag, size, from_z, terms):
    count = real.shape[0]
    rows = terms.shape[1] // count
    freq = rows // 2

    def body(xs, first):
        lines = []
        for x in xs:
            for ref in (real, imag):
                value = ref[x]
                main = value[:freq]
                if value.shape[0] > freq:
                    main = jnp.concatenate([main, unfold(value[freq:], freq // 8)], 1)
                lines.append(main)
        spread = dot(side_by_side(jnp.concatenate(lines, 0)), from_z[...])
        half = spread.shape[1] // 2
        values = []
        for k in range(len(xs)):
            r = spread[k * rows : k * rows + freq]
            i = spread[k * rows + freq : (k + 1) * rows]
            values += [r[:, :half] - i[:, half:], r[:, half:] + i[:, :half]]
        high, low = split(jnp.concatenate(values, 0), 2)
        terms[0, rows_at(first, rows, len(xs)), :] = high
        terms[1, rows_at(first, rows, len(xs)), :] = low

    batches(count, size, body)


def from_frequencies_y(terms, count, size, from_y, write):
    rows = terms.shape[1] // count

    def body(xs, first):
        for k in range(0, len(xs), 2):
            parts = []
            for x in xs[k : k + 2]:
                span = rows_at(x, rows, 1)
                high, low = terms[0, span, :], terms[1, span, :]
                parts.append(jnp.concatenate([high, low, high], 0))
            value = dot(from_y[...], jnp.concatenate(parts, 1))
            width = parts[0].shape[1]
            for j, x in enumerate(xs[k : k + 2]):
                write(x, value[:, j * width : (j + 1) * width])

    batches(count, size, body)


def along_x(real, imag, spectrum, out_real, out_imag, block, outputs=None, taken=None, before=None):
    kernel_r, kernel_d, kernel_s = spectrum
    taps, period = kernel_r.shape[:2]
    outputs = outputs or list(range(out_real.shape[0]))
    taken = taken or (lambda x: True)

    def body(part):
        rows = slice(8 * part, 8 * part + 8)
        for start in range(0, len(outputs), block):
            wanted = outputs[start : start + block]
            sums = [[None] * 3 for _ in wanted]
            seen = {}
            for a in range(taps):
                used = [i for i, out in enumerate(wanted) if taken(out + a)]
                if used:
                    weights = kernel_r[a, rows, :], kernel_d[a, rows, :], kernel_s[a, rows, :]
                for i in used:
                    x = wanted[i] + a
                    if x not in seen:
                        r, m = real(x, rows), imag(x, rows)
                        seen[x] = r + m, r, m
                    for k in range(3):
                        term = weights[k] * seen[x][k]
                        sums[i][k] = term if sums[i][k] is None else sums[i][k] + term
            for i, out in enumerate(wanted):
                value = sums[i][0] - sums[i][2], sums[i][0] + sums[i][1]
                if before is not None:
                    value = value[0] + before[0][out, rows, :], value[1] + before[1][out, rows, :]
                out_real[start + i, rows, :] = value[0]
                out_imag[start + i, rows, :] = value[1]

    for part in range(period // 8):
        body(part)


def all_terms(value):
    return jnp.concatenate(split(value, TERMS), 0)


def spectra_kernel(sizes, *refs):
    kernels, table, outs, (padded, lines) = refs[0], refs[1], refs[2:-2], refs[-2:]
    levels, taps = kernels.shape[:2]
    padded[...] = jnp.zeros(padded.shape, padded.dtype)
    at_z = 0
    for level in range(levels):
        outs_here = outs[3 * level : 3 * level + 3]
        rows, columns, row, lane = sizes[level]
        kernel_y = table[row : row + rows, lane : lane + 32]
        kernel_z = table[:, at_z : at_z + columns]
        at_z += columns
        for at in (0, 16, 32):
            padded[:, :taps, at : at + taps] = kernels[level].astype(F32)
        cells = jnp.concatenate([padded[a].astype(BF) for a in range(taps)], 1)
        spread = dot(kernel_y, jnp.concatenate([cells, cells], 0))
        lane = lax.broadcasted_iota(jnp.int32, (rows, LANES), 1)
        middle = (lane >= 16) & (lane < 32)
        for a in range(taps):
            high, low = (term.astype(F32) for term in split(spread[:, a * LANES : (a + 1) * LANES], 2))
            lines[a * rows : (a + 1) * rows, :] = jnp.where(middle, low, high).astype(BF)

        def body(xs, first, rows=rows, kernel_z=kernel_z, outs=outs_here):
            spread = dot(lines[rows_at(first, rows, len(xs)), :], kernel_z)
            for k, a in enumerate(xs):
                real, imag = joined(spread[k * rows : (k + 1) * rows], -1)
                outs[0][a] = real
                outs[1][a] = imag - real
                outs[2][a] = imag + real

        batches(taps, 5, body)


def chosen(flag, first, second):
    return jnp.where(flag, first, second)


def pack_kernel(
    own, got_a, got_b, down_z, down_y, ordered, near, coarse, next_a, next_b, far_a, far_b, part
):
    count, size = own.shape[:2]
    side = got_a.shape[1]
    up_y, up_x, up_far = leads("gy", 1), leads("gx", 1), leads("gx", 2)
    ended = lax.axis_index("gy") == lax.axis_size("gy") - 1
    width = near.shape[1]
    start = side - (width - size) // 2
    window = part.shape[1]

    def body(xs, first):
        rows = []
        for x in xs:
            a, b, o = got_a[x], got_b[x], own[x].astype(BF)
            l, r = chosen(up_y, b, a), chosen(up_y, a, b)
            near[x] = jnp.concatenate([l[start:], o, r[: side - start]], 0)
            low = jnp.concatenate([l, o[: window - side]], 0)
            high = jnp.concatenate([o[size + side - window :], r], 0)
            rows.append(jnp.concatenate([low, high], 1))
        value = dot(jnp.concatenate(rows, 0), down_z[...])
        for k, x in enumerate(xs):
            part[x] = value[k * window : (k + 1) * window]

    batches(count, 4, body)
    half = down_y.shape[0] // 2
    shape = (half, LANES)
    high_lanes = lax.broadcasted_iota(jnp.int32, shape, 1) >= LANES // 2
    outside = high_lanes & (lax.broadcasted_iota(jnp.int32, shape, 0) >= half // 2)
    outside = outside & ended
    last = count // 2
    totals = []
    for i in range(last + 1):
        if i == 0:
            total = part[0] + 0.5 * part[1]
        elif i == last:
            total = 0.5 * part[count - 1]
        else:
            total = 0.5 * part[2 * i - 1] + part[2 * i] + 0.5 * part[2 * i + 1]
        totals.append(dot(down_y[...], all_terms(total)))
    for i, total in enumerate(totals):
        row = jnp.where(high_lanes, total[half:], total[:half])
        row = jnp.where(outside, 0.0, row)
        if i == 0:
            for k, term in enumerate(split(row, PARTS)):
                coarse[k] = term
        elif i == last:
            for k, term in enumerate(split(row, PARTS)):
                coarse[last + PARTS - 1 + k] = term
        else:
            coarse[i + PARTS - 1] = row.astype(BF)
    lines = next_a.shape[0] - coarse.shape[0] * half
    tail = count - lines // width
    far_tail = coarse.shape[0] - far_a.shape[0]
    for out, upward in ((next_a, up_x), (next_b, jnp.logical_not(up_x))):
        first = jnp.where(upward, tail, 0)
        for x in range(lines // width):
            out[x * width : (x + 1) * width, :] = near[first + x]
        for k in range(coarse.shape[0]):
            out[lines + k * half : lines + (k + 1) * half, :] = coarse[k]
    for out, upward in ((far_a, up_far), (far_b, jnp.logical_not(up_far))):
        first = jnp.where(upward, far_tail, 0)
        for k in range(far_a.shape[0]):
            out[k] = coarse[first + k]


def own_kernel(near, to_y, to_z, real, imag, ahead):
    count = real.shape[0]
    to_frequencies_y(lambda x: near[x], count, 8, to_y, ahead)
    to_frequencies_z(ahead, 4, to_z, real, imag)


def own_sum_kernel(
    real,
    imag,
    coarse,
    kr,
    kd,
    ks,
    from_z,
    from_y,
    mr,
    md,
    ms,
    m_to_y,
    m_to_z,
    out_real,
    out_imag,
    whole,
    m_part_real,
    m_part_imag,
    back,
    m_real,
    m_imag,
    m_ahead,
):
    count = real.shape[0]
    half = kr.shape[0] // 2
    along_x(
        lambda x, rows: real[x - half, rows, :],
        lambda x, rows: imag[x - half, rows, :],
        (kr, kd, ks),
        out_real,
        out_imag,
        BLOCK,
        None,
        lambda x: half <= x < half + count,
    )
    lines = m_real.shape[0]
    first = half + 1
    to_frequencies_y(lambda k: coarse[k + PARTS], lines, 6, m_to_y, m_ahead, True)
    to_frequencies_z(m_ahead, 6, m_to_z, m_real, m_imag)
    along_x(
        lambda x, rows: m_real[x - first, rows, :],
        lambda x, rows: m_imag[x - first, rows, :],
        (mr, md, ms),
        m_part_real,
        m_part_imag,
        7,
        None,
        lambda x: first <= x < first + lines,
    )
    inner = slice(half, count - half)

    def write(x, value):
        whole[x] = value

    from_frequencies_z(out_real.at[inner], out_imag.at[inner], 4, from_z, back)
    from_frequencies_y(back, whole.shape[0], 8, from_y, write)


def final_kernel(
    t_columns,
    part_real,
    part_imag,
    whole,
    m_part_real,
    m_part_imag,
    next_a,
    next_b,
    far_a,
    far_b,
    coarse,
    kr,
    kd,
    ks,
    to_y,
    to_z,
    from_z,
    from_y,
    mr,
    md,
    ms,
    m_to_y,
    m_to_z,
    m_from_z,
    m_from_y,
    tr,
    td,
    ts,
    t_down_y,
    t_down_z,
    t_to_y,
    t_to_z,
    t_from_z,
    t_from_y,
    out,
    side_real,
    side_imag,
    er,
    ei,
    ahead,
    back,
    mid,
    m_real,
    m_imag,
    m_er,
    m_ei,
    m_ahead,
    m_back,
    m_out,
    t_real,
    t_imag,
    t_er,
    t_ei,
    t_cells,
    t_ahead,
    t_back,
    t_out,
):
    left_x = lax.axis_size("gx") - lax.axis_index("gx")
    ended_x, close_x = left_x == 1, left_x <= 2
    ended_y = (lax.axis_index("gy") == lax.axis_size("gy") - 1).astype(jnp.int32)
    up_x, up_far = leads("gx", 1), leads("gx", 2)
    count = part_real.shape[0]
    width = to_y.shape[1] // 2
    reach = side_real.shape[0] // 2
    top_rows = left_x * (count // 4) + reach

    def from_left(at):
        return chosen(up_x, next_b[at, :], next_a[at, :])

    def from_right(at):
        return chosen(up_x, next_a[at, :], next_b[at, :])

    def far_left(k):
        return chosen(up_far, far_b[k], far_a[k])

    def far_right(k):
        return chosen(up_far, far_a[k], far_b[k])

    def side_cells(x):
        read, first = (from_left, x) if x < reach else (from_right, x - reach)
        return read(slice(first * width, (first + 1) * width))

    for first in range(0, 2 * reach, 2):
        xs = [first, first + 1]
        cells = jnp.concatenate([side_cells(x) for x in xs], 1)
        spread = dot(to_y[...], jnp.concatenate([cells, cells], 0))
        store_terms(ahead, first, to_y.shape[0], [spread[:, :LANES], spread[:, LANES:]])
    to_frequencies_z(ahead, 7, to_z, side_real, side_imag)

    def source(side):
        return lambda x, rows: side[x if x < reach else x - count, rows, :]

    edges = list(range(reach)) + list(range(count - reach, count))
    along_x(
        source(side_real),
        source(side_imag),
        (kr, kd, ks),
        er,
        ei,
        reach,
        edges,
        lambda x: x < reach or x >= reach + count,
        (part_real, part_imag),
    )
    from_frequencies_z(er, ei, 4, from_z, back)

    def fine_write(x, value):
        out[edges[x]] = value

    from_frequencies_y(back, len(edges), 8, from_y, fine_write)
    for x in range(whole.shape[0]):
        out[reach + x] = whole[x]

    half = mid.shape[1]
    last = count // 2
    lines = next_a.shape[0] - coarse.shape[0] * half

    def left_row(k):
        return from_left(slice(lines + k * half, lines + (k + 1) * half))

    def right_row(k):
        return from_right(slice(lines + k * half, lines + (k + 1) * half))

    def added(first, second, dropped=None):
        value = sum(first(PARTS - 1 - k).astype(F32) for k in range(PARTS))
        value = value + sum(second(last + 2 * PARTS - 2 - k).astype(F32) for k in range(PARTS))
        if dropped is not None:
            value = jnp.where(dropped, 0.0, value)
        return value.astype(BF)

    spare = far_a.shape[0] - PARTS
    far_first = coarse.shape[0] - far_a.shape[0]
    rows = [far_left(k) for k in range(spare)]
    rows += [added(left_row, lambda k: far_left(k - far_first))]
    rows += [left_row(k) for k in range(PARTS, last - 1 + PARTS)]
    rows += [added(lambda k: coarse[k], left_row)]
    rows += [coarse[k] for k in range(PARTS, last - 1 + PARTS)]
    rows += [added(right_row, lambda k: coarse[k], ended_x)]
    rows += [right_row(k) for k in range(PARTS, last - 1 + PARTS)]
    rows += [added(far_right, right_row, close_x)]
    rows += [far_right(k) for k in range(PARTS, PARTS + spare)]
    for k, row in enumerate(rows):
        mid[k] = row

    own_lines = last - 1
    m_rows = m_real.shape[0] + own_lines
    skip = (mid.shape[0] - m_rows) // 2
    sides = [x for x in range(m_rows) if not reach < x <= reach + own_lines]
    to_frequencies_y(lambda k: mid[sides[k] + skip], len(sides), 8, m_to_y, m_ahead, True)
    to_frequencies_z(m_ahead, 8, m_to_z, m_real, m_imag)

    t_width = t_cells.shape[1]
    spare = (t_width - t_columns) // 2
    inside = lax.broadcasted_iota(jnp.int32, (t_width, t_cells.shape[2]), 0)
    inside = inside < jnp.where(ended_y == 1, t_width - spare, t_width)

    def top_cells(xs, first):
        spreads = []
        for t in xs:
            total = 0.5 * mid[2 * t].astype(F32) + mid[2 * t + 1].astype(F32) + 0.5 * mid[2 * t + 2].astype(F32)
            spreads.append(dot(t_down_y[...], all_terms(total)))
        low = jnp.concatenate([spread[:t_width] for spread in spreads], 0)
        high = jnp.concatenate([spread[t_width:] for spread in spreads], 0)
        value = dot(jnp.concatenate(split(low, TERMS) + split(high, TERMS), 1), t_down_z[...])
        for k, t in enumerate(xs):
            row = jnp.where(inside, value[k * t_width : (k + 1) * t_width], 0.0)
            t_cells[t] = jnp.where(t < top_rows, row, 0.0).astype(BF)

    batches(t_real.shape[0], 7, top_cells)
    to_frequencies_y(lambda x: t_cells[x], t_real.shape[0], 7, t_to_y, t_ahead)
    to_frequencies_z(t_ahead, 7, t_to_z, t_real, t_imag)

    def plain(ref):
        return lambda x, rows: ref[x, rows, :]

    along_x(
        lambda x, rows: m_real[sides.index(x), rows, :],
        lambda x, rows: m_imag[sides.index(x), rows, :],
        (mr, md, ms),
        m_er,
        m_ei,
        7,
        None,
        lambda x: x in sides,
        (m_part_real, m_part_imag),
    )
    along_x(plain(t_real), plain(t_imag), (tr, td, ts), t_er, t_ei, 7)

    def top_write(x, value):
        t_out[x] = value

    def mid_write(x, value):
        m_out[x] = value

    from_frequencies_z(t_er, t_ei, 7, t_from_z, t_back)
    from_frequencies_z(m_er, m_ei, 7, m_from_z, m_back)
    from_frequencies_y(t_back, t_out.shape[0], 7, t_from_y.at[ended_y], top_write)
    from_frequencies_y(m_back, m_out.shape[0], 7, m_from_y.at[ended_y], mid_write)
    keep = jnp.where(ended_x, 0.0, 1.0)
    top = t_out.shape[0] - 1
    t_out[top] = t_out[top] * keep
    for i in range(top):
        m_out[2 * i] += t_out[i]
        m_out[2 * i + 1] += 0.5 * (t_out[i] + t_out[i + 1])
    m_out[2 * top] = (m_out[2 * top] + t_out[top]) * keep

    def finish(i):
        out[2 * i] += m_out[i]
        out[2 * i + 1] += 0.5 * (m_out[i] + m_out[i + 1])

    for i in range(count // 2):
        finish(i)


def call(kernel, outs, scratch, args, mib, loose=()):
    vmem = pl.BlockSpec(memory_space=pltpu.VMEM)
    return pl.pallas_call(
        kernel,
        out_shape=outs,
        in_specs=[
            pl.BlockSpec(memory_space=pl.ANY) if i in loose else vmem for i in range(len(args))
        ],
        out_specs=jax.tree.map(lambda _: vmem, outs),
        scratch_shapes=[pltpu.VMEM(shape, dtype) for dtype, shape in scratch],
        compiler_params=pltpu.CompilerParams(vmem_limit_bytes=mib << 20),
    )(*args)


def level_scratch(level, in_x, ny, nz, lanes, extra=()):
    rows = [
        (F32, (count, level.rows, LANES))
        for count in (in_x, in_x, level.out_x, level.out_x)
    ]
    terms = [
        (BF, (2, in_x * 2 * level.freq, lanes)),
        (BF, (2, level.out_x * 2 * level.freq, nz)),
    ]
    return [*rows, *extra, *terms, (F32, (level.out_x, ny, nz))]


def leads(axis, by):
    return lax.rem(lax.div(lax.axis_index(axis), by), 2) == 0


def swapped(first, second, axis, by):
    length = lax.axis_size(axis)
    outs = []
    for value, turn in ((first, 0), (second, 1)):
        up = [i for i in range(length - by) if i // by % 2 == turn]
        pairs = [(i, i + by) for i in up] + [(i + by, i) for i in up]
        outs.append(lax.ppermute(value, axis, pairs))
    return outs


def block(charges, kernel_fine, kernel_mid, kernel_top):
    nx, ny, nz = charges.shape
    taps = kernel_fine.shape[0]
    half = taps // 2
    wide = half + 1

    ident = np.eye(ny)
    width = ny + 2 * wide
    fine = Level(taps, nx, ny, wide, width, nz, ident, ident, np.eye(nz))
    my, mz = ny // 2, nz // 2
    to_fine = up(my)
    ended = np.diag([1.0] * my + [0.0])
    mid = Level(
        taps, nx // 2 + 1, my + 1, ny // 4, ny, mz, to_fine, to_fine @ ended, up_closed(mz)
    )
    ty, tz = my // 2, mz // 2
    to_mid = np.concatenate([up(ty), np.eye(ty + 1)[-1:]], 0)
    top_ended = np.diag([1.0] * ty + [0.0])
    top = Level(
        taps,
        nx // 4 + 1,
        ty + 1,
        wide,
        ty + 2 * wide,
        tz,
        to_fine @ to_mid,
        to_fine @ to_mid @ top_ended,
        up_closed(mz) @ up_closed(tz),
    )

    levels = (fine, mid, top)
    outs = [
        jax.ShapeDtypeStruct((taps, level.rows, LANES), F32)
        for level in levels
        for _ in range(3)
    ]
    table = np.concatenate([level.kernel_z for level in levels], 1)
    sizes = []
    for level, other in ((fine, None), (mid, None), (top, mid)):
        rows, columns = level.kernel_y.shape[0], level.kernel_z.shape[1]
        row, lane = 48 + (other.kernel_y.shape[0] if other else 0), 0 if level is fine else LANES
        assert row + rows <= LANES
        table[row : row + rows, lane : lane + 32] = level.kernel_y
        sizes.append((rows, columns, row, lane))
    spectra = call(
        functools.partial(spectra_kernel, sizes),
        outs,
        [(F32, (taps, 16, LANES)), (BF, (taps * 2 * fine.freq, LANES))],
        [jnp.stack([kernel_fine, kernel_mid, kernel_top]), table],
        8,
    )

    side = ny // 2
    up_y = leads("gy", 1)
    got_a, got_b = swapped(
        *(
            lax.dynamic_slice_in_dim(charges, jnp.where(flag, side, 0), side, 1).astype(BF)
            for flag in (up_y, jnp.logical_not(up_y))
        ),
        "gy",
        1,
    )

    window = side + ny // 2 + 16
    packed = ny // 2
    down_z = np.concatenate([np.pad(down(mz, 0, nz).T, ((0, 0), (at, mz - at))) for at in (0, mz)], 0)
    shift = ny + 2 * side - window
    down_y = np.concatenate([down(packed, 0, window), down(packed, 2 * packed - shift, window)], 0)
    mx = nx // 2
    lines = mx - 1 + 2 * PARTS
    reach = 2 * half + 1 - mx
    assert 0 < reach <= mx - 1 and 2 * mz == LANES == nz
    shapes = [
        (nx, width, LANES),
        (lines, packed, LANES),
        (half * width + lines * packed, LANES),
        (half * width + lines * packed, LANES),
        (reach + PARTS, packed, LANES),
        (reach + PARTS, packed, LANES),
    ]
    near, coarse, next_a, next_b, far_a, far_b = call(
        pack_kernel,
        [jax.ShapeDtypeStruct(shape, BF) for shape in shapes],
        [(F32, (nx, window, LANES))],
        [
            charges,
            got_a,
            got_b,
            down_z.astype(BF),
            np.tile(down_y, (1, TERMS)).astype(BF),
            spectra[0],
        ],
        8,
        loose=(5,),
    )
    far_a, far_b = swapped(far_a, far_b, "gx", 2)
    next_a, next_b = swapped(next_a, next_b, "gx", 1)

    parts = [np.concatenate(two(mid.table_y[:, at : at + packed]), 1) for at in (0, packed)]
    mid_to_y = np.concatenate(parts, 0)
    mid_to_z = terms_below(np.tile(mid.table_z, (2, 1)))
    spectrum = [jax.ShapeDtypeStruct((nx, fine.rows, LANES), F32)] * 2
    own = call(
        own_kernel,
        spectrum,
        [(BF, (2, nx * 2 * fine.freq, nz))],
        [near, fine.to_y, fine.to_z],
        10,
    )
    inner = nx - 2 * half
    own = call(
        own_sum_kernel,
        [
            *spectrum,
            jax.ShapeDtypeStruct((inner, ny, nz), F32),
            *[jax.ShapeDtypeStruct((mid.out_x, mid.rows, LANES), F32)] * 2,
        ],
        [
            (BF, (2, inner * 2 * fine.freq, nz)),
            *[(F32, (mx - 1, mid.rows, LANES))] * 2,
            (BF, (2, (mx - 1) * 2 * mid.freq, LANES)),
        ],
        [
            *own,
            coarse,
            *spectra[:3],
            fine.from_z,
            fine.from_y[0],
            *spectra[3:6],
            mid_to_y,
            mid_to_z,
        ],
        10,
    )

    wide_top = ty + 2 * wide
    t_down_y = down(wide_top, 0, 2 * packed)
    t_down_y = np.concatenate([t_down_y[:, :packed], t_down_y[:, packed:]], 0)
    t_down_z = np.concatenate(
        [np.tile(table, (TERMS, 1)) for table in both_sides(down(tz, 0, mz).T)], 0
    )
    return call(
        functools.partial(final_kernel, ty),
        jax.ShapeDtypeStruct((nx, ny, nz), F32),
        [
            (F32, (2 * half, fine.rows, LANES)),
            (F32, (2 * half, fine.rows, LANES)),
            (F32, (2 * half, fine.rows, LANES)),
            (F32, (2 * half, fine.rows, LANES)),
            (BF, (2, 2 * half * 2 * fine.freq, nz)),
            (BF, (2, 2 * half * 2 * fine.freq, nz)),
            (BF, (3 * mx + 1 + 2 * reach, packed, LANES)),
            *level_scratch(mid, mid.in_x - mx + 1, ny, nz, LANES),
            *level_scratch(top, top.in_x, ny, nz, tz, [(BF, (top.in_x, wide_top, tz))]),
        ],
        [
            *own,
            next_a,
            next_b,
            far_a,
            far_b,
            coarse,
            *spectra[:3],
            fine.to_y,
            fine.to_z,
            fine.from_z,
            fine.from_y[0],
            *spectra[3:6],
            mid_to_y,
            mid_to_z,
            mid.from_z,
            np.stack(mid.from_y),
            *spectra[6:],
            np.tile(t_down_y, (1, TERMS)).astype(BF),
            t_down_z.astype(BF),
            top.to_y,
            top.to_z,
            top.from_z,
            np.stack(top.from_y),
        ],
        26,
    )


def solution(mesh):
    placed = (P("gx", "gy", None), P(), P(), P())
    return jax.shard_map(
        block, mesh=mesh, in_specs=placed, out_specs=P("gx", "gy", None), check_vma=False
    )
```
